32 devices in a mesh: rep: 8 (over z, core), shard: 4 (over y, x).
Axes of the slice: x: 2, y: 2, z: 4, core: 2. Of those that a mesh axis runs over, the one named last changes fastest.
Arguments:
- tokens: bfloat16 [32, 1024, 1024], P(('rep', 'shard')), may hold values from -6 to 6
- segments: int32 [32, 1024], P(('rep', 'shard')), may hold values from 0 to 7, never falling along the last dimension, each value on 1 to 512 neighbouring positions
- cotangent: bfloat16 [32, 1024, 1024], P(('rep', 'shard')), may hold values from -6 to 6
- norm_mix: bfloat16 [1024], P('shard'), may hold values from 0.5 to 1.5
- w_query: bfloat16 [1024, 512], P('shard'), may hold values from -0.1875 to 0.1875
- w_key: bfloat16 [1024, 512], P('shard'), may hold values from -0.1875 to 0.1875
- w_value: bfloat16 [1024, 1024], P('shard'), may hold values from -0.1875 to 0.1875
- w_outgate: bfloat16 [1024, 1024], P('shard'), may hold values from -0.1875 to 0.1875
- w_low: bfloat16 [1024, 16], P('shard'), may hold values from -0.1875 to 0.1875
- w_high: bfloat16 [16, 512], P(None, 'shard'), may hold values from -1.5 to 1.5
- decay_bias: bfloat16 [512], P('shard'), may hold values from 0.5 to 4.5
- head_gain: bfloat16 [256], P('shard'), may hold values from 0.5 to 1.5
- w_out: bfloat16 [1024, 1024], P('shard'), may hold values from -0.1875 to 0.1875
- norm_mlp: bfloat16 [1024], P('shard'), may hold values from 0.5 to 1.5
- w_gate: bfloat16 [1024, 2816], P('shard'), may hold values from -0.1875 to 0.1875
- w_up: bfloat16 [1024, 2816], P('shard'), may hold values from -0.1875 to 0.1875
- w_down: bfloat16 [2816, 1024], P('shard'), may hold values from -0.109375 to 0.109375
Outputs:
- block_out: bfloat16 [32, 1024, 1024], P(('rep', 'shard'))
- grad_tokens: float32 [32, 1024, 1024], P(('rep', 'shard'))
- grad_norm_mix: float32 [1024], P('shard')
- grad_w_query: float32 [1024, 512], P('shard')
- grad_w_key: float32 [1024, 512], P('shard')
- grad_w_value: float32 [1024, 1024], P('shard')
- grad_w_outgate: float32 [1024, 1024], P('shard')
- grad_w_low: float32 [1024, 16], P('shard')
- grad_w_high: float32 [16, 512], P(None, 'shard')
- grad_decay_bias: float32 [512], P('shard')
- grad_head_gain: float32 [256], P('shard')
- grad_w_out: float32 [1024, 1024], P('shard')
- grad_norm_mlp: float32 [1024], P('shard')
- grad_w_gate: float32 [1024, 2816], P('shard')
- grad_w_up: float32 [1024, 2816], P('shard')
- grad_w_down: float32 [2816, 1024], P('shard')
The draws below stay inside these ranges and needn't reach their ends.
Inputs may be any that keep to these rules, and one draw needn't show every extreme that they name: `segments`: segment numbers never fall along a sequence; a document has 1 to 512 tokens and some document has exactly 512.
All inputs are finite; a program needn't handle non-finite values.
Results may differ from the reference program's by a relative error of at most 0.018.
Values may be sent and summed in bfloat16 or wider, within the bound.
A program may use at most 256 MiB of HBM per device.

```python
import math
import jax
import jax.numpy as jnp
import numpy as np
from jax import lax

D = 1024
HEADS = 4
KH = 128
VH = 256
RANK = 16
FF = 2816
BLOCK = 64
LEN = 1024
DOCS = 8
KD = 512
VD = 1024
SEQS = 32


def levels(key, extent, cuts, least, largest):
    def one(dim, shards_of):
        draws = jax.random.uniform(jax.random.fold_in(jax.random.fold_in(key, 6), dim), (shards_of,), jnp.float32, least / len(cuts), largest / len(cuts))
        return jnp.repeat(jnp.exp(draws), extent[dim] // shards_of).reshape((-1,) + (1,) * (len(extent) - dim - 1))

    level = one(*cuts[0])
    for cut in cuts[1:]:
        level = level * one(*cut)
    return level


def profile(amount, total, bound, lean):
    weights = [(1 << 20) // math.isqrt(grade ** lean) + 1 for grade in range(2, amount + 1)]
    rest, holding = total - bound - (amount - 1), [1] * (amount - 1)
    while rest > 0:
        free = [i for i in range(amount - 1) if holding[i] < bound]
        mass, budget = sum([weights[i] for i in free]), rest
        for i in free:
            extra = min(bound - holding[i], max(1, budget * weights[i] // mass), rest)
            holding[i] = holding[i] + extra
            rest = rest - extra
    return np.array([bound] + holding)


def ragged_sizes(rng, number_of, total, most, lean):
    if number_of == 2:
        one = jax.random.randint(rng, (), max(1, total - most), min(most, total - 1) + 1)
        return jnp.stack([one, total - one])
    lengths = jnp.asarray(profile(number_of, total, most, lean), jnp.int32)
    couples = (number_of - 1) // 2
    source_of, taker = lengths[1:1 + 2 * couples:2], lengths[2:2 + 2 * couples:2]
    room = jnp.minimum(source_of - 1, most - taker)
    passed = jax.random.randint(jax.random.fold_in(rng, 1), (couples,), 0, 1 << 20) % (room + 1)
    lengths = lengths.at[1:1 + 2 * couples:2].set(source_of - passed).at[2:2 + 2 * couples:2].set(taker + passed)
    return lengths[jax.random.permutation(jax.random.fold_in(rng, 2), number_of)]


def gaussian(rng, dims, scale, most, pieces=(), dtype=jnp.bfloat16):
    values = scale * jax.random.normal(rng, dims, jnp.float32)
    if pieces:
        values = values * levels(rng, dims, pieces, -0.22, 0.18)
    return jnp.clip(values, -most, most).astype(dtype)


def setup_inputs(seed: int = 0) -> dict:
    arg_keys = jax.random.split(jax.random.key(seed), 18)
    tokens = gaussian(arg_keys[0], (SEQS, LEN, D), 1.0, 6.0, ((0, 32),))
    segments = jax.vmap(lambda own: jnp.searchsorted(jnp.cumsum(ragged_sizes(own, DOCS, LEN, LEN // 2, 2)), jnp.arange(LEN), side="right"))(jax.random.split(arg_keys[1], SEQS)).reshape((SEQS, LEN)).astype(jnp.int32)
    cotangent = gaussian(arg_keys[2], (SEQS, LEN, D), 1.0, 6.0, ((0, 32),))
    norm_mix = jnp.clip(1.0 + 0.1 * jax.random.normal(arg_keys[3], (D,), jnp.float32), 0.5, 1.5).astype(jnp.bfloat16)
    w_query = gaussian(arg_keys[4], (D, KD), D ** -0.5, 0.1875, ((0, 4),))
    w_key = gaussian(arg_keys[5], (D, KD), D ** -0.5, 0.1875, ((0, 4),))
    w_value = gaussian(arg_keys[6], (D, VD), D ** -0.5, 0.1875, ((0, 4),))
    w_outgate = gaussian(arg_keys[7], (D, VD), D ** -0.5, 0.1875, ((0, 4),))
    w_low = gaussian(arg_keys[8], (D, RANK), D ** -0.5, 0.1875, ((0, 4),))
    w_high = gaussian(arg_keys[9], (RANK, KD), RANK ** -0.5, 1.5, ((1, 4),))
    decay_bias = jnp.clip(0.5 + 4.0 * jax.random.uniform(arg_keys[10], (KD,), jnp.float32) ** levels(arg_keys[10], (KD,), ((0, 4),), -0.2, 0.2), 0.5, 4.5).astype(jnp.bfloat16)
    head_gain = jnp.clip(1.0 + 0.1 * jax.random.normal(arg_keys[11], (VH,), jnp.float32), 0.5, 1.5).astype(jnp.bfloat16)
    w_out = gaussian(arg_keys[12], (VD, D), VD ** -0.5, 0.1875, ((0, 4),))
    norm_mlp = jnp.clip(1.0 + 0.1 * jax.random.normal(arg_keys[13], (D,), jnp.float32), 0.5, 1.5).astype(jnp.bfloat16)
    w_gate = gaussian(arg_keys[14], (D, FF), D ** -0.5, 0.1875, ((0, 4),))
    w_up = gaussian(arg_keys[15], (D, FF), D ** -0.5, 0.1875, ((0, 4),))
    w_down = gaussian(arg_keys[16], (FF, D), FF ** -0.5, 0.109375, ((0, 4),))
    return {"tokens": tokens, "segments": segments, "cotangent": cotangent, "norm_mix": norm_mix, "w_query": w_query, "w_key": w_key, "w_value": w_value, "w_outgate": w_outgate, "w_low": w_low, "w_high": w_high, "decay_bias": decay_bias, "head_gain": head_gain, "w_out": w_out, "norm_mlp": norm_mlp, "w_gate": w_gate, "w_up": w_up, "w_down": w_down}


HEAD_EPS = 1.0

@jax.custom_vjp
def low(v):
    return lax.optimization_barrier(v.astype(jnp.bfloat16)).astype(jnp.float32)

@jax.custom_vjp
def low_back(v):
    return v

def low_keep(v):
    return (low(v), None)

def low_pass(kept, grad):
    return (grad,)

def back_keep(v):
    return (v, None)

def back_low(kept, grad):
    return (low(grad),)
low.defvjp(low_keep, low_pass)
low_back.defvjp(back_keep, back_low)

def matmul(left, right):
    return jnp.dot(left, right, precision=lax.Precision.HIGHEST, preferred_element_type=jnp.float32)

def rms_scale(values, gain, epsilon=1e-05):
    inverse = lax.rsqrt(lax.optimization_barrier(jnp.mean(values * values, axis=-1, keepdims=True)) + epsilon)
    return values * inverse * gain

def block_pass(query, keys, values, decay, segment):
    length, heads, key_size = query.shape
    value_size = values.shape[-1]
    blocks = length // BLOCK
    query = query * key_size ** (-0.5)
    lower = lax.broadcasted_iota(jnp.int32, (BLOCK, BLOCK), 0) >= lax.broadcasted_iota(jnp.int32, (BLOCK, BLOCK), 1)

    def advance(carry, item):
        state, last_seg = carry
        qblk, kblk, vblk, dblk, sblk = item
        cumul = jnp.cumsum(dblk, axis=0)
        diff = cumul[:, None] - cumul[None, :]
        weight = jnp.exp(jnp.where(lower[:, :, None, None], diff, 0.0))
        same = ((sblk[:, None] == sblk[None, :]) & lower).astype(jnp.float32)
        scores = jnp.einsum('thd,tshd,shd->tsh', qblk, weight, kblk, precision=lax.Precision.HIGHEST) * same[:, :, None]
        inner = jnp.einsum('tsh,she->the', scores, vblk, precision=lax.Precision.HIGHEST)
        keep = (sblk == last_seg).astype(jnp.float32)
        carried = jnp.einsum('thd,hde->the', qblk * jnp.exp(cumul), state, precision=lax.Precision.HIGHEST) * keep[:, None, None]
        final = cumul[-1]
        tail = (sblk == sblk[-1]).astype(jnp.float32)
        scaled = kblk * jnp.exp(final[None] - cumul) * tail[:, None, None]
        fresh = jnp.einsum('shd,she->hde', scaled, vblk, precision=lax.Precision.HIGHEST)
        stay = (sblk[-1] == last_seg).astype(jnp.float32)
        state = jnp.exp(final)[:, :, None] * state * stay + fresh
        return ((state, sblk[-1]), inner + carried)

    def shaped(array):
        return array.reshape((blocks, BLOCK) + array.shape[1:])
    start = (jnp.zeros((heads, key_size, value_size), jnp.float32), jnp.int32(-1))
    _, outputs = lax.scan(jax.checkpoint(advance), start, (shaped(query), shaped(keys), shaped(values), shaped(decay), shaped(segment)))
    return outputs.reshape(length, heads, value_size)

def mixer_core(query, keys, values, outgate, lowpre, decay_bias, head_gain, segment):
    total = query.shape[0]
    seqs = segment.shape[0]
    length = segment.shape[1]
    decay = jax.nn.log_sigmoid(lowpre + decay_bias) / 16.0

    def split(array, width):
        return array.reshape(seqs, length, HEADS, width)
    mixed = jax.vmap(block_pass)(split(query, KH), split(keys, KH), split(values, VH), split(decay, KH), segment)
    normed = rms_scale(mixed, head_gain, HEAD_EPS)
    return normed.reshape(total, VD) * jax.nn.silu(outgate)

def block_rows(inputs, segment, params):
    norm_mix, w_query, w_key, w_value, w_outgate, w_low, w_high, decay_bias, head_gain, w_out, norm_mlp, w_gate, w_up, w_down = params
    first = low(rms_scale(inputs, norm_mix))
    query = low_back(matmul(first, w_query))
    keys = low_back(matmul(first, w_key))
    values = low_back(matmul(first, w_value))
    outgate = low_back(matmul(first, w_outgate))
    lowrank = low(low_back(matmul(first, w_low)))
    lowpre = low_back(matmul(lowrank, w_high))
    mixed = low(mixer_core(query, keys, values, outgate, lowpre, decay_bias, head_gain, segment))
    resid = inputs + low_back(matmul(mixed, w_out))
    second = low(rms_scale(resid, norm_mlp))
    gate = low_back(matmul(second, w_gate))
    upward = low_back(matmul(second, w_up))
    hidden = low(jax.nn.silu(gate) * upward)
    return resid + low_back(matmul(hidden, w_down))

def reference(tokens, segments, cotangent, norm_mix, w_query, w_key, w_value, w_outgate, w_low, w_high, decay_bias, head_gain, w_out, norm_mlp, w_gate, w_up, w_down):
    group = math.gcd(SEQS, max(1, 4096 // LEN))
    grouped_segs = segments.reshape(SEQS // group, group, LEN)

    def forward(inputs, *params):
        grouped = inputs.reshape(SEQS // group, group * LEN, D)

        def one_group(item):
            return block_rows(item[0], item[1], params)
        outputs = lax.map(jax.checkpoint(one_group), (grouped, grouped_segs))
        return outputs.reshape(SEQS, LEN, D)
    weights = (norm_mix, w_query, w_key, w_value, w_outgate, w_low, w_high, decay_bias, head_gain, w_out, norm_mlp, w_gate, w_up, w_down)
    floats = [weight.astype(jnp.float32) for weight in weights]
    result, pull = jax.vjp(forward, tokens.astype(jnp.float32), *floats)
    grads = pull(cotangent.astype(jnp.float32))
    return (result.astype(jnp.bfloat16), grads[0], grads[1], grads[2], grads[3], grads[4], grads[5], grads[6], grads[7], grads[8], grads[9], grads[10], grads[11], grads[12], grads[13], grads[14])
```

```python
import functools
import numpy as np
import jax, jax.numpy as jnp
from jax import lax
from jax.experimental import pallas as pl
from jax.experimental.pallas import tpu as pltpu
from jax.sharding import PartitionSpec as P
HEADS=4; KH=128; VH=256; C=128
SCALE=KH**-0.5
LEVELS=(64,32,16,8,4,2,1)
F32=jnp.float32; BF=jnp.bfloat16

def level_sums():
    t=np.arange(C)[:,None]; u=np.arange(C)[None,:]
    rows=[]
    for h in LEVELS:
        ref=(t//(2*h))*(2*h)+h-1
        second=t>ref
        rows.append(np.where(second,(u>ref)&(u<=t),(u>t)&(u<=ref)))
    rows.append(u<=t); rows.append(u>t)
    return np.concatenate(rows,0).astype(np.float32)

def dot(a,b): return lax.dot_general(a,b,(((1,),(0,)),((),())),preferred_element_type=F32)
def dot_nt(a,b): return lax.dot_general(a,b,(((1,),(1,)),((),())),preferred_element_type=F32)
def dot_tn(a,b): return lax.dot_general(a,b,(((0,),(0,)),((),())),preferred_element_type=F32)

def gate_in(r_ref,wh_ref,bias_ref):
    return dot(r_ref[...],wh_ref[...])+bias_ref[...]

def log_rate(zb):
    return (jnp.minimum(zb,0.0)-jnp.log1p(jnp.exp(-jnp.abs(zb))))*(1.0/16.0)

def level_map(segc,segr):
    t=lax.broadcasted_iota(jnp.int32,(C,C),0); s=lax.broadcasted_iota(jnp.int32,(C,C),1)
    x=t^s
    return jnp.where(segc==segr,x,-1),t,s

def fwd_body(q_ref,k_ref,v_ref,g_ref,r_ref,wh_ref,bias_ref,gain_ref,cols_ref,segr_ref,m_ref,y_ref,o_ref,st_ref,state,esc):
    i=pl.program_id(0)
    @pl.when(i==0)
    def _(): state[...]=jnp.zeros_like(state)
    f=log_rate(gate_in(r_ref,wh_ref,bias_ref)).astype(BF)
    esc[...]=jnp.exp(dot(m_ref[...],f))
    segc=cols_ref[:,0:1]; segr=segr_ref[i]
    lv,t,s=level_map(segc,segr)
    lv=jnp.where(t>=s,lv,-1)
    prev=jnp.where(i==0,-1,segr_ref[jnp.maximum(i-1,0)][:,C-1:C])
    last=segr[:,C-1:C]
    keep=(segc==prev).astype(F32); tail=(segc==last).astype(F32)
    stay=(prev==last).astype(F32)
    row=lax.broadcasted_iota(jnp.int32,(C,KH),0)
    nl=len(LEVELS)
    for h in range(HEADS):
        ks=slice(h*KH,(h+1)*KH); vs=slice(h*VH,(h+1)*VH)
        q=q_ref[:,ks].astype(F32)*SCALE; k=k_ref[:,ks].astype(F32); v=v_ref[:,vs]
        a=jnp.where(lv==0,dot_nt(q.astype(BF),k_ref[:,ks]),0.0)
        for l,hs in enumerate(LEVELS):
            x=(jnp.where((row&hs)!=0,q,k)*esc[l*C:(l+1)*C,ks]).astype(BF)
            a=jnp.where((lv>=hs)&(lv<2*hs),dot_nt(x,x),a)
        ec=esc[nl*C:(nl+1)*C,ks]; es=esc[(nl+1)*C:(nl+2)*C,ks]
        st=state[h]
        stb=st.astype(BF)
        st_ref[0,h]=stb
        o=dot(a.astype(BF),v)+dot_nt((q*ec*keep).astype(BF),stb)
        state[h]=st*(ec[C-1:C,:]*stay)+dot_tn(v,(k*es*tail).astype(BF))
        o_ref[:,vs]=o.astype(BF)
        m=lax.rsqrt(jnp.mean(o*o,axis=-1,keepdims=True)+1.0)
        g=g_ref[:,vs].astype(F32)
        y_ref[:,vs]=(o*m*gain_ref[...]*(g*jax.nn.sigmoid(g))).astype(BF)

def bwd_body(q_ref,k_ref,v_ref,g_ref,r_ref,o_ref,st_ref,dy_ref,wh_ref,bias_ref,gain_ref,cols_ref,segr_ref,m_ref,u_ref,
             dq_ref,dk_ref,dv_ref,dg_ref,dz_ref,gb_ref,gg_ref,dstate,rcar,esc,dcs):
    nc=pl.num_programs(0); step=pl.program_id(0); i=nc-1-step
    @pl.when(step==0)
    def _():
        dstate[...]=jnp.zeros_like(dstate); rcar[...]=jnp.zeros_like(rcar)
        gb_ref[...]=jnp.zeros_like(gb_ref); gg_ref[...]=jnp.zeros_like(gg_ref)
    zb=gate_in(r_ref,wh_ref,bias_ref)
    f=log_rate(zb).astype(BF)
    esc[...]=jnp.exp(dot(m_ref[...],f))
    segc=cols_ref[:,0:1]; segr=segr_ref[i]
    lv,t,s=level_map(segc,segr)
    lvu=jnp.where(t<=s,lv,-1)
    lower=t>=s
    prev=jnp.where(i==0,-1,segr_ref[jnp.maximum(i-1,0)][:,C-1:C])
    last=segr[:,C-1:C]
    keep=(segc==prev).astype(F32); tail=(segc==last).astype(F32)
    stay=(prev==last).astype(F32)
    row=lax.broadcasted_iota(jnp.int32,(C,KH),0)
    nl=len(LEVELS)
    gain=gain_ref[...]
    ggacc=jnp.zeros((1,VH),F32)
    for h in range(HEADS):
        ks=slice(h*KH,(h+1)*KH); vs=slice(h*VH,(h+1)*VH)
        o=o_ref[:,vs].astype(F32); g=g_ref[:,vs].astype(F32); dy=dy_ref[:,vs].astype(F32)
        m=lax.rsqrt(jnp.mean(o*o,axis=-1,keepdims=True)+1.0)
        sg=jax.nn.sigmoid(g); om=o*m
        u=dy*(g*sg)
        dg_ref[:,vs]=(dy*om*gain*(sg*(1.0+g*(1.0-sg)))).astype(BF)
        ggacc=ggacc+jnp.sum(u*om,axis=0,keepdims=True)
        ug=u*gain
        do=(m*ug-om*(m*m)*jnp.mean(ug*o,axis=-1,keepdims=True)).astype(BF)
        q=q_ref[:,ks].astype(F32)*SCALE; k=k_ref[:,ks].astype(F32); v=v_ref[:,vs]
        qb=q.astype(BF); kb=k_ref[:,ks]
        das=jnp.where(lower,dot_nt(do,v),dot_nt(v,do))
        dd=jnp.sum(jnp.where(t==s,das,0.0),axis=1,keepdims=True)
        at=jnp.where(lvu==0,dot_nt(kb,qb),0.0)
        ec=esc[nl*C:(nl+1)*C,ks]; es=esc[(nl+1)*C:(nl+2)*C,ks]
        stb=st_ref[0,h]
        ds=dstate[h]; dsb=ds.astype(BF)
        qe=(q*ec*keep).astype(BF); ke=(k*es*tail).astype(BF)
        dq=dd*k+dot(do,stb)*(ec*keep)
        dk=dd*q+dot(v,dsb)*(es*tail)
        for l,hs in enumerate(LEVELS):
            e=esc[l*C:(l+1)*C,ks]
            sec=(row&hs)!=0
            x=(jnp.where(sec,q,k)*e).astype(BF)
            sx=dot_nt(x,x)
            at=jnp.where((lvu>=hs)&(lvu<2*hs),sx,at)
            gl=jnp.where((lv>=hs)&(lv<2*hs),das,0.0).astype(BF)
            tt=dot(gl,x)*e
            dq=dq+jnp.where(sec,tt,0.0)
            dk=dk+jnp.where(sec,0.0,tt)
        dv_ref[:,vs]=(dot(at.astype(BF),do)+dot_nt(ke,dsb)).astype(BF)
        dq_ref[:,ks]=(dq*SCALE).astype(BF)
        dk_ref[:,ks]=dk.astype(BF)
        dsn=ds*(ec[C-1:C,:]*stay)+dot_tn(do,qe)
        dstate[h]=dsn
        dc=q*dq-k*dk
        hi=dc.astype(BF)
        dcs[:,ks]=hi; dcs[:,HEADS*KH+h*KH:HEADS*KH+(h+1)*KH]=(dc-hi.astype(F32)).astype(BF)
        rold=rcar[:,ks]
        rcar[:,ks]=jnp.sum(stb.astype(F32)*dsn,axis=0,keepdims=True)
        dcs2=rold
        um=jnp.where((lv>=0)&(t<=s),1.0,0.0).astype(BF)
        df=dot(um,dcs[:,ks])+dot(um,dcs[:,HEADS*KH+h*KH:HEADS*KH+(h+1)*KH])+tail*dcs2
        start=cols_ref[:,1:2]!=segc
        dp=jnp.where(start,0.0,df)*(jax.nn.sigmoid(-zb[:,ks])*(1.0/16.0))
        dz_ref[:,ks]=dp.astype(BF)
        gb_ref[:,ks]+=jnp.sum(dp,axis=0,keepdims=True)
    gg_ref[...]+=ggacc

def seg_views(segments):
    b,l=segments.shape
    seg=(segments+8*lax.broadcasted_iota(jnp.int32,(b,l),0)).reshape(-1)
    prev=jnp.concatenate([jnp.full((1,),-1,jnp.int32),seg[:-1]])
    cols=jnp.stack([seg,prev],axis=1)
    return cols,seg.reshape(-1,1,C)

def forward(q,k,v,g,r,wh,bias,gain,cols,segr):
    T=q.shape[0]; nc=T//C
    M=jnp.asarray(level_sums(),BF); nr=M.shape[0]
    blk=lambda w: pl.BlockSpec((C,w),lambda i:(i,0))
    full=lambda *sh: pl.BlockSpec(sh,lambda i:(0,)*len(sh))
    return pl.pallas_call(fwd_body,grid=(nc,),
        in_specs=[blk(512),blk(512),blk(1024),blk(1024),blk(16),full(16,512),full(1,512),full(1,256),blk(2),full(nc,1,C),full(nr,C)],
        out_specs=[blk(1024),blk(1024),pl.BlockSpec((1,HEADS,VH,KH),lambda i:(i,0,0,0))],
        out_shape=[jax.ShapeDtypeStruct((T,1024),BF),jax.ShapeDtypeStruct((T,1024),BF),jax.ShapeDtypeStruct((nc,HEADS,VH,KH),BF)],
        scratch_shapes=[pltpu.VMEM((HEADS,VH,KH),F32),pltpu.VMEM((nr,512),F32)],
        compiler_params=pltpu.CompilerParams(vmem_limit_bytes=48<<20),
        cost_estimate=pl.CostEstimate(flops=20_000_000_000,bytes_accessed=16_000_000,transcendentals=0),
        name="gla_fwd")(q,k,v,g,r,wh,bias,gain,cols,segr,M)

def backward(q,k,v,g,r,o,st,dy,wh,bias,gain,cols,segr):
    T=q.shape[0]; nc=T//C
    M=jnp.asarray(level_sums(),BF); nr=M.shape[0]
    blk=lambda w: pl.BlockSpec((C,w),lambda i:(nc-1-i,0))
    full=lambda *sh: pl.BlockSpec(sh,lambda i:(0,)*len(sh))
    sd=jax.ShapeDtypeStruct
    return pl.pallas_call(bwd_body,grid=(nc,),
        in_specs=[blk(512),blk(512),blk(1024),blk(1024),blk(16),blk(1024),pl.BlockSpec((1,HEADS,VH,KH),lambda i:(nc-1-i,0,0,0)),blk(1024),
                  full(16,512),full(1,512),full(1,256),blk(2),full(nc,1,C),full(nr,C),full(8,128)],
        out_specs=[blk(512),blk(512),blk(1024),blk(1024),blk(512),full(1,512),full(1,256)],
        out_shape=[sd((T,512),BF),sd((T,512),BF),sd((T,1024),BF),sd((T,1024),BF),sd((T,512),BF),sd((1,512),F32),sd((1,256),F32)],
        scratch_shapes=[pltpu.VMEM((HEADS,VH,KH),F32),pltpu.VMEM((1,512),F32),pltpu.VMEM((nr,512),F32),pltpu.VMEM((C,1024),BF)],
        compiler_params=pltpu.CompilerParams(vmem_limit_bytes=48<<20),
        cost_estimate=pl.CostEstimate(flops=40_000_000_000,bytes_accessed=24_000_000,transcendentals=0),
        name="gla_bwd")(q,k,v,g,r,o,st,dy,wh,bias,gain,cols,segr,M,jnp.zeros((8,128),F32))

MESH = pl.DeviceIdType.MESH


class Place:
    def __init__(self, n, reps):
        self.n, self.z = n, reps // 2
        self.rep = lax.axis_index("rep")
        self.me = lax.axis_index("shard")
        self.core = lax.rem(self.rep, 2)
        self.chip = self.rep // 2
        self.sib = (self.rep + 1 - 2 * self.core, self.me)

    def peer(self, step):
        return lax.rem(self.me + step, self.n)

    def flip(self, bit):
        if bit == 1:
            return self.me + 1 - 2 * lax.rem(self.me, 2)
        return lax.rem(self.me + 2, 4)

    def first(self):
        return jnp.where(self.core == 0, self.flip(1), self.flip(2))

    def second(self):
        return jnp.where(self.core == 0, self.flip(2), self.flip(1))


def greet(ids):
    barrier = pltpu.get_barrier_semaphore()
    for d in ids:
        pl.semaphore_signal(barrier, inc=1, device_id=d, device_id_type=MESH)
    pl.semaphore_wait(barrier, len(ids))


def remote(src, dst, ssem, rsem, device):
    return pltpu.make_async_remote_copy(
        src_ref=src, dst_ref=dst, send_sem=ssem, recv_sem=rsem, device_id=device, device_id_type=MESH
    )


def gather_sems(n, count):
    kinds = 2 * (n - 1)
    return [
        pltpu.SemaphoreType.DMA((count, kinds)),
        pltpu.SemaphoreType.DMA((count, kinds)),
        pltpu.SemaphoreType.DMA((count,)),
    ]


class Gather:
    def __init__(self, place, owns, fulls, sems):
        self.p, self.owns, self.fulls = place, owns, fulls
        self.ssem, self.rsem, self.lsem = sems

    def peers(self):
        p = self.p
        return [(p.rep, p.peer(j)) for j in range(1, p.n)] + [p.sib]

    def local(self, i):
        return pltpu.make_async_copy(self.owns[i], self.fulls[i].at[self.p.me], self.lsem.at[i])

    def direct(self, i, kind, target):
        p = self.p
        return remote(
            self.owns[i].at[p.core],
            self.fulls[i].at[p.me, p.core],
            self.ssem.at[i, kind],
            self.rsem.at[i, kind],
            (p.rep, target),
        )

    def onward(self, i, kind, block, device):
        p = self.p
        view = self.fulls[i].at[block, p.core]
        return remote(view, view, self.ssem.at[i, kind], self.rsem.at[i, kind], device)

    def start(self):
        p = self.p
        for i in range(len(self.owns)):
            if p.n == 4:
                self.direct(i, 0, p.first()).start()
                self.direct(i, 1, p.second()).start()
            else:
                for j in range(1, p.n):
                    self.direct(i, j - 1, p.peer(j)).start()
            self.local(i).start()

    def finish(self):
        p = self.p
        count = len(self.owns)
        last = p.n - 1
        if p.n == 4:
            blocks = [p.first(), p.second(), 3 - p.me]
            for i in range(count):
                self.direct(i, 1, blocks[1]).wait_recv()
                self.onward(i, 2, blocks[1], (p.rep, blocks[0])).start()
                self.onward(i, last + 1, blocks[1], p.sib).start()
                self.direct(i, 0, blocks[0]).wait_recv()
                self.onward(i, last, blocks[0], p.sib).start()
            for i in range(count):
                self.onward(i, 2, blocks[2], (p.rep, blocks[0])).wait_recv()
                self.onward(i, last + 2, blocks[2], p.sib).start()
        else:
            blocks = [p.peer(p.n - j) for j in range(1, p.n)]
            for i in range(count):
                for j in range(last):
                    self.direct(i, j, p.me).wait_recv()
                    self.onward(i, last + j, blocks[j], p.sib).start()
        for i in range(count):
            self.local(i).wait()
            for j in range(last):
                self.direct(i, j, p.me).wait_send()
                arrival = self.onward(i, last + j, blocks[j], p.sib)
                arrival.wait_send()
                arrival.wait_recv()


def halves(w):
    return w.reshape(2, w.shape[0] // 2, w.shape[1])


def gather_kernel(n, reps, count, *refs):
    pack = refs[0]
    owns = refs[1 : 1 + count]
    packs = refs[1 + count]
    fulls = refs[2 + count : 2 + 2 * count]
    psend, precv, plocal, *sems = refs[2 + 2 * count :]
    p = Place(n, reps)
    gather = Gather(p, owns, fulls, sems)
    greet(gather.peers())

    def small(j):
        return remote(pack, packs.at[p.me], psend.at[j - 1], precv.at[j - 1], (p.rep, p.peer(j)))

    for j in range(1, n):
        small(j).start()
    gather.start()
    here = pltpu.make_async_copy(pack, packs.at[p.me], plocal)
    here.start()
    gather.finish()
    here.wait()
    for j in range(1, n):
        small(j).wait()


def gather_weights(n, reps, pack, weights):
    count = len(weights)
    owns = [halves(w) for w in weights]
    outs = pl.pallas_call(
        functools.partial(gather_kernel, n, reps, count),
        out_shape=[jax.ShapeDtypeStruct((n,) + pack.shape, pack.dtype)]
        + [jax.ShapeDtypeStruct((n,) + o.shape, o.dtype) for o in owns],
        in_specs=[pl.BlockSpec(memory_space=pl.ANY)] * (1 + count),
        out_specs=[pl.BlockSpec(memory_space=pl.ANY)] * (1 + count),
        scratch_shapes=[
            pltpu.SemaphoreType.DMA((n - 1,)),
            pltpu.SemaphoreType.DMA((n - 1,)),
            pltpu.SemaphoreType.DMA,
        ]
        + gather_sems(n, count),
        compiler_params=pltpu.CompilerParams(collective_id=0, has_side_effects=True),
        name="gather_mixer",
    )(pack, *owns)
    return outs[0], [o.reshape(-1, w.shape[1]) for o, w in zip(outs[1:], weights)]


def add_rows(dst, a, b):
    rows, width = dst.shape
    slab = 32 if rows % 32 == 0 else 16

    def step(j, _):
        at = pl.ds(pl.multiple_of(j * slab, slab), slab)
        dst[at, :] = (a[at, :].astype(F32) + b[at, :].astype(F32)).astype(dst.dtype)
        return 0

    lax.fori_loop(0, rows // slab, step, 0)


class Reduce:
    STAGES = 7

    def __init__(self, place, part, out, cols, bufs, sems):
        self.p, self.part, self.out, self.cols = place, part, out, cols
        self.mine, self.other, self.group, self.ring = bufs
        self.ssem, self.rsem, self.lsem = sems
        self.square = place.n == 4
        self.line = place.z == 4
        self.zbase = place.n
        self.end = self.zbase + (3 if self.line else place.z - 1)
        self.total = self.ring.at[self.ring.shape[0] - 1]

    def copy(self, kind, src, dst, device):
        return remote(src, dst, self.ssem.at[kind], self.rsem.at[kind], device)

    def load(self):
        return pltpu.make_async_copy(self.part.at[:, self.p.core, :, self.cols], self.mine, self.lsem.at[0])

    def swap(self):
        return self.copy(0, self.part.at[:, 1 - self.p.core, :, self.cols], self.other, self.p.sib)

    def start(self):
        self.swap().start()
        self.load().start()

    def group_sends(self):
        p = self.p
        if self.square:
            to = (p.rep, p.first())
            return [
                self.copy(1, self.mine.at[p.first()], self.group.at[0], to),
                self.copy(2, self.mine.at[3 - p.me], self.group.at[1], to),
            ]
        return [
            self.copy(j, self.mine.at[p.peer(j)], self.group.at[j - 1], (p.rep, p.peer(j)))
            for j in range(1, p.n)
        ]

    def second_send(self):
        p = self.p
        return self.copy(3, self.mine.at[p.second()], self.group.at[2], (p.rep, p.second()))

    def line_send(self, step):
        p, own = self.p, self.mine.at[self.p.me]
        if step == 0:
            return self.copy(self.zbase, own, self.ring.at[0], (jnp.where(p.chip == 0, p.rep + 2, p.rep - 2), p.me))
        if step == 1:
            return self.copy(self.zbase + 1, own, self.ring.at[1], (jnp.where(p.chip == 1, p.rep + 2, p.rep - 2), p.me))
        return self.copy(
            self.zbase + 2, self.total, self.total, (jnp.where(p.chip == 1, p.rep - 2, p.rep + 2), p.me)
        )

    def ring_sends(self):
        p = self.p
        return [
            self.copy(
                self.zbase + j - 1, self.mine.at[p.me], self.ring.at[p.chip], (lax.rem(p.rep + 2 * j, 2 * p.z), p.me)
            )
            for j in range(1, p.z)
        ]

    def last_swap(self):
        half = self.out.at[self.p.core, :, self.cols]
        return self.copy(self.end, self.total, half, self.p.sib)

    def store(self):
        return pltpu.make_async_copy(self.total, self.out.at[self.p.core, :, self.cols], self.lsem.at[1])

    def stage(self, k):
        p = self.p
        own = self.mine.at[p.me]
        outer = (p.chip == 0) | (p.chip == 3)
        if k == 0:
            self.load().wait()
            self.swap().wait_recv()
            for b in range(p.n):
                add_rows(self.mine.at[b], self.mine.at[b], self.other.at[b])
            for c in self.group_sends():
                c.start()
        elif k == 1:
            sends = self.group_sends()
            for c in sends:
                c.wait_recv()
            add_rows(own, own, self.group.at[0])
            if self.square:
                rest = self.mine.at[p.second()]
                add_rows(rest, rest, self.group.at[1])
                self.second_send().start()
            else:
                for j in range(1, p.n - 1):
                    add_rows(own, own, self.group.at[j])
        elif k == 2:
            if self.square:
                self.second_send().wait_recv()
                add_rows(own, own, self.group.at[2])
            if self.line:

                @pl.when(outer)
                def _():
                    self.line_send(0).start()

            else:
                for c in self.ring_sends():
                    c.start()
        elif k == 3:
            if self.line:

                @pl.when(jnp.logical_not(outer))
                def _():
                    self.line_send(0).wait_recv()
                    add_rows(own, own, self.ring.at[0])
                    self.line_send(1).start()

            else:
                for c in self.ring_sends():
                    c.wait_recv()
                self.ring[p.chip] = self.mine[p.me]
                add_rows(self.total, self.ring.at[0], self.ring.at[1])
                for j in range(2, p.z):
                    add_rows(self.total, self.total, self.ring.at[j])
        elif k == 4:
            if self.line:

                @pl.when(jnp.logical_not(outer))
                def _():
                    self.line_send(1).wait_recv()
                    add_rows(self.total, own, self.ring.at[1])
                    self.line_send(2).start()

        elif k == 5:
            if self.line:

                @pl.when(outer)
                def _():
                    self.line_send(2).wait_recv()

            self.last_swap().start()
            self.store().start()
        else:
            self.last_swap().wait_recv()
            self.store().wait()

    def settle(self):
        p = self.p
        outer = (p.chip == 0) | (p.chip == 3)
        self.swap().wait_send()
        for c in self.group_sends():
            c.wait_send()
        if self.square:
            self.second_send().wait_send()
        if self.line:

            @pl.when(outer)
            def _():
                self.line_send(0).wait_send()

            @pl.when(jnp.logical_not(outer))
            def _():
                self.line_send(1).wait_send()
                self.line_send(2).wait_send()

        else:
            for c in self.ring_sends():
                c.wait_send()
        self.last_swap().wait_send()

    @staticmethod
    def peers(p):
        group = [(p.rep, p.peer(j)) for j in range(1, p.n)]
        along = [(lax.rem(p.rep + 2 * j, 2 * p.z), p.me) for j in range(1, p.z)]
        return group + along + [p.sib]

    @staticmethod
    def scratch(n, z, half, width):
        slots = 3 if z == 4 else z + 1
        kinds = n + (3 if z == 4 else z - 1) + 1
        return [
            pltpu.VMEM((n, half, width), BF),
            pltpu.VMEM((n, half, width), BF),
            pltpu.VMEM((n - 1, half, width), BF),
            pltpu.VMEM((slots, half, width), BF),
            pltpu.SemaphoreType.DMA((kinds,)),
            pltpu.SemaphoreType.DMA((kinds,)),
            pltpu.SemaphoreType.DMA((2,)),
        ]


class Small:
    def __init__(self, place, part, out, bufs, sems):
        self.p, self.part, self.out = place, part, out
        self.pair, self.other, self.group, self.ring = bufs
        self.ssem, self.rsem = sems

    def copy(self, kind, src, dst, device):
        return remote(src, dst, self.ssem.at[kind], self.rsem.at[kind], device)

    def swap(self):
        return self.copy(0, self.part, self.other, self.p.sib)

    def sends(self):
        p = self.p
        return [
            self.copy(j, self.pair.at[p.peer(j)], self.group.at[j - 1], (p.rep, p.peer(j))) for j in range(1, p.n)
        ]

    def along(self):
        p = self.p
        return [
            self.copy(p.n + j - 1, self.pair.at[p.me], self.ring.at[p.chip], (lax.rem(p.rep + 2 * j, 2 * p.z), p.me))
            for j in range(1, p.z)
        ]

    def stage(self, k):
        p = self.p
        if k == 0:
            self.swap().wait_recv()
            self.pair[...] = self.part[...] + self.other[...]
            for c in self.sends():
                c.start()
        elif k == 1:
            for c in self.sends():
                c.wait_recv()
            own = self.pair[p.me]
            for j in range(p.n - 1):
                own = own + self.group[j]
            self.pair[p.me] = own
            self.ring[p.chip] = own
            for c in self.along():
                c.start()
        else:
            for c in self.along():
                c.wait_recv()
            own = self.ring[0]
            for j in range(1, p.z):
                own = own + self.ring[j]
            self.out[...] = own

    def settle(self):
        self.swap().wait_send()
        for c in self.sends() + self.along():
            c.wait_send()

    @staticmethod
    def scratch(n, z, rows):
        return [
            pltpu.VMEM((n, rows, 128), F32),
            pltpu.VMEM((n, rows, 128), F32),
            pltpu.VMEM((n - 1, rows, 128), F32),
            pltpu.VMEM((z, rows, 128), F32),
            pltpu.SemaphoreType.DMA((n + z - 1,)),
            pltpu.SemaphoreType.DMA((n + z - 1,)),
        ]


def waves(items, small=None):
    stages = Reduce.STAGES
    for t in range(len(items) + stages - 1):
        for k in reversed(range(stages)):
            if 0 <= t - k < len(items):
                items[t - k].stage(k)
        if small is not None and t < 3:
            small.stage(t)


def reduce_kernel(n, reps, cuts, *refs):
    count = 1 + max(c[0] for c in cuts)
    parts, pack = refs[:count], refs[count]
    outs, packed = refs[count + 1 : 2 * count + 1], refs[2 * count + 1]
    scratch = refs[2 * count + 2 :]
    p = Place(n, reps)
    items = []
    for j, (which, at, width) in enumerate(cuts):
        mem = scratch[7 * j : 7 * j + 7]
        items.append(Reduce(p, parts[which], outs[which], pl.ds(at, width), mem[:4], mem[4:]))
    mem = scratch[7 * len(cuts) :]
    small = Small(p, pack, packed, mem[:4], mem[4:])
    greet(Reduce.peers(p))
    small.swap().start()
    for item in items:
        item.start()
    waves(items, small)
    for item in items:
        item.settle()
    small.settle()


def reduce_all(n, reps, partials, pieces, pack):
    z = reps // 2
    views = [q.reshape(n, 2, q.shape[0] // (2 * n), q.shape[1]) for q in partials]
    cuts, scratch = [], []
    for which, (view, cut) in enumerate(zip(views, pieces)):
        width = view.shape[3] // cut
        for j in range(cut):
            cuts.append((which, j * width, width))
            scratch += Reduce.scratch(n, z, view.shape[2], width)
    scratch += Small.scratch(n, z, pack.shape[1])
    anywhere = pl.BlockSpec(memory_space=pl.ANY)
    vmem = pl.BlockSpec(memory_space=pltpu.VMEM)
    outs = pl.pallas_call(
        functools.partial(reduce_kernel, n, reps, tuple(cuts)),
        out_shape=[jax.ShapeDtypeStruct(v.shape[1:], BF) for v in views]
        + [jax.ShapeDtypeStruct(pack.shape[1:], F32)],
        in_specs=[anywhere] * len(views) + [vmem],
        out_specs=[anywhere] * len(views) + [vmem],
        scratch_shapes=scratch,
        compiler_params=pltpu.CompilerParams(collective_id=2, has_side_effects=True, vmem_limit_bytes=60 << 20),
        name="reduce_grads",
    )(*views, pack)
    return [o.reshape(-1, o.shape[2]) for o in outs[:-1]], outs[-1]


def matmul(left, right):
    return jnp.dot(left, right, preferred_element_type=F32)


def rms_parts(values):
    return lax.rsqrt(jnp.mean(values * values, axis=-1, keepdims=True) + 1e-05)


def local(
    shards,
    reps,
    tokens,
    segments,
    cotangent,
    norm_mix,
    w_query,
    w_key,
    w_value,
    w_outgate,
    w_low,
    w_high,
    decay_bias,
    head_gain,
    w_out,
    norm_mlp,
    w_gate,
    w_up,
    w_down,
):
    small = (norm_mix, norm_mlp, decay_bias, head_gain, w_low, w_high)
    sizes = [a.size for a in small]
    rows = -(-sum(sizes) // 2048) * 16
    packed = jnp.concatenate([a.reshape(-1) for a in small])
    packed = jnp.pad(packed, (0, rows * 128 - sum(sizes))).reshape(rows, 128)
    packs, (query_w, key_w, value_w, outgate_w, out_w, gate_w, up_w, down_w) = gather_weights(
        shards, reps, packed, (w_query, w_key, w_value, w_outgate, w_out, w_gate, w_up, w_down)
    )
    packs = packs.reshape(shards, -1)
    offsets = np.cumsum([0] + sizes)
    cut = [packs[:, offsets[i] : offsets[i + 1]] for i in range(len(small))]
    gain_mix = cut[0].reshape(-1).astype(F32)
    gain_feed = cut[1].reshape(-1).astype(F32)
    bias = cut[2].reshape(1, -1).astype(F32)
    gain_head = cut[3].reshape(1, -1).astype(F32)
    low_w = cut[4].reshape(-1, w_low.shape[1])
    high_w = cut[5].reshape(shards, w_high.shape[0], -1).transpose(1, 0, 2).reshape(w_high.shape[0], -1)
    total = tokens.shape[0] * tokens.shape[1]
    width = tokens.shape[2]
    cols, segr = seg_views(segments)
    inputs = tokens.reshape(total, width).astype(F32)
    inv_mix = rms_parts(inputs)
    first = (inputs * inv_mix * gain_mix).astype(BF)
    query = matmul(first, query_w).astype(BF)
    keys = matmul(first, key_w).astype(BF)
    values = matmul(first, value_w).astype(BF)
    outgate = matmul(first, outgate_w).astype(BF)
    lowrank = matmul(first, low_w).astype(BF)
    mixed, heads, states = forward(
        query, keys, values, outgate, lowrank, high_w, bias, gain_head, cols, segr
    )
    resid = inputs + matmul(mixed, out_w)
    inv_feed = rms_parts(resid)
    second = (resid * inv_feed * gain_feed).astype(BF)
    gate = matmul(second, gate_w)
    upward = matmul(second, up_w)
    sigma = jax.nn.sigmoid(gate)
    swish = gate * sigma
    hidden = (swish * upward).astype(BF)
    result = (resid + matmul(hidden, down_w)).astype(BF)
    grad_out = cotangent.reshape(total, width)
    part_down = dot_tn(hidden, grad_out)
    grad_hidden = dot_nt(grad_out, down_w)
    slope = sigma * (1.0 + gate * (1.0 - sigma))
    grad_gate = (grad_hidden * upward * slope).astype(BF)
    grad_up = (grad_hidden * swish).astype(BF)
    part_gate = dot_tn(second, grad_gate)
    part_up = dot_tn(second, grad_up)
    grad_second = dot_nt(grad_gate, gate_w) + dot_nt(grad_up, up_w)
    part_norm_mlp = jnp.sum(grad_second * resid * inv_feed, axis=0)
    scaled = grad_second * gain_feed
    grad_resid = (
        grad_out.astype(F32)
        + inv_feed * scaled
        - resid * inv_feed**3 * jnp.mean(scaled * resid, axis=-1, keepdims=True)
    )
    branch = grad_resid.astype(BF)
    part_out = dot_tn(mixed, branch)
    grad_mixed = dot_nt(branch, out_w).astype(BF)
    grad_q, grad_k, grad_v, grad_g, grad_z, part_bias, part_head = backward(
        query, keys, values, outgate, lowrank, heads, states, grad_mixed, high_w, bias, gain_head, cols, segr
    )
    part_high = dot_tn(lowrank, grad_z)
    grad_low = dot_nt(grad_z, high_w).astype(BF)
    part_low = dot_tn(first, grad_low)
    part_query = dot_tn(first, grad_q)
    part_key = dot_tn(first, grad_k)
    part_value = dot_tn(first, grad_v)
    part_outgate = dot_tn(first, grad_g)
    grad_first = (
        dot_nt(grad_q, query_w)
        + dot_nt(grad_k, key_w)
        + dot_nt(grad_v, value_w)
        + dot_nt(grad_g, outgate_w)
        + dot_nt(grad_low, low_w)
    )
    part_norm_mix = jnp.sum(grad_first * inputs * inv_mix, axis=0)
    scaled_mix = grad_first * gain_mix
    grad_inputs = (
        grad_resid
        + inv_mix * scaled_mix
        - inputs * inv_mix**3 * jnp.mean(scaled_mix * inputs, axis=-1, keepdims=True)
    )
    parts = (
        part_norm_mix,
        part_norm_mlp,
        part_bias,
        part_head,
        part_low,
        part_high.reshape(w_high.shape[0], shards, -1).transpose(1, 0, 2),
    )
    pack = jnp.concatenate([p.reshape(shards, -1) for p in parts], axis=1)
    pack = jnp.pad(pack, ((0, 0), (0, rows * 128 - sum(sizes)))).reshape(shards, rows, 128)
    partials = (part_down, part_gate, part_up, part_out, part_query, part_key, part_value, part_outgate)
    sums, mine = reduce_all(shards, reps, [p.astype(BF) for p in partials], (2, 2, 2, 1, 1, 1, 1, 1), pack)
    sum_down, sum_gate, sum_up, sum_out, sum_query, sum_key, sum_value, sum_outgate = [s.astype(F32) for s in sums]
    mine = mine.reshape(-1)
    own = [mine[offsets[i] : offsets[i + 1]].reshape(small[i].shape) for i in range(len(small))]
    return (
        result.reshape(tokens.shape),
        grad_inputs.reshape(tokens.shape),
        own[0],
        sum_query,
        sum_key,
        sum_value,
        sum_outgate,
        own[4],
        own[5],
        own[2],
        own[3],
        sum_out,
        own[1],
        sum_gate,
        sum_up,
        sum_down,
    )


def solution(mesh):
    in_specs = (
        P(("rep", "shard"), None, None),
        P(("rep", "shard"), None),
        P(("rep", "shard"), None, None),
        P("shard"),
        P("shard", None),
        P("shard", None),
        P("shard", None),
        P("shard", None),
        P("shard", None),
        P(None, "shard"),
        P("shard"),
        P("shard"),
        P("shard", None),
        P("shard"),
        P("shard", None),
        P("shard", None),
        P("shard", None),
    )
    out_specs = (
        P(("rep", "shard"), None, None),
        P(("rep", "shard"), None, None),
        P("shard"),
        P("shard", None),
        P("shard", None),
        P("shard", None),
        P("shard", None),
        P("shard", None),
        P(None, "shard"),
        P("shard"),
        P("shard"),
        P("shard", None),
        P("shard"),
        P("shard", None),
        P("shard", None),
        P("shard", None),
    )
    return jax.shard_map(
        functools.partial(local, mesh.shape["shard"], mesh.shape["rep"]), mesh=mesh, in_specs=in_specs, out_specs=out_specs, check_vma=False)
```

```python
import functools
import numpy as np
import jax, jax.numpy as jnp
from jax import lax
from jax.experimental import pallas as pl
from jax.experimental.pallas import tpu as pltpu
from jax.sharding import PartitionSpec as P
HEADS=4; KH=128; VH=256; C=128
SCALE=KH**-0.5
LEVELS=(64,32,16,8,4,2,1)
F32=jnp.float32; BF=jnp.bfloat16

def level_sums():
    t=np.arange(C)[:,None]; u=np.arange(C)[None,:]
    rows=[]
    for h in LEVELS:
        ref=(t//(2*h))*(2*h)+h-1
        second=t>ref
        rows.append(np.where(second,(u>ref)&(u<=t),(u>t)&(u<=ref)))
    rows.append(u<=t); rows.append(u>t)
    return np.concatenate(rows,0).astype(np.float32)

def dot(a,b): return lax.dot_general(a,b,(((1,),(0,)),((),())),preferred_element_type=F32)
def dot_nt(a,b): return lax.dot_general(a,b,(((1,),(1,)),((),())),preferred_element_type=F32)
def dot_tn(a,b): return lax.dot_general(a,b,(((0,),(0,)),((),())),preferred_element_type=F32)

def gate_in(r_ref,wh_ref,bias_ref):
    return dot(r_ref[...],wh_ref[...])+bias_ref[...]

def log_rate(zb):
    return (jnp.minimum(zb,0.0)-jnp.log1p(jnp.exp(-jnp.abs(zb))))*(1.0/16.0)

def level_map(segc,segr):
    t=lax.broadcasted_iota(jnp.int32,(C,C),0); s=lax.broadcasted_iota(jnp.int32,(C,C),1)
    x=t^s
    return jnp.where(segc==segr,x,-1),t,s

def fwd_body(q_ref,k_ref,v_ref,g_ref,r_ref,wh_ref,bias_ref,gain_ref,cols_ref,segr_ref,m_ref,y_ref,o_ref,st_ref,state,esc):
    i=pl.program_id(0)
    @pl.when(i==0)
    def _(): state[...]=jnp.zeros_like(state)
    f=log_rate(gate_in(r_ref,wh_ref,bias_ref)).astype(BF)
    esc[...]=jnp.exp(dot(m_ref[...],f))
    segc=cols_ref[:,0:1]; segr=segr_ref[i]
    lv,t,s=level_map(segc,segr)
    lv=jnp.where(t>=s,lv,-1)
    prev=jnp.where(i==0,-1,segr_ref[jnp.maximum(i-1,0)][:,C-1:C])
    last=segr[:,C-1:C]
    keep=(segc==prev).astype(F32); tail=(segc==last).astype(F32)
    stay=(prev==last).astype(F32)
    row=lax.broadcasted_iota(jnp.int32,(C,KH),0)
    nl=len(LEVELS)
    for h in range(HEADS):
        ks=slice(h*KH,(h+1)*KH); vs=slice(h*VH,(h+1)*VH)
        q=q_ref[:,ks].astype(F32)*SCALE; k=k_ref[:,ks].astype(F32); v=v_ref[:,vs]
        a=jnp.where(lv==0,dot_nt(q.astype(BF),k_ref[:,ks]),0.0)
        for l,hs in enumerate(LEVELS):
            x=(jnp.where((row&hs)!=0,q,k)*esc[l*C:(l+1)*C,ks]).astype(BF)
            a=jnp.where((lv>=hs)&(lv<2*hs),dot_nt(x,x),a)
        ec=esc[nl*C:(nl+1)*C,ks]; es=esc[(nl+1)*C:(nl+2)*C,ks]
        st=state[h]
        stb=st.astype(BF)
        st_ref[0,h]=stb
        o=dot(a.astype(BF),v)+dot_nt((q*ec*keep).astype(BF),stb)
        state[h]=st*(ec[C-1:C,:]*stay)+dot_tn(v,(k*es*tail).astype(BF))
        o_ref[:,vs]=o.astype(BF)
        m=lax.rsqrt(jnp.mean(o*o,axis=-1,keepdims=True)+1.0)
        g=g_ref[:,vs].astype(F32)
        y_ref[:,vs]=(o*m*gain_ref[...]*(g*jax.nn.sigmoid(g))).astype(BF)

def bwd_chunk(i,q_ref,k_ref,v_ref,g_ref,r_ref,o_ref,st_ref,dy_ref,wh_ref,bias_ref,gain_ref,cols_ref,segr_ref,m_ref,
             dq_ref,dk_ref,dv_ref,dg_ref,dz_ref,gb_ref,gg_ref,dstate,rcar,esc,dcs):
    zb=gate_in(r_ref,wh_ref,bias_ref)
    f=log_rate(zb).astype(BF)
    esc[...]=jnp.exp(dot(m_ref[...],f))
    segc=cols_ref[:,0:1]; segr=segr_ref[i]
    lv,t,s=level_map(segc,segr)
    lvu=jnp.where(t<=s,lv,-1)
    lower=t>=s
    prev=jnp.where(i==0,-1,segr_ref[jnp.maximum(i-1,0)][:,C-1:C])
    last=segr[:,C-1:C]
    keep=(segc==prev).astype(F32); tail=(segc==last).astype(F32)
    stay=(prev==last).astype(F32)
    row=lax.broadcasted_iota(jnp.int32,(C,KH),0)
    nl=len(LEVELS)
    gain=gain_ref[...]
    ggacc=jnp.zeros((1,VH),F32)
    for h in range(HEADS):
        ks=slice(h*KH,(h+1)*KH); vs=slice(h*VH,(h+1)*VH)
        o=o_ref[:,vs].astype(F32); g=g_ref[:,vs].astype(F32); dy=dy_ref[:,vs].astype(F32)
        m=lax.rsqrt(jnp.mean(o*o,axis=-1,keepdims=True)+1.0)
        sg=jax.nn.sigmoid(g); om=o*m
        u=dy*(g*sg)
        dg_ref[:,vs]=(dy*om*gain*(sg*(1.0+g*(1.0-sg)))).astype(BF)
        ggacc=ggacc+jnp.sum(u*om,axis=0,keepdims=True)
        ug=u*gain
        do=(m*ug-om*(m*m)*jnp.mean(ug*o,axis=-1,keepdims=True)).astype(BF)
        q=q_ref[:,ks].astype(F32)*SCALE; k=k_ref[:,ks].astype(F32); v=v_ref[:,vs]
        qb=q.astype(BF); kb=k_ref[:,ks]
        das=jnp.where(lower,dot_nt(do,v),dot_nt(v,do))
        dd=jnp.sum(jnp.where(t==s,das,0.0),axis=1,keepdims=True)
        at=jnp.where(lvu==0,dot_nt(kb,qb),0.0)
        ec=esc[nl*C:(nl+1)*C,ks]; es=esc[(nl+1)*C:(nl+2)*C,ks]
        stb=st_ref[0,h]
        ds=dstate[h]; dsb=ds.astype(BF)
        qe=(q*ec*keep).astype(BF); ke=(k*es*tail).astype(BF)
        dq=dd*k+dot(do,stb)*(ec*keep)
        dk=dd*q+dot(v,dsb)*(es*tail)
        for l,hs in enumerate(LEVELS):
            e=esc[l*C:(l+1)*C,ks]
            sec=(row&hs)!=0
            x=(jnp.where(sec,q,k)*e).astype(BF)
            sx=dot_nt(x,x)
            at=jnp.where((lvu>=hs)&(lvu<2*hs),sx,at)
            gl=jnp.where((lv>=hs)&(lv<2*hs),das,0.0).astype(BF)
            tt=dot(gl,x)*e
            dq=dq+jnp.where(sec,tt,0.0)
            dk=dk+jnp.where(sec,0.0,tt)
        dv_ref[:,vs]=(dot(at.astype(BF),do)+dot_nt(ke,dsb)).astype(BF)
        dq_ref[:,ks]=(dq*SCALE).astype(BF)
        dk_ref[:,ks]=dk.astype(BF)
        dsn=ds*(ec[C-1:C,:]*stay)+dot_tn(do,qe)
        dstate[h]=dsn
        dc=q*dq-k*dk
        hi=dc.astype(BF)
        dcs[:,ks]=hi; dcs[:,HEADS*KH+h*KH:HEADS*KH+(h+1)*KH]=(dc-hi.astype(F32)).astype(BF)
        rold=rcar[:,ks]
        rcar[:,ks]=jnp.sum(stb.astype(F32)*dsn,axis=0,keepdims=True)
        dcs2=rold
        um=jnp.where((lv>=0)&(t<=s),1.0,0.0).astype(BF)
        df=dot(um,dcs[:,ks])+dot(um,dcs[:,HEADS*KH+h*KH:HEADS*KH+(h+1)*KH])+tail*dcs2
        start=cols_ref[:,1:2]!=segc
        dp=jnp.where(start,0.0,df)*(jax.nn.sigmoid(-zb[:,ks])*(1.0/16.0))
        dz_ref[:,ks]=dp.astype(BF)
        gb_ref[:,ks]+=jnp.sum(dp,axis=0,keepdims=True)
    gg_ref[...]+=ggacc

def seg_views(segments):
    b,l=segments.shape
    seg=(segments+8*lax.broadcasted_iota(jnp.int32,(b,l),0)).reshape(-1)
    prev=jnp.concatenate([jnp.full((1,),-1,jnp.int32),seg[:-1]])
    cols=jnp.stack([seg,prev],axis=1)
    return cols,seg.reshape(-1,1,C)

def forward(q,k,v,g,r,wh,bias,gain,cols,segr):
    T=q.shape[0]; nc=T//C
    M=jnp.asarray(level_sums(),BF); nr=M.shape[0]
    blk=lambda w: pl.BlockSpec((C,w),lambda i:(i,0))
    full=lambda *sh: pl.BlockSpec(sh,lambda i:(0,)*len(sh))
    return pl.pallas_call(fwd_body,grid=(nc,),
        in_specs=[blk(512),blk(512),blk(1024),blk(1024),blk(16),full(16,512),full(1,512),full(1,256),blk(2),full(nc,1,C),full(nr,C)],
        out_specs=[blk(1024),blk(1024),pl.BlockSpec((1,HEADS,VH,KH),lambda i:(i,0,0,0))],
        out_shape=[jax.ShapeDtypeStruct((T,1024),BF),jax.ShapeDtypeStruct((T,1024),BF),jax.ShapeDtypeStruct((nc,HEADS,VH,KH),BF)],
        scratch_shapes=[pltpu.VMEM((HEADS,VH,KH),F32),pltpu.VMEM((nr,512),F32)],
        compiler_params=pltpu.CompilerParams(vmem_limit_bytes=48<<20),
        cost_estimate=pl.CostEstimate(flops=20_000_000_000,bytes_accessed=16_000_000,transcendentals=0),
        name="gla_fwd")(q,k,v,g,r,wh,bias,gain,cols,segr,M)


MESH = pl.DeviceIdType.MESH


class Place:
    def __init__(self, n, reps):
        self.n, self.z = n, reps // 2
        self.rep = lax.axis_index("rep")
        self.me = lax.axis_index("shard")
        self.core = lax.rem(self.rep, 2)
        self.chip = self.rep // 2
        self.sib = (self.rep + 1 - 2 * self.core, self.me)

    def peer(self, step):
        return lax.rem(self.me + step, self.n)

    def flip(self, bit):
        if bit == 1:
            return self.me + 1 - 2 * lax.rem(self.me, 2)
        return lax.rem(self.me + 2, 4)

    def first(self):
        return jnp.where(self.core == 0, self.flip(1), self.flip(2))

    def second(self):
        return jnp.where(self.core == 0, self.flip(2), self.flip(1))


def greet(ids):
    barrier = pltpu.get_barrier_semaphore()
    for d in ids:
        pl.semaphore_signal(barrier, inc=1, device_id=d, device_id_type=MESH)
    pl.semaphore_wait(barrier, len(ids))


def remote(src, dst, ssem, rsem, device):
    return pltpu.make_async_remote_copy(
        src_ref=src, dst_ref=dst, send_sem=ssem, recv_sem=rsem, device_id=device, device_id_type=MESH
    )


def gather_sems(n, count):
    kinds = 2 * (n - 1) + 1
    return [pltpu.SemaphoreType.DMA((count, kinds)), pltpu.SemaphoreType.DMA((count, kinds))]


class Gather:
    def __init__(self, place, owns, fulls, sems):
        self.p, self.owns, self.fulls = place, owns, fulls
        self.ssem, self.rsem = sems

    def peers(self):
        p = self.p
        return [(p.rep, p.peer(j)) for j in range(1, p.n)] + [p.sib]

    def same(self, i):
        kind = 2 * (self.p.n - 1)
        return remote(
            self.owns[i], self.fulls[i].at[self.p.me], self.ssem.at[i, kind], self.rsem.at[i, kind], self.p.sib
        )

    def direct(self, i, kind, target):
        p = self.p
        return remote(
            self.owns[i].at[p.core],
            self.fulls[i].at[p.me, p.core],
            self.ssem.at[i, kind],
            self.rsem.at[i, kind],
            (p.rep, target),
        )

    def onward(self, i, kind, block, device):
        p = self.p
        view = self.fulls[i].at[block, p.core]
        return remote(view, view, self.ssem.at[i, kind], self.rsem.at[i, kind], device)

    def start(self):
        p = self.p
        for i in range(len(self.owns)):
            if p.n == 4:
                self.direct(i, 0, p.first()).start()
                self.direct(i, 1, p.second()).start()
            else:
                for j in range(1, p.n):
                    self.direct(i, j - 1, p.peer(j)).start()
            self.same(i).start()

    def finish(self):
        p = self.p
        count = len(self.owns)
        last = p.n - 1
        if p.n == 4:
            blocks = [p.first(), p.second(), 3 - p.me]
            for i in range(count):
                self.direct(i, 1, blocks[1]).wait_recv()
                self.onward(i, 2, blocks[1], (p.rep, blocks[0])).start()
                self.onward(i, last + 1, blocks[1], p.sib).start()
                self.direct(i, 0, blocks[0]).wait_recv()
                self.onward(i, last, blocks[0], p.sib).start()
            for i in range(count):
                self.onward(i, 2, blocks[2], (p.rep, blocks[0])).wait_recv()
                self.onward(i, last + 2, blocks[2], p.sib).start()
        else:
            blocks = [p.peer(p.n - j) for j in range(1, p.n)]
            for i in range(count):
                for j in range(last):
                    self.direct(i, j, p.me).wait_recv()
                    self.onward(i, last + j, blocks[j], p.sib).start()
        for i in range(count):
            self.same(i).wait()
            for j in range(last):
                self.direct(i, j, p.me).wait_send()
                arrival = self.onward(i, last + j, blocks[j], p.sib)
                arrival.wait_send()
                arrival.wait_recv()


def halves(w):
    return w.reshape(2, w.shape[0] // 2, w.shape[1])


def gather_kernel(n, reps, count, *refs):
    pack = refs[0]
    owns = refs[1 : 1 + count]
    packs = refs[1 + count]
    fulls = refs[2 + count : 2 + 2 * count]
    psend, precv, plocal, *sems = refs[2 + 2 * count :]
    p = Place(n, reps)
    gather = Gather(p, owns, fulls, sems)
    greet(gather.peers())

    def small(j):
        return remote(pack, packs.at[p.me], psend.at[j - 1], precv.at[j - 1], (p.rep, p.peer(j)))

    for j in range(1, n):
        small(j).start()
    gather.start()
    here = pltpu.make_async_copy(pack, packs.at[p.me], plocal)
    here.start()
    gather.finish()
    here.wait()
    for j in range(1, n):
        small(j).wait()


def gather_weights(n, reps, pack, weights):
    count = len(weights)
    owns = [halves(w) for w in weights]
    outs = pl.pallas_call(
        functools.partial(gather_kernel, n, reps, count),
        out_shape=[jax.ShapeDtypeStruct((n,) + pack.shape, pack.dtype)]
        + [jax.ShapeDtypeStruct((n,) + o.shape, o.dtype) for o in owns],
        in_specs=[pl.BlockSpec(memory_space=pl.ANY)] * (1 + count),
        out_specs=[pl.BlockSpec(memory_space=pl.ANY)] * (1 + count),
        scratch_shapes=[
            pltpu.SemaphoreType.DMA((n - 1,)),
            pltpu.SemaphoreType.DMA((n - 1,)),
            pltpu.SemaphoreType.DMA,
        ]
        + gather_sems(n, count),
        compiler_params=pltpu.CompilerParams(collective_id=0, has_side_effects=True),
        name="gather_mixer",
    )(pack, *owns)
    return outs[0], [o.reshape(-1, w.shape[1]) for o, w in zip(outs[1:], weights)]


def add_rows(dst, a, b):
    rows = dst.shape[0]
    slab = 32 if rows % 32 == 0 else 16

    def step(j, _):
        at = pl.ds(pl.multiple_of(j * slab, slab), slab)
        dst[at, :] = (a[at, :].astype(F32) + b[at, :].astype(F32)).astype(dst.dtype)
        return 0

    lax.fori_loop(0, rows // slab, step, 0)


class Reduce:
    STAGES = 7

    def __init__(self, place, out, bufs, sems, mine=None, give=None, paired=None):
        self.p, self.out = place, out
        self.mine, self.give, self.paired = mine, give, paired
        self.square = place.n == 4
        self.line = place.z == 4
        bufs = list(bufs)
        if paired is None:
            self.other = bufs.pop(0)
            self.own, self.rest = mine.at[place.me], mine.at[place.second()]
        else:
            self.kept = bufs.pop(0)
            self.own, self.rest = self.kept.at[0], self.kept.at[1 if self.square else 0]
        self.group, self.ring = bufs
        self.ssem, self.rsem, self.lsem = sems
        self.zbase = place.n
        self.end = self.zbase + (3 if self.line else place.z - 1)
        self.total = self.ring.at[2] if self.line else self.group.at[0]

    def copy(self, kind, src, dst, device):
        return remote(src, dst, self.ssem.at[kind], self.rsem.at[kind], device)

    def loads(self):
        p = self.p
        which = [p.me, p.second()] if self.square else [p.me]
        return [
            pltpu.make_async_copy(self.paired.at[b], self.kept.at[j], self.lsem.at[j]) for j, b in enumerate(which)
        ]

    def swap(self):
        return self.copy(0, self.give, self.other, self.p.sib)

    def start(self):
        if self.paired is None:
            self.swap().start()
        else:
            for c in self.loads() + self.group_sends():
                c.start()

    def source(self, b):
        return self.mine.at[b] if self.paired is None else self.paired.at[b]

    def group_sends(self):
        p = self.p
        if self.square:
            to = (p.rep, p.first())
            return [
                self.copy(1, self.source(p.first()), self.group.at[0], to),
                self.copy(2, self.source(3 - p.me), self.group.at[1], to),
            ]
        return [
            self.copy(j, self.source(p.peer(j)), self.group.at[j - 1], (p.rep, p.peer(j))) for j in range(1, p.n)
        ]

    def second_send(self):
        p = self.p
        return self.copy(3, self.rest, self.group.at[2], (p.rep, p.second()))

    def line_send(self, step):
        p = self.p
        if step == 0:
            to = jnp.where(p.chip == 0, p.rep + 2, p.rep - 2)
            return self.copy(self.zbase, self.own, self.ring.at[0], (to, p.me))
        if step == 1:
            to = jnp.where(p.chip == 1, p.rep + 2, p.rep - 2)
            return self.copy(self.zbase + 1, self.own, self.ring.at[1], (to, p.me))
        to = jnp.where(p.chip == 1, p.rep - 2, p.rep + 2)
        return self.copy(self.zbase + 2, self.total, self.total, (to, p.me))

    def ring_sends(self):
        p = self.p
        return [
            self.copy(self.zbase + j - 1, self.own, self.ring.at[p.chip], (lax.rem(p.rep + 2 * j, 2 * p.z), p.me))
            for j in range(1, p.z)
        ]

    def last_swap(self):
        return self.copy(self.end, self.total, self.out(self.p.core), self.p.sib)

    def store(self):
        return pltpu.make_async_copy(self.total, self.out(self.p.core), self.lsem.at[2])

    def stage(self, k):
        p = self.p
        outer = (p.chip == 0) | (p.chip == 3)
        if k == 0:
            if self.paired is None:
                self.swap().wait_recv()
                for b in range(p.n):
                    add_rows(self.mine.at[b], self.mine.at[b], self.other.at[b])
                for c in self.group_sends():
                    c.start()
        elif k == 1:
            if self.paired is not None:
                for c in self.loads():
                    c.wait()
            for c in self.group_sends():
                c.wait_recv()
            add_rows(self.own, self.own, self.group.at[0])
            if self.square:
                add_rows(self.rest, self.rest, self.group.at[1])
                self.second_send().start()
            else:
                for j in range(1, p.n - 1):
                    add_rows(self.own, self.own, self.group.at[j])
        elif k == 2:
            if self.square:
                self.second_send().wait_recv()
                add_rows(self.own, self.own, self.group.at[2])
            if self.line:

                @pl.when(outer)
                def _():
                    self.line_send(0).start()

            else:
                for c in self.ring_sends():
                    c.start()
        elif k == 3:
            if self.line:

                @pl.when(jnp.logical_not(outer))
                def _():
                    self.line_send(0).wait_recv()
                    add_rows(self.own, self.own, self.ring.at[0])
                    self.line_send(1).start()

            else:
                for c in self.ring_sends():
                    c.wait_recv()
                self.ring[p.chip] = self.own[...]
                add_rows(self.total, self.ring.at[0], self.ring.at[1])
                for j in range(2, p.z):
                    add_rows(self.total, self.total, self.ring.at[j])
        elif k == 4:
            if self.line:

                @pl.when(jnp.logical_not(outer))
                def _():
                    self.line_send(1).wait_recv()
                    add_rows(self.total, self.own, self.ring.at[1])
                    self.line_send(2).start()

        elif k == 5:
            if self.line:

                @pl.when(outer)
                def _():
                    self.line_send(2).wait_recv()

            self.last_swap().start()
            self.store().start()
        else:
            self.last_swap().wait_recv()
            self.store().wait()

    def settle(self):
        p = self.p
        outer = (p.chip == 0) | (p.chip == 3)
        if self.paired is None:
            self.swap().wait_send()
        for c in self.group_sends():
            c.wait_send()
        if self.square:
            self.second_send().wait_send()
        if self.line:

            @pl.when(outer)
            def _():
                self.line_send(0).wait_send()

            @pl.when(jnp.logical_not(outer))
            def _():
                self.line_send(1).wait_send()
                self.line_send(2).wait_send()

        else:
            for c in self.ring_sends():
                c.wait_send()
        self.last_swap().wait_send()

    @staticmethod
    def peers(p):
        group = [(p.rep, p.peer(j)) for j in range(1, p.n)]
        along = [(lax.rem(p.rep + 2 * j, 2 * p.z), p.me) for j in range(1, p.z)]
        return group + along + [p.sib]

    @staticmethod
    def scratch(n, z, half, width, paired):
        slots = 3 if z == 4 else z
        kinds = n + (3 if z == 4 else z - 1) + 1
        return [
            pltpu.VMEM(((2 if n == 4 else 1) if paired else n, half, width), BF),
            pltpu.VMEM((n - 1, half, width), BF),
            pltpu.VMEM((slots, half, width), BF),
            pltpu.SemaphoreType.DMA((kinds,)),
            pltpu.SemaphoreType.DMA((kinds,)),
            pltpu.SemaphoreType.DMA((3,)),
        ]


class Small:
    def __init__(self, place, part, out, bufs, sems):
        self.p, self.part, self.out = place, part, out
        self.pair, self.other, self.group, self.ring = bufs
        self.ssem, self.rsem = sems

    def copy(self, kind, src, dst, device):
        return remote(src, dst, self.ssem.at[kind], self.rsem.at[kind], device)

    def swap(self):
        return self.copy(0, self.part, self.other, self.p.sib)

    def sends(self):
        p = self.p
        return [
            self.copy(j, self.pair.at[p.peer(j)], self.group.at[j - 1], (p.rep, p.peer(j))) for j in range(1, p.n)
        ]

    def along(self):
        p = self.p
        return [
            self.copy(p.n + j - 1, self.pair.at[p.me], self.ring.at[p.chip], (lax.rem(p.rep + 2 * j, 2 * p.z), p.me))
            for j in range(1, p.z)
        ]

    def stage(self, k):
        p = self.p
        if k == 0:
            self.swap().wait_recv()
            self.pair[...] = self.part[...] + self.other[...]
            for c in self.sends():
                c.start()
        elif k == 1:
            for c in self.sends():
                c.wait_recv()
            own = self.pair[p.me]
            for j in range(p.n - 1):
                own = own + self.group[j]
            self.pair[p.me] = own
            self.ring[p.chip] = own
            for c in self.along():
                c.start()
        else:
            for c in self.along():
                c.wait_recv()
            own = self.ring[0]
            for j in range(1, p.z):
                own = own + self.ring[j]
            self.out[...] = own

    def settle(self):
        self.swap().wait_send()
        for c in self.sends() + self.along():
            c.wait_send()

    @staticmethod
    def scratch(n, z, rows, width):
        return [
            pltpu.VMEM((n, rows, width), F32),
            pltpu.VMEM((n, rows, width), F32),
            pltpu.VMEM((n - 1, rows, width), F32),
            pltpu.VMEM((z, rows, width), F32),
            pltpu.SemaphoreType.DMA((n + z - 1,)),
            pltpu.SemaphoreType.DMA((n + z - 1,)),
        ]


def pair_kernel(n, reps, count, *refs):
    parts, outs = refs[:count], refs[count : 2 * count]
    scratch = refs[2 * count :]
    p = Place(n, reps)
    greet([p.sib])
    work = []
    for i in range(count):
        mine, other, sems, lsem = scratch[4 * i : 4 * i + 4]
        swap = remote(parts[i].at[:, 1 - p.core], other, sems.at[0], sems.at[1], p.sib)
        load = pltpu.make_async_copy(parts[i].at[:, p.core], mine, lsem.at[0])
        store = pltpu.make_async_copy(mine, outs[i], lsem.at[1])
        swap.start()
        load.start()
        work.append((mine, other, swap, load, store))
    for mine, other, swap, load, store in work:
        load.wait()
        swap.wait_recv()
        for b in range(n):
            add_rows(mine.at[b], mine.at[b], other.at[b])
        store.start()
    for mine, other, swap, load, store in work:
        store.wait()
        swap.wait_send()


def pair_sums(n, reps, partials):
    views = [q.reshape(n, 2, q.shape[0] // (2 * n), q.shape[1]) for q in partials]
    scratch = []
    for v in views:
        shape = (n,) + v.shape[2:]
        scratch += [pltpu.VMEM(shape, BF), pltpu.VMEM(shape, BF), pltpu.SemaphoreType.DMA((2,)), pltpu.SemaphoreType.DMA((2,))]
    anywhere = pl.BlockSpec(memory_space=pl.ANY)
    return pl.pallas_call(
        functools.partial(pair_kernel, n, reps, len(views)),
        out_shape=[jax.ShapeDtypeStruct((n,) + v.shape[2:], BF) for v in views],
        in_specs=[anywhere] * len(views),
        out_specs=[anywhere] * len(views),
        scratch_shapes=scratch,
        compiler_params=pltpu.CompilerParams(collective_id=1, has_side_effects=True, vmem_limit_bytes=40 << 20),
        name="pair_sums",
    )(*views)


def backward_kernel(n,reps,plan,half,*refs):
    (q_ref,k_ref,v_ref,g_ref,r_ref,o_ref,st_ref,dy_ref,a_ref,x_ref,dx_ref,cols_ref,
     wh_ref,bias_ref,gain_ref,gmix_ref,nmlp_ref,segr_ref,m_ref,wq_ref,wk_ref,wv_ref,wg_ref,wl_ref)=refs[:24]
    paired=refs[24:28]
    gt_ref,small_ref=refs[28:30]
    outs=refs[30:38]
    dstate,rcar,esc,dcs,dall,at_ref,dz_ref,low_acc,high_acc,gb_ref,gg_ref,nmix_ref,smb,both=refs[38:52]
    rest=refs[52:]
    steps=pl.num_programs(0); step=pl.program_id(0); nc=steps-1
    p=Place(n,reps)
    items=[]
    for j,(which,at,width,source) in enumerate(plan):
        mem=rest[6*j:6*j+6]
        cols=pl.ds(at,width)
        out=lambda c,which=which,cols=cols: outs[which].at[c,:,cols]
        if source is None:
            items.append(Reduce(p,out,mem[:3],mem[3:],paired=paired[which].at[:,:,cols]))
        else:
            cols=pl.ds(source,width)
            items.append(Reduce(p,out,mem[:3],mem[3:],mine=both.at[0,:,:,cols],give=both.at[1,:,:,cols]))
    mem=rest[6*len(plan):]
    small=Small(p,smb,small_ref,mem[:4],mem[4:])
    ready=[it for it in items if it.paired is not None]
    fresh=[it for it in items if it.paired is None]

    def slot(t):
        for k in range(Reduce.STAGES):
            if 0<=t-k<len(items): items[t-k].stage(k)

    @pl.when(step==0)
    def _():
        greet(Reduce.peers(p))
        for it in ready: it.start()
        for ref in (dstate,rcar,gb_ref,gg_ref,low_acc,high_acc,nmix_ref,smb): ref[...]=jnp.zeros_like(ref)

    @pl.when(step<nc)
    def _():
        i=nc-1-step
        rows=pl.ds(pl.multiple_of(i*C,C),C)
        bwd_chunk(i,q_ref,k_ref,v_ref,g_ref,r_ref,o_ref,st_ref,dy_ref,wh_ref,bias_ref,gain_ref,cols_ref,segr_ref,m_ref,
                  dall.at[rows,0:512],dall.at[rows,512:1024],dall.at[rows,1024:2048],dall.at[rows,2048:3072],dz_ref,gb_ref,gg_ref,dstate,rcar,esc,dcs)
        dz=dz_ref[...]; a=a_ref[...]
        dr=dot_nt(dz,wh_ref[...]).astype(BF)
        high_acc[...]+=dot_tn(r_ref[...],dz)
        low_acc[...]+=dot_tn(dr,a)
        at_ref[:,rows]=jnp.transpose(a)
        da=dot_nt(dall[rows,0:512],wq_ref[...])+dot_nt(dall[rows,512:1024],wk_ref[...])
        da=da+dot_nt(dall[rows,1024:2048],wv_ref[...])+dot_nt(dall[rows,2048:3072],wg_ref[...])+dot_nt(dr,wl_ref[...])
        x=x_ref[...].astype(F32)
        n1=lax.rsqrt(jnp.mean(x*x,axis=-1,keepdims=True)+1e-5)
        xn=x*n1
        nmix_ref[...]+=jnp.sum(da*xn,axis=0,keepdims=True)
        dm=da*gmix_ref[...]
        gt_ref[...]=dx_ref[...]+n1*(dm-xn*jnp.mean(dm*xn,axis=-1,keepdims=True))

    for t in range(8):
        @pl.when(step==t)
        def _(): slot(t)

    @pl.when(step==nc)
    def _():
        rs=2*half
        smb[:,16:32,:]=jnp.broadcast_to(high_acc[...][None],(n,16,512))
        smb[:,32:33,:]=jnp.broadcast_to(gb_ref[...][None],(n,1,512))
        smb[:,33:34,0:256]=jnp.broadcast_to(gg_ref[...][None],(n,1,256))
        for s in range(n):
            at=slice(s*rs,(s+1)*rs)
            smb[s,0:16,0:rs]=low_acc[:,at]
            smb[s,34:35,0:rs]=nmix_ref[:,at]
            smb[s,35:36,0:rs]=nmlp_ref[:,at]
        small.swap().start()

        def product(at,width):
            cols=slice(at,at+width)
            def one(s,_):
                rows=pl.ds(pl.multiple_of(s*rs,rs),rs)
                w=dot(at_ref[rows,:],dall[:,cols]).astype(BF)
                both[p.core,s,:,cols]=w[:half]
                both[1-p.core,s,:,cols]=w[half:]
                return 0
            lax.fori_loop(0,n,one,0)

        t=8; f=0
        for at,width,count in ((2048,1024,2),(1024,1024,2),(0,1024,2)):
            product(at,width)
            for it in fresh[f:f+count]: it.start()
            f+=count
            slot(t); t+=1
            small.stage((t-9))
        last=len(items)+Reduce.STAGES-1
        while t<last:
            slot(t); t+=1
        for it in items: it.settle()
        small.settle()

def backward(n,reps,q,k,v,g,r,o,st,dy,first,tokens,dx2,wh,bias,gain,gmix,nmlp,cols,segr,weights,pairs):
    T=q.shape[0]; nc=T//C; z=reps//2
    assert nc==8
    M=jnp.asarray(level_sums(),BF); nr=M.shape[0]
    blk=lambda w: pl.BlockSpec((C,w),lambda i:(jnp.maximum(nc-1-i,0),0))
    full=lambda *sh: pl.BlockSpec(sh,lambda i:(0,)*len(sh),pipeline_mode=pl.Buffered(1))
    sd=jax.ShapeDtypeStruct
    anywhere=pl.BlockSpec(memory_space=pl.ANY)
    half=first.shape[1]//(2*n)
    plan,scratch=[],[]
    for which,(pair,cut) in enumerate(zip(pairs,(4,4,4,2))):
        tiles=pair.shape[2]//128
        edges=[128*(tiles*j//cut) for j in range(cut+1)]
        for at,end in zip(edges[:-1],edges[1:]):
            plan.append((which,at,end-at,None)); scratch+=Reduce.scratch(n,z,pair.shape[1],end-at,True)
    for which,at,width,source in ((7,0,512,2048),(7,512,512,2560),(6,0,512,1024),(6,512,512,1536),(4,0,512,0),(5,0,512,512)):
        plan.append((which,at,width,source)); scratch+=Reduce.scratch(n,z,half,width,False)
    scratch+=Small.scratch(n,z,40,512)
    out=lambda h,w: sd((2,h,w),BF)
    res=pl.pallas_call(functools.partial(backward_kernel,n,reps,tuple(plan),half),grid=(nc+1,),
        in_specs=[blk(512),blk(512),blk(1024),blk(1024),blk(16),blk(1024),pl.BlockSpec((1,HEADS,VH,KH),lambda i:(jnp.maximum(nc-1-i,0),0,0,0)),blk(1024),
                  blk(1024),blk(1024),blk(1024),blk(2),
                  full(16,512),full(1,512),full(1,256),full(1,1024),full(1,1024),full(nc,1,C),full(nr,C),
                  full(1024,512),full(1024,512),full(1024,1024),full(1024,1024),full(1024,16)]+[anywhere]*4,
        out_specs=[blk(1024),pl.BlockSpec((40,512),lambda i:(0,0))]+[anywhere]*8,
        out_shape=[sd((T,1024),F32),sd((40,512),F32)]+[out(q.shape[1],q.shape[2]) for q in pairs]+[out(half,512),out(half,512),out(half,1024),out(half,1024)],
        scratch_shapes=[pltpu.VMEM((HEADS,VH,KH),F32),pltpu.VMEM((1,512),F32),pltpu.VMEM((nr,512),F32),pltpu.VMEM((C,1024),BF),
                        pltpu.VMEM((T,3072),BF),pltpu.VMEM((1024,T),BF),pltpu.VMEM((C,512),BF),pltpu.VMEM((16,1024),F32),pltpu.VMEM((16,512),F32),
                        pltpu.VMEM((1,512),F32),pltpu.VMEM((1,256),F32),pltpu.VMEM((1,1024),F32),pltpu.VMEM((n,40,512),F32),
                        pltpu.VMEM((2,n,half,3072),BF)]+scratch,
        compiler_params=pltpu.CompilerParams(collective_id=2,has_side_effects=True,vmem_limit_bytes=63<<20),
        name="gla_bwd_reduce")(q,k,v,g,r,o,st,dy,first,tokens,dx2,cols,wh,bias,gain,gmix,nmlp,segr,M,*weights,*pairs)
    return res[0],res[1],[x.reshape(-1,x.shape[2]) for x in res[2:]]


def matmul(left, right):
    return jnp.dot(left, right, preferred_element_type=F32)


def rms_parts(values):
    return lax.rsqrt(jnp.mean(values * values, axis=-1, keepdims=True) + 1e-05)


def local(
    shards,
    reps,
    tokens,
    segments,
    cotangent,
    norm_mix,
    w_query,
    w_key,
    w_value,
    w_outgate,
    w_low,
    w_high,
    decay_bias,
    head_gain,
    w_out,
    norm_mlp,
    w_gate,
    w_up,
    w_down,
):
    small = (norm_mix, norm_mlp, decay_bias, head_gain, w_low, w_high)
    sizes = [a.size for a in small]
    rows = -(-sum(sizes) // 2048) * 16
    packed = jnp.concatenate([a.reshape(-1) for a in small])
    packed = jnp.pad(packed, (0, rows * 128 - sum(sizes))).reshape(rows, 128)
    packs, (query_w, key_w, value_w, outgate_w, out_w, gate_w, up_w, down_w) = gather_weights(
        shards, reps, packed, (w_query, w_key, w_value, w_outgate, w_out, w_gate, w_up, w_down)
    )
    packs = packs.reshape(shards, -1)
    offsets = np.cumsum([0] + sizes)
    cut = [packs[:, offsets[i] : offsets[i + 1]] for i in range(len(small))]
    gain_mix = cut[0].reshape(-1).astype(F32)
    gain_feed = cut[1].reshape(-1).astype(F32)
    bias = cut[2].reshape(1, -1).astype(F32)
    gain_head = cut[3].reshape(1, -1).astype(F32)
    low_w = cut[4].reshape(-1, w_low.shape[1])
    high_w = cut[5].reshape(shards, w_high.shape[0], -1).transpose(1, 0, 2).reshape(w_high.shape[0], -1)
    total = tokens.shape[0] * tokens.shape[1]
    width = tokens.shape[2]
    cols, segr = seg_views(segments)
    inputs = tokens.reshape(total, width).astype(F32)
    inv_mix = rms_parts(inputs)
    first = (inputs * inv_mix * gain_mix).astype(BF)
    query = matmul(first, query_w).astype(BF)
    keys = matmul(first, key_w).astype(BF)
    values = matmul(first, value_w).astype(BF)
    outgate = matmul(first, outgate_w).astype(BF)
    lowrank = matmul(first, low_w).astype(BF)
    mixed, heads, states = forward(
        query, keys, values, outgate, lowrank, high_w, bias, gain_head, cols, segr
    )
    resid = inputs + matmul(mixed, out_w)
    inv_feed = rms_parts(resid)
    second = (resid * inv_feed * gain_feed).astype(BF)
    gate = matmul(second, gate_w)
    upward = matmul(second, up_w)
    sigma = jax.nn.sigmoid(gate)
    swish = gate * sigma
    hidden = (swish * upward).astype(BF)
    result = (resid + matmul(hidden, down_w)).astype(BF)
    grad_out = cotangent.reshape(total, width)
    part_down = dot_tn(hidden, grad_out)
    grad_hidden = dot_nt(grad_out, down_w)
    slope = sigma * (1.0 + gate * (1.0 - sigma))
    grad_gate = (grad_hidden * upward * slope).astype(BF)
    grad_up = (grad_hidden * swish).astype(BF)
    part_gate = dot_tn(second, grad_gate)
    part_up = dot_tn(second, grad_up)
    grad_second = dot_nt(grad_gate, gate_w) + dot_nt(grad_up, up_w)
    part_norm_mlp = jnp.sum(grad_second * resid * inv_feed, axis=0)
    scaled = grad_second * gain_feed
    grad_resid = (
        grad_out.astype(F32)
        + inv_feed * scaled
        - resid * inv_feed**3 * jnp.mean(scaled * resid, axis=-1, keepdims=True)
    )
    branch = grad_resid.astype(BF)
    part_out = dot_tn(mixed, branch)
    grad_mixed = dot_nt(branch, out_w).astype(BF)
    pairs = pair_sums(
        shards, reps, [q.astype(BF) for q in (part_down, part_gate, part_up, part_out)]
    )
    grad_inputs, small_sums, sums = backward(
        shards,
        reps,
        query,
        keys,
        values,
        outgate,
        lowrank,
        heads,
        states,
        grad_mixed,
        first,
        tokens.reshape(total, width),
        grad_resid,
        high_w,
        bias,
        gain_head,
        gain_mix[None],
        part_norm_mlp[None],
        cols,
        segr,
        (query_w, key_w, value_w, outgate_w, low_w),
        pairs,
    )
    sum_down, sum_gate, sum_up, sum_out, sum_query, sum_key, sum_value, sum_outgate = [s.astype(F32) for s in sums]
    me = lax.axis_index("shard")
    rs = w_low.shape[0]

    def across(block, width):
        return lax.dynamic_slice_in_dim(block, me * width, width, axis=1)

    own = (
        small_sums[34, :rs],
        small_sums[35, :rs],
        across(small_sums[32:33], decay_bias.shape[0]).reshape(-1),
        across(small_sums[33:34, :VH], head_gain.shape[0]).reshape(-1),
        small_sums[:16, :rs].T,
        across(small_sums[16:32], w_high.shape[1]),
    )
    return (
        result.reshape(tokens.shape),
        grad_inputs.reshape(tokens.shape),
        own[0],
        sum_query,
        sum_key,
        sum_value,
        sum_outgate,
        own[4],
        own[5],
        own[2],
        own[3],
        sum_out,
        own[1],
        sum_gate,
        sum_up,
        sum_down,
    )


def solution(mesh):
    in_specs = (
        P(("rep", "shard"), None, None),
        P(("rep", "shard"), None),
        P(("rep", "shard"), None, None),
        P("shard"),
        P("shard", None),
        P("shard", None),
        P("shard", None),
        P("shard", None),
        P("shard", None),
        P(None, "shard"),
        P("shard"),
        P("shard"),
        P("shard", None),
        P("shard"),
        P("shard", None),
        P("shard", None),
        P("shard", None),
    )
    out_specs = (
        P(("rep", "shard"), None, None),
        P(("rep", "shard"), None, None),
        P("shard"),
        P("shard", None),
        P("shard", None),
        P("shard", None),
        P("shard", None),
        P("shard", None),
        P(None, "shard"),
        P("shard"),
        P("shard"),
        P("shard", None),
        P("shard"),
        P("shard", None),
        P("shard", None),
        P("shard", None),
    )
    return jax.shard_map(
        functools.partial(local, mesh.shape["shard"], mesh.shape["rep"]), mesh=mesh, in_specs=in_specs, out_specs=out_specs, check_vma=False)
```

```python
import functools
import numpy as np
import jax, jax.numpy as jnp
from jax import lax
from jax.experimental import pallas as pl
from jax.experimental.pallas import tpu as pltpu
from jax.sharding import PartitionSpec as P
HEADS=4; KH=128; VH=256; C=128
SCALE=KH**-0.5
LEVELS=(64,32,16,8,4,2,1)
F32=jnp.float32; BF=jnp.bfloat16

def level_sums():
    t=np.arange(C)[:,None]; u=np.arange(C)[None,:]
    rows=[]
    for h in LEVELS:
        ref=(t//(2*h))*(2*h)+h-1
        second=t>ref
        rows.append(np.where(second,(u>ref)&(u<=t),(u>t)&(u<=ref)))
    rows.append(u<=t); rows.append(u>t)
    return np.concatenate(rows,0).astype(np.float32)

def dot(a,b): return lax.dot_general(a,b,(((1,),(0,)),((),())),preferred_element_type=F32)
def dot_nt(a,b): return lax.dot_general(a,b,(((1,),(1,)),((),())),preferred_element_type=F32)
def dot_tn(a,b): return lax.dot_general(a,b,(((0,),(0,)),((),())),preferred_element_type=F32)

def gate_in(r_ref,wh_ref,bias_ref):
    return dot(r_ref[...],wh_ref[...])+bias_ref[...]

def log_rate(zb):
    return (jnp.minimum(zb,0.0)-jnp.log1p(jnp.exp(-jnp.abs(zb))))*(1.0/16.0)

def level_map(segc,segr):
    t=lax.broadcasted_iota(jnp.int32,(C,C),0); s=lax.broadcasted_iota(jnp.int32,(C,C),1)
    x=t^s
    return jnp.where(segc==segr,x,-1),t,s

def fwd_chunk(i,q_ref,k_ref,v_ref,g_ref,r_ref,wh_ref,bias_ref,gain_ref,cols_ref,segr_ref,m_ref,y_ref,o_ref,st_ref,state,esc):
    f=log_rate(gate_in(r_ref,wh_ref,bias_ref)).astype(BF)
    esc[...]=jnp.exp(dot(m_ref[...],f))
    segc=cols_ref[:,0:1]; segr=segr_ref[i]
    lv,t,s=level_map(segc,segr)
    lv=jnp.where(t>=s,lv,-1)
    prev=jnp.where(i==0,-1,segr_ref[jnp.maximum(i-1,0)][:,C-1:C])
    last=segr[:,C-1:C]
    keep=(segc==prev).astype(F32); tail=(segc==last).astype(F32)
    stay=(prev==last).astype(F32)
    row=lax.broadcasted_iota(jnp.int32,(C,KH),0)
    nl=len(LEVELS)
    for h in range(HEADS):
        ks=slice(h*KH,(h+1)*KH); vs=slice(h*VH,(h+1)*VH)
        q=q_ref[:,ks].astype(F32)*SCALE; k=k_ref[:,ks].astype(F32); v=v_ref[:,vs]
        a=jnp.where(lv==0,dot_nt(q.astype(BF),k_ref[:,ks]),0.0)
        for l,hs in enumerate(LEVELS):
            x=(jnp.where((row&hs)!=0,q,k)*esc[l*C:(l+1)*C,ks]).astype(BF)
            a=jnp.where((lv>=hs)&(lv<2*hs),dot_nt(x,x),a)
        ec=esc[nl*C:(nl+1)*C,ks]; es=esc[(nl+1)*C:(nl+2)*C,ks]
        st=state[h]
        stb=st.astype(BF)
        st_ref[0,h]=stb
        o=dot(a.astype(BF),v)+dot_nt((q*ec*keep).astype(BF),stb)
        state[h]=st*(ec[C-1:C,:]*stay)+dot_tn(v,(k*es*tail).astype(BF))
        o_ref[:,vs]=o.astype(BF)
        m=lax.rsqrt(jnp.mean(o*o,axis=-1,keepdims=True)+1.0)
        g=g_ref[:,vs].astype(F32)
        y_ref[:,vs]=(o*m*gain_ref[...]*(g*jax.nn.sigmoid(g))).astype(BF)

def bwd_chunk(i,q_ref,k_ref,v_ref,g_ref,r_ref,o_ref,st_ref,dy_ref,wh_ref,bias_ref,gain_ref,cols_ref,segr_ref,m_ref,
             dq_ref,dk_ref,dv_ref,dg_ref,dz_ref,gb_ref,gg_ref,dstate,rcar,esc,dcs):
    zb=gate_in(r_ref,wh_ref,bias_ref)
    f=log_rate(zb).astype(BF)
    esc[...]=jnp.exp(dot(m_ref[...],f))
    segc=cols_ref[:,0:1]; segr=segr_ref[i]
    lv,t,s=level_map(segc,segr)
    lvu=jnp.where(t<=s,lv,-1)
    lower=t>=s
    prev=jnp.where(i==0,-1,segr_ref[jnp.maximum(i-1,0)][:,C-1:C])
    last=segr[:,C-1:C]
    keep=(segc==prev).astype(F32); tail=(segc==last).astype(F32)
    stay=(prev==last).astype(F32)
    row=lax.broadcasted_iota(jnp.int32,(C,KH),0)
    nl=len(LEVELS)
    gain=gain_ref[...]
    ggacc=jnp.zeros((1,VH),F32)
    for h in range(HEADS):
        ks=slice(h*KH,(h+1)*KH); vs=slice(h*VH,(h+1)*VH)
        o=o_ref[:,vs].astype(F32); g=g_ref[:,vs].astype(F32); dy=dy_ref[:,vs].astype(F32)
        m=lax.rsqrt(jnp.mean(o*o,axis=-1,keepdims=True)+1.0)
        sg=jax.nn.sigmoid(g); om=o*m
        u=dy*(g*sg)
        dg_ref[:,vs]=(dy*om*gain*(sg*(1.0+g*(1.0-sg)))).astype(BF)
        ggacc=ggacc+jnp.sum(u*om,axis=0,keepdims=True)
        ug=u*gain
        do=(m*ug-om*(m*m)*jnp.mean(ug*o,axis=-1,keepdims=True)).astype(BF)
        q=q_ref[:,ks].astype(F32)*SCALE; k=k_ref[:,ks].astype(F32); v=v_ref[:,vs]
        qb=q.astype(BF); kb=k_ref[:,ks]
        das=jnp.where(lower,dot_nt(do,v),dot_nt(v,do))
        dd=jnp.sum(jnp.where(t==s,das,0.0),axis=1,keepdims=True)
        at=jnp.where(lvu==0,dot_nt(kb,qb),0.0)
        ec=esc[nl*C:(nl+1)*C,ks]; es=esc[(nl+1)*C:(nl+2)*C,ks]
        stb=st_ref[0,h]
        ds=dstate[h]; dsb=ds.astype(BF)
        qe=(q*ec*keep).astype(BF); ke=(k*es*tail).astype(BF)
        dq=dd*k+dot(do,stb)*(ec*keep)
        dk=dd*q+dot(v,dsb)*(es*tail)
        for l,hs in enumerate(LEVELS):
            e=esc[l*C:(l+1)*C,ks]
            sec=(row&hs)!=0
            x=(jnp.where(sec,q,k)*e).astype(BF)
            sx=dot_nt(x,x)
            at=jnp.where((lvu>=hs)&(lvu<2*hs),sx,at)
            gl=jnp.where((lv>=hs)&(lv<2*hs),das,0.0).astype(BF)
            tt=dot(gl,x)*e
            dq=dq+jnp.where(sec,tt,0.0)
            dk=dk+jnp.where(sec,0.0,tt)
        dv_ref[:,vs]=(dot(at.astype(BF),do)+dot_nt(ke,dsb)).astype(BF)
        dq_ref[:,ks]=(dq*SCALE).astype(BF)
        dk_ref[:,ks]=dk.astype(BF)
        dsn=ds*(ec[C-1:C,:]*stay)+dot_tn(do,qe)
        dstate[h]=dsn
        dc=q*dq-k*dk
        hi=dc.astype(BF)
        dcs[:,ks]=hi; dcs[:,HEADS*KH+h*KH:HEADS*KH+(h+1)*KH]=(dc-hi.astype(F32)).astype(BF)
        rold=rcar[:,ks]
        rcar[:,ks]=jnp.sum(stb.astype(F32)*dsn,axis=0,keepdims=True)
        dcs2=rold
        um=jnp.where((lv>=0)&(t<=s),1.0,0.0).astype(BF)
        df=dot(um,dcs[:,ks])+dot(um,dcs[:,HEADS*KH+h*KH:HEADS*KH+(h+1)*KH])+tail*dcs2
        start=cols_ref[:,1:2]!=segc
        dp=jnp.where(start,0.0,df)*(jax.nn.sigmoid(-zb[:,ks])*(1.0/16.0))
        dz_ref[:,ks]=dp.astype(BF)
        gb_ref[:,ks]+=jnp.sum(dp,axis=0,keepdims=True)
    gg_ref[...]+=ggacc

def seg_views(segments):
    b,l=segments.shape
    seg=(segments+8*lax.broadcasted_iota(jnp.int32,(b,l),0)).reshape(-1)
    prev=jnp.concatenate([jnp.full((1,),-1,jnp.int32),seg[:-1]])
    cols=jnp.stack([seg,prev],axis=1)
    return cols,seg.reshape(-1,1,C)


MESH = pl.DeviceIdType.MESH


class Place:
    def __init__(self, n, reps):
        self.n, self.z = n, reps // 2
        self.rep = lax.axis_index("rep")
        self.me = lax.axis_index("shard")
        self.core = lax.rem(self.rep, 2)
        self.chip = self.rep // 2
        self.sib = (self.rep + 1 - 2 * self.core, self.me)

    def peer(self, step):
        return lax.rem(self.me + step, self.n)

    def flip(self, bit):
        if bit == 1:
            return self.me + 1 - 2 * lax.rem(self.me, 2)
        return lax.rem(self.me + 2, 4)

    def first(self):
        return jnp.where(self.core == 0, self.flip(1), self.flip(2))

    def second(self):
        return jnp.where(self.core == 0, self.flip(2), self.flip(1))


def greet(ids):
    barrier = pltpu.get_barrier_semaphore()
    for d in ids:
        pl.semaphore_signal(barrier, inc=1, device_id=d, device_id_type=MESH)
    pl.semaphore_wait(barrier, len(ids))


def remote(src, dst, ssem, rsem, device):
    return pltpu.make_async_remote_copy(
        src_ref=src, dst_ref=dst, send_sem=ssem, recv_sem=rsem, device_id=device, device_id_type=MESH
    )


def gather_sems(n, count):
    kinds = 2 * (n - 1) + 1
    return [pltpu.SemaphoreType.DMA((count, kinds)), pltpu.SemaphoreType.DMA((count, kinds))]


class Gather:
    def __init__(self, place, owns, fulls, sems):
        self.p, self.owns, self.fulls = place, owns, fulls
        self.ssem, self.rsem = sems

    def peers(self):
        p = self.p
        return [(p.rep, p.peer(j)) for j in range(1, p.n)] + [p.sib]

    def same(self, i):
        kind = 2 * (self.p.n - 1)
        return remote(
            self.owns[i], self.fulls[i].at[self.p.me], self.ssem.at[i, kind], self.rsem.at[i, kind], self.p.sib
        )

    def direct(self, i, kind, target):
        p = self.p
        return remote(
            self.owns[i].at[p.core],
            self.fulls[i].at[p.me, p.core],
            self.ssem.at[i, kind],
            self.rsem.at[i, kind],
            (p.rep, target),
        )

    def onward(self, i, kind, block, device):
        p = self.p
        view = self.fulls[i].at[block, p.core]
        return remote(view, view, self.ssem.at[i, kind], self.rsem.at[i, kind], device)

    def start(self, i):
        p = self.p
        if p.n == 4:
            self.direct(i, 0, p.first()).start()
            self.direct(i, 1, p.second()).start()
        else:
            for j in range(1, p.n):
                self.direct(i, j - 1, p.peer(j)).start()
        self.same(i).start()

    def blocks(self):
        p = self.p
        if p.n == 4:
            return [p.first(), p.second(), 3 - p.me]
        return [p.peer(p.n - j) for j in range(1, p.n)]

    def relay(self, i):
        p, blocks, last = self.p, self.blocks(), self.p.n - 1
        if p.n == 4:
            self.direct(i, 1, blocks[1]).wait_recv()
            self.onward(i, 2, blocks[1], (p.rep, blocks[0])).start()
            self.onward(i, last + 1, blocks[1], p.sib).start()
            self.direct(i, 0, blocks[0]).wait_recv()
            self.onward(i, last, blocks[0], p.sib).start()
        else:
            for j in range(last):
                self.direct(i, j, p.me).wait_recv()
                self.onward(i, last + j, blocks[j], p.sib).start()

    def pass_on(self, i):
        p, blocks, last = self.p, self.blocks(), self.p.n - 1
        if p.n == 4:
            self.onward(i, 2, blocks[2], (p.rep, blocks[0])).wait_recv()
            self.onward(i, last + 2, blocks[2], p.sib).start()

    def done(self, i):
        p, blocks, last = self.p, self.blocks(), self.p.n - 1
        self.same(i).wait()
        for j in range(last):
            self.direct(i, j, p.me).wait_send()
            arrival = self.onward(i, last + j, blocks[j], p.sib)
            arrival.wait_send()
            arrival.wait_recv()


def halves(w):
    return w.reshape(2, w.shape[0] // 2, w.shape[1])


def add_rows(dst, a, b):
    rows = dst.shape[0]
    slab = 32 if rows % 32 == 0 else 16

    def step(j, _):
        at = pl.ds(pl.multiple_of(j * slab, slab), slab)
        dst[at, :] = a[at, :] + b[at, :]
        return 0

    lax.fori_loop(0, rows // slab, step, 0)


class Reduce:
    STAGES = 7

    def __init__(self, place, out, bufs, sems, mine=None, give=None, part=None):
        self.p, self.out = place, out
        self.part = part
        self.square = place.n == 4
        self.line = place.z == 4
        bufs = list(bufs)
        if part is not None:
            mine, give = bufs.pop(0), part.at[:, 1 - place.core]
        self.mine, self.give = mine, give
        self.other, self.group, self.ring = bufs
        self.own = mine.at[place.me]
        self.rest = mine.at[place.second()] if self.square else None
        self.ssem, self.rsem, self.lsem = sems
        self.zbase = place.n
        self.end = self.zbase + (3 if self.line else place.z - 1)
        self.total = self.ring.at[2] if self.line else self.group.at[0]

    def copy(self, kind, src, dst, device):
        return remote(src, dst, self.ssem.at[kind], self.rsem.at[kind], device)

    def load(self):
        return pltpu.make_async_copy(self.part.at[:, self.p.core], self.mine, self.lsem.at[0])

    def swap(self):
        return self.copy(0, self.give, self.other, self.p.sib)

    def start(self):
        self.swap().start()
        if self.part is not None:
            self.load().start()

    def group_sends(self):
        p = self.p
        if self.square:
            to = (p.rep, p.first())
            return [
                self.copy(1, self.mine.at[p.first()], self.group.at[0], to),
                self.copy(2, self.mine.at[3 - p.me], self.group.at[1], to),
            ]
        return [
            self.copy(j, self.mine.at[p.peer(j)], self.group.at[j - 1], (p.rep, p.peer(j))) for j in range(1, p.n)
        ]

    def second_send(self):
        p = self.p
        return self.copy(3, self.rest, self.group.at[2], (p.rep, p.second()))

    def line_send(self, step):
        p = self.p
        if step == 0:
            to = jnp.where(p.chip == 0, p.rep + 2, p.rep - 2)
            return self.copy(self.zbase, self.own, self.ring.at[0], (to, p.me))
        if step == 1:
            to = jnp.where(p.chip == 1, p.rep + 2, p.rep - 2)
            return self.copy(self.zbase + 1, self.own, self.ring.at[1], (to, p.me))
        to = jnp.where(p.chip == 1, p.rep - 2, p.rep + 2)
        return self.copy(self.zbase + 2, self.total, self.total, (to, p.me))

    def ring_sends(self):
        p = self.p
        return [
            self.copy(self.zbase + j - 1, self.own, self.ring.at[p.chip], (lax.rem(p.rep + 2 * j, 2 * p.z), p.me))
            for j in range(1, p.z)
        ]

    def last_swaps(self):
        return [
            self.copy(self.end + j, self.total.at[:, lanes], half(self.p.core), self.p.sib)
            for j, (half, lanes) in enumerate(self.out)
        ]

    def stores(self):
        return [
            pltpu.make_async_copy(self.total.at[:, lanes], half(self.p.core), self.lsem.at[2 + j])
            for j, (half, lanes) in enumerate(self.out)
        ]

    def stage(self, k):
        p = self.p
        outer = (p.chip == 0) | (p.chip == 3)
        if k == 0:
            if self.part is not None:
                self.load().wait()
            self.swap().wait_recv()
            for b in range(p.n):
                add_rows(self.mine.at[b], self.mine.at[b], self.other.at[b])
            for c in self.group_sends():
                c.start()
        elif k == 1:
            for c in self.group_sends():
                c.wait_recv()
            add_rows(self.own, self.own, self.group.at[0])
            if self.square:
                add_rows(self.rest, self.rest, self.group.at[1])
                self.second_send().start()
            else:
                for j in range(1, p.n - 1):
                    add_rows(self.own, self.own, self.group.at[j])
        elif k == 2:
            if self.square:
                self.second_send().wait_recv()
                add_rows(self.own, self.own, self.group.at[2])
            if self.line:

                @pl.when(outer)
                def _():
                    self.line_send(0).start()

            else:
                for c in self.ring_sends():
                    c.start()
        elif k == 3:
            if self.line:

                @pl.when(jnp.logical_not(outer))
                def _():
                    self.line_send(0).wait_recv()
                    add_rows(self.own, self.own, self.ring.at[0])
                    self.line_send(1).start()

            else:
                for c in self.ring_sends():
                    c.wait_recv()
                self.ring[p.chip] = self.own[...]
                add_rows(self.total, self.ring.at[0], self.ring.at[1])
                for j in range(2, p.z):
                    add_rows(self.total, self.total, self.ring.at[j])
        elif k == 4:
            if self.line:

                @pl.when(jnp.logical_not(outer))
                def _():
                    self.line_send(1).wait_recv()
                    add_rows(self.total, self.own, self.ring.at[1])
                    self.line_send(2).start()

        elif k == 5:
            if self.line:

                @pl.when(outer)
                def _():
                    self.line_send(2).wait_recv()

            for c in self.last_swaps() + self.stores():
                c.start()
        else:
            for c in self.last_swaps():
                c.wait_recv()
            for c in self.stores():
                c.wait()

    def settle(self):
        p = self.p
        outer = (p.chip == 0) | (p.chip == 3)
        self.swap().wait_send()
        for c in self.group_sends():
            c.wait_send()
        if self.square:
            self.second_send().wait_send()
        if self.line:

            @pl.when(outer)
            def _():
                self.line_send(0).wait_send()

            @pl.when(jnp.logical_not(outer))
            def _():
                self.line_send(1).wait_send()
                self.line_send(2).wait_send()

        else:
            for c in self.ring_sends():
                c.wait_send()
        for c in self.last_swaps():
            c.wait_send()

    @staticmethod
    def peers(p):
        group = [(p.rep, p.peer(j)) for j in range(1, p.n)]
        along = [(lax.rem(p.rep + 2 * j, 2 * p.z), p.me) for j in range(1, p.z)]
        return group + along + [p.sib]

    @staticmethod
    def kinds(n, z):
        return n + (3 if z == 4 else z - 1) + 2

    @staticmethod
    def scratch(n, z, half, width, loaded, lead=()):
        lead = tuple(lead)
        kinds = Reduce.kinds(n, z)
        return ([pltpu.VMEM(lead + (n, half, width), BF)] if loaded else []) + [
            pltpu.VMEM(lead + (n, half, width), BF),
            pltpu.VMEM(lead + (n - 1, half, width), BF),
            pltpu.VMEM(lead + (3 if z == 4 else z, half, width), BF),
            pltpu.SemaphoreType.DMA(lead + (kinds,)),
            pltpu.SemaphoreType.DMA(lead + (kinds,)),
            pltpu.SemaphoreType.DMA(lead + (4,)),
        ]


class Small:
    def __init__(self, place, part, out, bufs, sems):
        self.p, self.part, self.out = place, part, out
        self.pair, self.other, self.group, self.ring = bufs
        self.ssem, self.rsem = sems

    def copy(self, kind, src, dst, device):
        return remote(src, dst, self.ssem.at[kind], self.rsem.at[kind], device)

    def swap(self):
        return self.copy(0, self.part, self.other, self.p.sib)

    def sends(self):
        p = self.p
        return [
            self.copy(j, self.pair.at[p.peer(j)], self.group.at[j - 1], (p.rep, p.peer(j))) for j in range(1, p.n)
        ]

    def along(self):
        p = self.p
        return [
            self.copy(p.n + j - 1, self.pair.at[p.me], self.ring.at[p.chip], (lax.rem(p.rep + 2 * j, 2 * p.z), p.me))
            for j in range(1, p.z)
        ]

    def stage(self, k):
        p = self.p
        if k == 0:
            self.swap().wait_recv()
            self.pair[...] = self.part[...] + self.other[...]
            for c in self.sends():
                c.start()
        elif k == 1:
            for c in self.sends():
                c.wait_recv()
            own = self.pair[p.me]
            for j in range(p.n - 1):
                own = own + self.group[j]
            self.pair[p.me] = own
            self.ring[p.chip] = own
            for c in self.along():
                c.start()
        else:
            for c in self.along():
                c.wait_recv()
            own = self.ring[0]
            for j in range(1, p.z):
                own = own + self.ring[j]
            self.out[...] = own

    def settle(self):
        self.swap().wait_send()
        for c in self.sends() + self.along():
            c.wait_send()

    @staticmethod
    def scratch(n, z, rows, width):
        return [
            pltpu.VMEM((n, rows, width), F32),
            pltpu.VMEM((n, rows, width), F32),
            pltpu.VMEM((n - 1, rows, width), F32),
            pltpu.VMEM((z, rows, width), F32),
            pltpu.SemaphoreType.DMA((n + z - 1,)),
            pltpu.SemaphoreType.DMA((n + z - 1,)),
        ]


def feed_kernel(n, reps, half, tile, *refs):
    (b_ref, e_ref, x_ref, gain_ref, wg_ref, wu_ref, wd_ref) = refs[:7]
    res_out, dx_out, dm_out, norm_ref, down_out, gate_out, up_out = refs[7:14]
    bt, acc, hid, dgate, dup, both, other, group, ring, ssem, rsem, lsem = refs[14:26]
    xs, res_ref, dx_ref, dm_ref, down_ref, moved = refs[26:]
    step, tiles = pl.program_id(0), pl.num_programs(0) - 1
    p = Place(n, reps)
    total = b_ref.shape[0]
    rs = 2 * half
    rows_at = lambda j, size: pl.ds(pl.multiple_of(j * size, size), size)

    def fetch():
        return pltpu.make_async_copy(x_ref, xs, moved.at[0])

    def write(k, ref, out, rows):
        return pltpu.make_async_copy(ref.at[rows], out.at[rows], moved.at[k])

    def item(j):
        cols = pl.ds(pl.multiple_of(j * tile, tile), tile)
        out = [
            (lambda c: gate_out.at[c, :, cols], pl.ds(0, tile)),
            (lambda c: up_out.at[c, :, cols], pl.ds(tile, tile)),
        ]
        return Reduce(
            p,
            out,
            [other.at[j], group.at[j], ring.at[j]],
            [ssem.at[j], rsem.at[j], lsem.at[j]],
            mine=both.at[j, 0],
            give=both.at[j, 1],
        )

    def slot(t):
        for k in range(Reduce.STAGES):

            @pl.when((t >= k) & (t - k < tiles))
            def _():
                item(t - k).stage(k)

    @pl.when(step == 0)
    def _():
        greet(Reduce.peers(p))
        fetch().start()
        acc[...] = jnp.zeros_like(acc)
        dx_ref[...] = jnp.zeros_like(dx_ref)

        def turn(j, _):
            rows = rows_at(j, 128)
            bt[:, rows] = jnp.transpose(b_ref[rows, :])
            return 0

        lax.fori_loop(0, total // 128, turn, 0)

    @pl.when(step < tiles)
    def _():
        def rows_step(j, _):
            rows = rows_at(j, 512)
            b, e = b_ref[rows, :], e_ref[rows, :]
            gate = dot(b, wg_ref[...])
            up = dot(b, wu_ref[...])
            dh = dot_nt(e, wd_ref[...])
            sig = jax.nn.sigmoid(gate)
            swish = gate * sig
            h = (swish * up).astype(BF)
            dg = (dh * up * (sig * (1.0 + gate * (1.0 - sig)))).astype(BF)
            du = (dh * swish).astype(BF)
            down_ref[rows_at(step, tile), rows] = jnp.transpose(h)
            hid[rows, :] = h
            dgate[rows, :] = dg
            dup[rows, :] = du
            return 0

        def sums_step(j, _):
            rows = rows_at(j, 512)
            acc[rows, :] += dot(hid[rows, :], wd_ref[...])
            dx_ref[rows, :] += dot_nt(dgate[rows, :], wg_ref[...]) + dot_nt(dup[rows, :], wu_ref[...])
            return 0

        lax.fori_loop(0, total // 512, rows_step, 0)

        @pl.when(step > 0)
        def _():
            slot(step - 1)

        for at, d in ((0, dgate), (tile, dup)):
            w = dot(bt[...], d[...]).astype(BF)
            for s in range(n):
                both[step, p.core, s, :, at : at + tile] = w[s * rs : s * rs + half]
                both[step, 1 - p.core, s, :, at : at + tile] = w[s * rs + half : (s + 1) * rs]
        item(step).start()
        lax.fori_loop(0, total // 512, sums_step, 0)

    @pl.when(step == tiles)
    def _():
        norm_ref[...] = jnp.zeros_like(norm_ref)

        def finish(j, _):
            rows = rows_at(j, 128)
            x = xs[rows, :]
            res_ref[rows, :] = (x + acc[rows, :]).astype(BF)
            inv = lax.rsqrt(jnp.mean(x * x, axis=-1, keepdims=True) + 1e-5)
            xn = x * inv
            db = dx_ref[rows, :]
            norm_ref[...] += jnp.sum(db * xn, axis=0, keepdims=True)
            dbg = db * gain_ref[...]
            dx = e_ref[rows, :].astype(F32) + inv * (dbg - xn * jnp.mean(dbg * xn, axis=-1, keepdims=True))
            dx_ref[rows, :] = dx
            dm_ref[rows, :] = dx.astype(BF)
            return 0

        fetch().wait()

        def turn_down(j, _):
            slot(tiles - 1 + j)
            rows = rows_at(j, down_ref.shape[0] // 4)
            down_ref[rows, :] = dot(down_ref[rows, :], e_ref[...]).astype(BF)
            write(1 + j, down_ref, down_out, rows).start()
            return 0

        lax.fori_loop(0, 4, turn_down, 0)
        slot(tiles + 3)
        lax.fori_loop(0, total // 128, finish, 0)
        every = pl.ds(0, total)
        results = [
            write(5, res_ref, res_out, every),
            write(6, dx_ref, dx_out, every),
            write(7, dm_ref, dm_out, every),
        ]
        for c in results:
            c.start()

        def tail(t, _):
            slot(t)
            return 0

        lax.fori_loop(tiles + 4, tiles + Reduce.STAGES - 1, tail, 0)

        def settle(j, _):
            item(j).settle()
            return 0

        lax.fori_loop(0, tiles, settle, 0)
        for j in range(4):
            write(1 + j, down_ref, down_out, rows_at(j, down_ref.shape[0] // 4)).wait()
        for c in results:
            c.wait()


def feed(n, reps, b, e, x2, gain, wg, wu, wd):
    total, width = b.shape
    ff = wg.shape[1]
    tile, z = 256, reps // 2
    tiles, half = ff // tile, width // (2 * n)
    once = lambda *sh: pl.BlockSpec(sh, lambda j: (0,) * len(sh), pipeline_mode=pl.Buffered(1))
    col = lambda: pl.BlockSpec((width, tile), lambda j: (0, jnp.minimum(j, tiles - 1)))
    row = lambda: pl.BlockSpec((tile, width), lambda j: (jnp.minimum(j, tiles - 1), 0))
    anywhere = pl.BlockSpec(memory_space=pl.ANY)
    sd = jax.ShapeDtypeStruct
    return pl.pallas_call(
        functools.partial(feed_kernel, n, reps, half, tile),
        grid=(tiles + 1,),
        in_specs=[once(total, width)] * 2 + [anywhere, once(1, width), col(), col(), row()],
        out_specs=[anywhere] * 3 + [once(1, width), anywhere, anywhere, anywhere],
        out_shape=[
            sd((total, width), BF),
            sd((total, width), F32),
            sd((total, width), BF),
            sd((1, width), F32),
            sd((ff, total), BF),
            sd((2, half, ff), BF),
            sd((2, half, ff), BF),
        ],
        scratch_shapes=[
            pltpu.VMEM((width, total), BF),
            pltpu.VMEM((total, width), F32),
            pltpu.VMEM((total, tile), BF),
            pltpu.VMEM((total, tile), BF),
            pltpu.VMEM((total, tile), BF),
            pltpu.VMEM((tiles, 2, n, half, 2 * tile), BF),
        ]
        + Reduce.scratch(n, z, half, 2 * tile, False, (tiles,))
        + [
            pltpu.VMEM((total, width), F32),
            pltpu.VMEM((total, width), BF),
            pltpu.VMEM((total, width), F32),
            pltpu.VMEM((total, width), BF),
            pltpu.VMEM((ff, total), BF),
            pltpu.SemaphoreType.DMA((8,)),
        ],
        compiler_params=pltpu.CompilerParams(collective_id=1, has_side_effects=True, vmem_limit_bytes=63 << 20),
        name="feed_forward",
    )(b, e, x2, gain, wg, wu, wd)


def forward_kernel(n, reps, width, *refs):
    x_ref, cols_ref, segr_ref, m_ref, vec_ref, high_ref, low_ref = refs[:7]
    owns = refs[7:15]
    a_ref, q_ref, k_ref, v_ref, g_ref, r_ref, y_ref, o_ref, st_ref = refs[15:24]
    x2_ref, b_ref, vec_out, high_out, low_out = refs[24:29]
    outs = refs[29:37]
    state, esc, xs, ys, vecs, highs, lows = refs[37:44]
    kept = refs[44:49]
    small_send, small_recv, ssem, rsem, lsem = refs[49:]
    step, nc = pl.program_id(0), pl.num_programs(0) - 1
    p = Place(n, reps)
    gather = Gather(p, owns, list(kept) + list(outs[5:]), [ssem, rsem])
    smalls = [(vec_ref, vecs), (high_ref, highs), (low_ref, lows)]

    def small(k, j):
        src, dst = smalls[k]
        return remote(src, dst.at[p.me], small_send.at[k, j - 1], small_recv.at[k, j - 1], (p.rep, p.peer(j)))

    def keep(i):
        return pltpu.make_async_copy(kept[i], outs[i], lsem.at[i])

    def whole(i):
        w = kept[i][...]
        return w.reshape(-1, w.shape[-1])

    @pl.when(step == 0)
    def _():
        greet(gather.peers())
        for i in range(4):
            gather.start(i)
        for k in range(3):
            for j in range(1, n):
                small(k, j).start()
            src, dst = smalls[k]
            dst[p.me] = src[...]
        for i in range(4):
            gather.relay(i)
        for i in range(4, 8):
            gather.start(i)
        for k in range(3):
            for j in range(1, n):
                small(k, j).wait()
        rs = low_ref.shape[0]
        for s in range(n):
            at = slice(s * rs, (s + 1) * rs)
            vec_out[0:2, at] = vecs[s, 0:2, 0:rs]
            low_out[at, :] = lows[s]

        def spread(part, out_width):
            own = part(0).shape[1]
            total = None
            for s in range(n):
                col = lax.broadcasted_iota(jnp.int32, (own, out_width), 1)
                row = lax.broadcasted_iota(jnp.int32, (own, out_width), 0)
                piece = dot(part(s), (col == row + s * own).astype(F32).astype(BF))
                total = piece if total is None else total + piece
            return total

        nb, ng = 512 // n, VH // n
        vec_out[2:3, 0:512] = spread(lambda s: vecs[s, 2:3, 0:nb].astype(BF), 512)
        vec_out[3:4, 0:VH] = spread(lambda s: vecs[s, 3:4, 0:ng].astype(BF), VH)
        high_out[...] = spread(lambda s: highs[s], 512).astype(BF)
        for i in range(4):
            gather.pass_on(i)
        for i in range(4):
            gather.done(i)
            keep(i).start()
        state[...] = jnp.zeros_like(state)

    @pl.when(step < nc)
    def _():
        rows = pl.ds(pl.multiple_of(step * C, C), C)
        xb = x_ref[...]
        xs[rows, :] = xb
        x = xb.astype(F32)
        inv = lax.rsqrt(jnp.mean(x * x, axis=-1, keepdims=True) + 1e-5)
        a = (x * inv * vec_out[0:1, :]).astype(BF)
        a_ref[...] = a
        q_ref[...] = dot(a, whole(0)).astype(BF)
        k_ref[...] = dot(a, whole(1)).astype(BF)
        v_ref[...] = dot(a, whole(2)).astype(BF)
        g_ref[...] = dot(a, whole(3)).astype(BF)
        r_ref[...] = dot(a, low_out[...]).astype(BF)
        fwd_chunk(
            step, q_ref, k_ref, v_ref, g_ref, r_ref, high_out, vec_out.at[2:3, 0:512], vec_out.at[3:4, 0:VH],
            cols_ref, segr_ref, m_ref, y_ref, o_ref, st_ref, state, esc,
        )
        ys[rows, :] = y_ref[...]

    @pl.when(step == 2)
    def _():
        gather.relay(4)

    @pl.when(step == 4)
    def _():
        gather.pass_on(4)

    @pl.when(step == nc)
    def _():
        gather.relay(5)
        gather.done(4)
        keep(4).start()

        def join(j, _):
            rows = pl.ds(pl.multiple_of(j * 256, 256), 256)
            x2 = xs[rows, :].astype(F32) + dot(ys[rows, :], whole(4))
            x2_ref[rows, :] = x2
            inv = lax.rsqrt(jnp.mean(x2 * x2, axis=-1, keepdims=True) + 1e-5)
            b_ref[rows, :] = (x2 * inv * vec_out[1:2, :]).astype(BF)
            return 0

        lax.fori_loop(0, xs.shape[0] // 256, join, 0)
        gather.pass_on(5)
        gather.relay(6)
        gather.pass_on(6)
        gather.relay(7)
        gather.pass_on(7)
        for i in range(5, 8):
            gather.done(i)
        for i in range(5):
            keep(i).wait()


def forward(n, reps, x, cols, segr, vec, high, low, weights):
    T, width = x.shape
    nc = T // C
    M = jnp.asarray(level_sums(), BF)
    nr = M.shape[0]
    owns = [halves(w) for w in weights]
    last = lambda i: jnp.minimum(i, nc - 1)
    blk = lambda w: pl.BlockSpec((C, w), lambda i: (last(i), 0))
    full = lambda *sh: pl.BlockSpec(sh, lambda i: (0,) * len(sh), pipeline_mode=pl.Buffered(1))
    anywhere = pl.BlockSpec(memory_space=pl.ANY)
    sd = jax.ShapeDtypeStruct
    shapes = [(n,) + o.shape for o in owns]
    kinds = 2 * (n - 1) + 1
    res = pl.pallas_call(
        functools.partial(forward_kernel, n, reps, width),
        grid=(nc + 1,),
        in_specs=[blk(width), blk(2), full(nc, 1, C), full(nr, C), full(*vec.shape), full(*high.shape), full(*low.shape)]
        + [anywhere] * 8,
        out_specs=[blk(w) for w in (width, 512, 512, 1024, 1024, 16, 1024, 1024)]
        + [pl.BlockSpec((1, HEADS, VH, KH), lambda i: (last(i), 0, 0, 0))]
        + [full(T, width), full(T, width), full(8, width), full(16, 512), full(width, 16)]
        + [anywhere] * 8,
        out_shape=[sd((T, w), BF) for w in (width, 512, 512, 1024, 1024, 16, 1024, 1024)]
        + [
            sd((nc, HEADS, VH, KH), BF),
            sd((T, width), F32),
            sd((T, width), BF),
            sd((8, width), F32),
            sd((16, 512), BF),
            sd((width, 16), BF),
        ]
        + [sd(shape, BF) for shape in shapes],
        scratch_shapes=[
            pltpu.VMEM((HEADS, VH, KH), F32),
            pltpu.VMEM((nr, 512), F32),
            pltpu.VMEM((T, width), BF),
            pltpu.VMEM((T, 1024), BF),
            pltpu.VMEM((n,) + vec.shape, F32),
            pltpu.VMEM((n,) + high.shape, BF),
            pltpu.VMEM((n,) + low.shape, BF),
        ]
        + [pltpu.VMEM(shape, BF) for shape in shapes[:5]]
        + [
            pltpu.SemaphoreType.DMA((3, n - 1)),
            pltpu.SemaphoreType.DMA((3, n - 1)),
            pltpu.SemaphoreType.DMA((8, kinds)),
            pltpu.SemaphoreType.DMA((8, kinds)),
            pltpu.SemaphoreType.DMA((5,)),
        ],
        compiler_params=pltpu.CompilerParams(collective_id=0, has_side_effects=True, vmem_limit_bytes=60 << 20),
        name="gla_fwd_gather",
    )(x, cols, segr, M, vec, high, low, *owns)
    return res[:14], [o.reshape(-1, o.shape[-1]) for o in res[14:]]


def backward_kernel(n,reps,plan,half,*refs):
    (q_ref,k_ref,v_ref,g_ref,r_ref,o_ref,st_ref,dy_ref,a_ref,x_ref,dx_ref,cols_ref,
     wh_ref,bias_ref,gain_ref,gmix_ref,nmlp_ref,segr_ref,m_ref,wq_ref,wk_ref,wv_ref,wg_ref,wl_ref)=refs[:24]
    parts=refs[24:26]
    gt_ref,small_ref=refs[26:28]
    outs=refs[28:34]
    dstate,rcar,esc,dcs,dall,at_ref,dz_ref,low_acc,high_acc,gb_ref,gg_ref,nmix_ref,smb,both=refs[34:48]
    rest=refs[48:]
    steps=pl.num_programs(0); step=pl.program_id(0); nc=steps-1
    p=Place(n,reps)
    items=[]
    for which,at,width,source in plan:
        count=7 if source is None else 6
        mem,rest=rest[:count],rest[count:]
        cols=pl.ds(at,width)
        out=[(lambda c,which=which,cols=cols: outs[which].at[c,:,cols],pl.ds(0,width))]
        if source is None:
            items.append(Reduce(p,out,mem[:4],mem[4:],part=parts[which].at[:,:,:,cols]))
        else:
            cols=pl.ds(source,width)
            items.append(Reduce(p,out,mem[:3],mem[3:],mine=both.at[0,:,:,cols],give=both.at[1,:,:,cols]))
    mem=rest
    small=Small(p,smb,small_ref,mem[:4],mem[4:])
    ready=[it for it in items if it.part is not None]
    fresh=[it for it in items if it.part is None]

    line=ready+[None]*(8-len(ready))+fresh

    def slot(t):
        for k in range(Reduce.STAGES):
            if 0<=t-k<len(line) and line[t-k] is not None: line[t-k].stage(k)

    @pl.when(step==0)
    def _():
        greet(Reduce.peers(p))
        for it in ready: it.start()
        for ref in (dstate,rcar,gb_ref,gg_ref,low_acc,high_acc,nmix_ref,smb): ref[...]=jnp.zeros_like(ref)

    @pl.when(step<nc)
    def _():
        i=nc-1-step
        rows=pl.ds(pl.multiple_of(i*C,C),C)
        bwd_chunk(i,q_ref,k_ref,v_ref,g_ref,r_ref,o_ref,st_ref,dy_ref,wh_ref,bias_ref,gain_ref,cols_ref,segr_ref,m_ref,
                  dall.at[rows,0:512],dall.at[rows,512:1024],dall.at[rows,1024:2048],dall.at[rows,2048:3072],dz_ref,gb_ref,gg_ref,dstate,rcar,esc,dcs)
        dz=dz_ref[...]; a=a_ref[...]
        dr=dot_nt(dz,wh_ref[...]).astype(BF)
        high_acc[...]+=dot_tn(r_ref[...],dz)
        low_acc[...]+=dot_tn(dr,a)
        at_ref[:,rows]=jnp.transpose(a)
        da=dot_nt(dall[rows,0:512],wq_ref[...])+dot_nt(dall[rows,512:1024],wk_ref[...])
        da=da+dot_nt(dall[rows,1024:2048],wv_ref[...])+dot_nt(dall[rows,2048:3072],wg_ref[...])+dot_nt(dr,wl_ref[...])
        x=x_ref[...].astype(F32)
        n1=lax.rsqrt(jnp.mean(x*x,axis=-1,keepdims=True)+1e-5)
        xn=x*n1
        nmix_ref[...]+=jnp.sum(da*xn,axis=0,keepdims=True)
        dm=da*gmix_ref[...]
        gt_ref[...]=dx_ref[...]+n1*(dm-xn*jnp.mean(dm*xn,axis=-1,keepdims=True))

    for t in range(8):
        @pl.when(step==t)
        def _(): slot(t)

    @pl.when(step==nc)
    def _():
        rs=2*half
        smb[:,16:32,:]=jnp.broadcast_to(high_acc[...][None],(n,16,512))
        smb[:,32:33,:]=jnp.broadcast_to(gb_ref[...][None],(n,1,512))
        smb[:,33:34,0:256]=jnp.broadcast_to(gg_ref[...][None],(n,1,256))
        for s in range(n):
            at=slice(s*rs,(s+1)*rs)
            smb[s,0:16,0:rs]=low_acc[:,at]
            smb[s,34:35,0:rs]=nmix_ref[:,at]
            smb[s,35:36,0:rs]=nmlp_ref[:,at]
        small.swap().start()

        def product(at,width):
            cols=slice(at,at+width)
            def one(s,_):
                rows=pl.ds(pl.multiple_of(s*rs,rs),rs)
                w=dot(at_ref[rows,:],dall[:,cols]).astype(BF)
                both[p.core,s,:,cols]=w[:half]
                both[1-p.core,s,:,cols]=w[half:]
                return 0
            lax.fori_loop(0,n,one,0)

        t=8; f=0
        for at,width,count in ((2048,1024,2),(1024,1024,2),(0,1024,2)):
            product(at,width)
            for it in fresh[f:f+count]: it.start()
            f+=count
            slot(t); t+=1
            small.stage((t-9))
        last=len(line)+Reduce.STAGES-1
        while t<last:
            slot(t); t+=1
        for it in items: it.settle()
        small.settle()

def backward(n,reps,q,k,v,g,r,o,st,dy,first,tokens,dx2,wh,bias,gain,gmix,nmlp,cols,segr,weights,partials):
    T=q.shape[0]; nc=T//C; z=reps//2
    assert nc==8
    M=jnp.asarray(level_sums(),BF); nr=M.shape[0]
    blk=lambda w: pl.BlockSpec((C,w),lambda i:(jnp.maximum(nc-1-i,0),0))
    full=lambda *sh: pl.BlockSpec(sh,lambda i:(0,)*len(sh),pipeline_mode=pl.Buffered(1))
    sd=jax.ShapeDtypeStruct
    anywhere=pl.BlockSpec(memory_space=pl.ANY)
    half=first.shape[1]//(2*n)
    pairs=[q.reshape(n,2,q.shape[0]//(2*n),q.shape[1]) for q in partials]
    plan,scratch=[],[]
    for which,(pair,cut) in enumerate(zip(pairs,(4,2))):
        tiles=pair.shape[3]//128
        edges=[128*(tiles*j//cut) for j in range(cut+1)]
        for at,end in zip(edges[:-1],edges[1:]):
            plan.append((which,at,end-at,None)); scratch+=Reduce.scratch(n,z,pair.shape[2],end-at,True)
    for which,at,width,source in ((5,0,512,2048),(5,512,512,2560),(4,0,512,1024),(4,512,512,1536),(2,0,512,0),(3,0,512,512)):
        plan.append((which,at,width,source)); scratch+=Reduce.scratch(n,z,half,width,False)
    scratch+=Small.scratch(n,z,40,512)
    out=lambda h,w: sd((2,h,w),BF)
    res=pl.pallas_call(functools.partial(backward_kernel,n,reps,tuple(plan),half),grid=(nc+1,),
        in_specs=[blk(512),blk(512),blk(1024),blk(1024),blk(16),blk(1024),pl.BlockSpec((1,HEADS,VH,KH),lambda i:(jnp.maximum(nc-1-i,0),0,0,0)),blk(1024),
                  blk(1024),blk(1024),blk(1024),blk(2),
                  full(16,512),full(1,512),full(1,256),full(1,1024),full(1,1024),full(nc,1,C),full(nr,C),
                  full(1024,512),full(1024,512),full(1024,1024),full(1024,1024),full(1024,16)]+[anywhere]*2,
        out_specs=[blk(1024),pl.BlockSpec((40,512),lambda i:(0,0))]+[anywhere]*6,
        out_shape=[sd((T,1024),F32),sd((40,512),F32)]+[out(q.shape[2],q.shape[3]) for q in pairs]+[out(half,512),out(half,512),out(half,1024),out(half,1024)],
        scratch_shapes=[pltpu.VMEM((HEADS,VH,KH),F32),pltpu.VMEM((1,512),F32),pltpu.VMEM((nr,512),F32),pltpu.VMEM((C,1024),BF),
                        pltpu.VMEM((T,3072),BF),pltpu.VMEM((1024,T),BF),pltpu.VMEM((C,512),BF),pltpu.VMEM((16,1024),F32),pltpu.VMEM((16,512),F32),
                        pltpu.VMEM((1,512),F32),pltpu.VMEM((1,256),F32),pltpu.VMEM((1,1024),F32),pltpu.VMEM((n,40,512),F32),
                        pltpu.VMEM((2,n,half,3072),BF)]+scratch,
        compiler_params=pltpu.CompilerParams(collective_id=2,has_side_effects=True,vmem_limit_bytes=63<<20),
        name="gla_bwd_reduce")(q,k,v,g,r,o,st,dy,first,tokens,dx2,cols,wh,bias,gain,gmix,nmlp,segr,M,*weights,*pairs)
    return res[0],res[1],[x.reshape(-1,x.shape[2]) for x in res[2:]]


def matmul(left, right):
    return jnp.dot(left, right, preferred_element_type=F32)


def local(
    shards,
    reps,
    tokens,
    segments,
    cotangent,
    norm_mix,
    w_query,
    w_key,
    w_value,
    w_outgate,
    w_low,
    w_high,
    decay_bias,
    head_gain,
    w_out,
    norm_mlp,
    w_gate,
    w_up,
    w_down,
):
    total = tokens.shape[0] * tokens.shape[1]
    width = tokens.shape[2]
    cols, segr = seg_views(segments)
    wide = max(norm_mix.shape[0], 128)
    rows = [jnp.pad(v.astype(F32), (0, wide - v.shape[0])) for v in (norm_mix, norm_mlp, decay_bias, head_gain)]
    vec = jnp.concatenate([jnp.stack(rows), jnp.zeros((4, wide), F32)])
    (
        (first, query, keys, values, outgate, lowrank, mixed, heads, states, resid, second, vecs, high_w, low_w),
        (query_w, key_w, value_w, outgate_w, out_w, gate_w, up_w, down_w),
    ) = forward(
        shards,
        reps,
        tokens.reshape(total, width),
        cols,
        segr,
        vec,
        w_high,
        w_low,
        (w_query, w_key, w_value, w_outgate, w_out, w_gate, w_up, w_down),
    )
    gain_mix, gain_feed, bias, gain_head = vecs[0:1], vecs[1:2], vecs[2:3, :512], vecs[3:4, :VH]
    grad_out = cotangent.reshape(total, width)
    result, grad_resid, branch, part_norm_mlp, part_down, sum_gate, sum_up = feed(
        shards, reps, second, grad_out, resid, gain_feed, gate_w, up_w, down_w
    )
    part_out = dot_tn(mixed, branch)
    grad_mixed = dot_nt(branch, out_w).astype(BF)
    grad_inputs, small_sums, sums = backward(
        shards,
        reps,
        query,
        keys,
        values,
        outgate,
        lowrank,
        heads,
        states,
        grad_mixed,
        first,
        tokens.reshape(total, width),
        grad_resid,
        high_w,
        bias,
        gain_head,
        gain_mix,
        part_norm_mlp,
        cols,
        segr,
        (query_w, key_w, value_w, outgate_w, low_w),
        (part_down, part_out.astype(BF)),
    )
    sum_gate, sum_up = [s.reshape(-1, s.shape[2]).astype(F32) for s in (sum_gate, sum_up)]
    sum_down, sum_out, sum_query, sum_key, sum_value, sum_outgate = [s.astype(F32) for s in sums]
    me = lax.axis_index("shard")
    rs = w_low.shape[0]

    def across(block, width):
        return lax.dynamic_slice_in_dim(block, me * width, width, axis=1)

    own = (
        small_sums[34, :rs],
        small_sums[35, :rs],
        across(small_sums[32:33], decay_bias.shape[0]).reshape(-1),
        across(small_sums[33:34, :VH], head_gain.shape[0]).reshape(-1),
        small_sums[:16, :rs].T,
        across(small_sums[16:32], w_high.shape[1]),
    )
    return (
        result.reshape(tokens.shape),
        grad_inputs.reshape(tokens.shape),
        own[0],
        sum_query,
        sum_key,
        sum_value,
        sum_outgate,
        own[4],
        own[5],
        own[2],
        own[3],
        sum_out,
        own[1],
        sum_gate,
        sum_up,
        sum_down,
    )


def solution(mesh):
    in_specs = (
        P(("rep", "shard"), None, None),
        P(("rep", "shard"), None),
        P(("rep", "shard"), None, None),
        P("shard"),
        P("shard", None),
        P("shard", None),
        P("shard", None),
        P("shard", None),
        P("shard", None),
        P(None, "shard"),
        P("shard"),
        P("shard"),
        P("shard", None),
        P("shard"),
        P("shard", None),
        P("shard", None),
        P("shard", None),
    )
    out_specs = (
        P(("rep", "shard"), None, None),
        P(("rep", "shard"), None, None),
        P("shard"),
        P("shard", None),
        P("shard", None),
        P("shard", None),
        P("shard", None),
        P("shard", None),
        P(None, "shard"),
        P("shard"),
        P("shard"),
        P("shard", None),
        P("shard"),
        P("shard", None),
        P("shard", None),
        P("shard", None),
    )
    return jax.shard_map(
        functools.partial(local, mesh.shape["shard"], mesh.shape["rep"]), mesh=mesh, in_specs=in_specs, out_specs=out_specs, check_vma=False)
```

```python
import functools
import numpy as np
import jax, jax.numpy as jnp
from jax import lax
from jax.experimental import pallas as pl
from jax.experimental.pallas import tpu as pltpu
from jax.sharding import PartitionSpec as P
HEADS=4; KH=128; VH=256; C=128
SCALE=KH**-0.5
LEVELS=(64,32,16,8,4,2,1)
F32=jnp.float32; BF=jnp.bfloat16

def level_sums():
    t=np.arange(C)[:,None]; u=np.arange(C)[None,:]
    rows=[]
    for h in LEVELS:
        ref=(t//(2*h))*(2*h)+h-1
        second=t>ref
        rows.append(np.where(second,(u>ref)&(u<=t),(u>t)&(u<=ref)))
    rows.append(u<=t); rows.append(u>t)
    return np.concatenate(rows,0).astype(np.float32)

def dot(a,b): return lax.dot_general(a,b,(((1,),(0,)),((),())),preferred_element_type=F32)
def dot_nt(a,b): return lax.dot_general(a,b,(((1,),(1,)),((),())),preferred_element_type=F32)
def dot_tn(a,b): return lax.dot_general(a,b,(((0,),(0,)),((),())),preferred_element_type=F32)

def gate_in(r_ref,wh_ref,bias_ref):
    return dot(r_ref[...],wh_ref[...])+bias_ref[...]

def log_rate(zb):
    return (jnp.minimum(zb,0.0)-jnp.log1p(jnp.exp(-jnp.abs(zb))))*(1.0/16.0)

def level_map(i,segr_ref):
    t=lax.broadcasted_iota(jnp.int32,(C,C),0); s=lax.broadcasted_iota(jnp.int32,(C,C),1)
    segr=segr_ref[i].astype(F32)
    prev=jnp.where(i==0,-1.0,segr_ref[jnp.maximum(i-1,0)][:,C-1:C].astype(F32))
    segc=jnp.sum(jnp.where(t==s,segr,0.0),axis=1,keepdims=True)
    before=jnp.sum(jnp.where(t==s+1,segr,0.0),axis=1,keepdims=True)
    first=lax.broadcasted_iota(jnp.int32,(C,1),0)==0
    start=jnp.where(first,prev,before)!=segc
    last=segr[:,C-1:C]
    lv=jnp.where(segc==segr,t^s,-1)
    return lv,t,s,(segc==prev).astype(F32),(segc==last).astype(F32),(prev==last).astype(F32),start

def fwd_chunk(i,q_ref,k_ref,v_ref,g_ref,r_ref,wh_ref,bias_ref,gain_ref,segr_ref,m_ref,y_ref,o_ref,st_ref,state,esc):
    f=log_rate(gate_in(r_ref,wh_ref,bias_ref)).astype(BF)
    esc[...]=jnp.exp(dot(m_ref[...],f))
    lv,t,s,keep,tail,stay,start=level_map(i,segr_ref)
    lv=jnp.where(t>=s,lv,-1)
    row=lax.broadcasted_iota(jnp.int32,(C,KH),0)
    nl=len(LEVELS)
    for h in range(HEADS):
        ks=slice(h*KH,(h+1)*KH); vs=slice(h*VH,(h+1)*VH)
        q=q_ref[:,ks].astype(F32)*SCALE; k=k_ref[:,ks].astype(F32); v=v_ref[:,vs]
        a=jnp.where(lv==0,dot_nt(q.astype(BF),k_ref[:,ks]),0.0)
        for l,hs in enumerate(LEVELS):
            x=(jnp.where((row&hs)!=0,q,k)*esc[l*C:(l+1)*C,ks]).astype(BF)
            a=jnp.where((lv>=hs)&(lv<2*hs),dot_nt(x,x),a)
        ec=esc[nl*C:(nl+1)*C,ks]; es=esc[(nl+1)*C:(nl+2)*C,ks]
        st=state[h]
        stb=st.astype(BF)
        st_ref[0,h]=stb
        o=dot(a.astype(BF),v)+dot_nt((q*ec*keep).astype(BF),stb)
        state[h]=st*(ec[C-1:C,:]*stay)+dot_tn(v,(k*es*tail).astype(BF))
        o_ref[:,vs]=o.astype(BF)
        m=lax.rsqrt(jnp.mean(o*o,axis=-1,keepdims=True)+1.0)
        g=g_ref[:,vs].astype(F32)
        y_ref[:,vs]=(o*m*gain_ref[...]*(g*jax.nn.sigmoid(g))).astype(BF)

def bwd_chunk(i,q_ref,k_ref,v_ref,g_ref,r_ref,o_ref,st_ref,dy_ref,wh_ref,bias_ref,gain_ref,segr_ref,m_ref,
             dq_ref,dk_ref,dv_ref,dg_ref,dz_ref,gb_ref,gg_ref,dstate,rcar,esc,dcs):
    zb=gate_in(r_ref,wh_ref,bias_ref)
    f=log_rate(zb).astype(BF)
    esc[...]=jnp.exp(dot(m_ref[...],f))
    lv,t,s,keep,tail,stay,start=level_map(i,segr_ref)
    lvu=jnp.where(t<=s,lv,-1)
    lower=t>=s
    row=lax.broadcasted_iota(jnp.int32,(C,KH),0)
    nl=len(LEVELS)
    gain=gain_ref[...]
    ggacc=jnp.zeros((1,VH),F32)
    for h in range(HEADS):
        ks=slice(h*KH,(h+1)*KH); vs=slice(h*VH,(h+1)*VH)
        o=o_ref[:,vs].astype(F32); g=g_ref[:,vs].astype(F32); dy=dy_ref[:,vs].astype(F32)
        m=lax.rsqrt(jnp.mean(o*o,axis=-1,keepdims=True)+1.0)
        sg=jax.nn.sigmoid(g); om=o*m
        u=dy*(g*sg)
        dg_ref[:,vs]=(dy*om*gain*(sg*(1.0+g*(1.0-sg)))).astype(BF)
        ggacc=ggacc+jnp.sum(u*om,axis=0,keepdims=True)
        ug=u*gain
        do=(m*ug-om*(m*m)*jnp.mean(ug*o,axis=-1,keepdims=True)).astype(BF)
        q=q_ref[:,ks].astype(F32)*SCALE; k=k_ref[:,ks].astype(F32); v=v_ref[:,vs]
        qb=q.astype(BF); kb=k_ref[:,ks]
        das=jnp.where(lower,dot_nt(do,v),dot_nt(v,do))
        dd=jnp.sum(jnp.where(t==s,das,0.0),axis=1,keepdims=True)
        at=jnp.where(lvu==0,dot_nt(kb,qb),0.0)
        ec=esc[nl*C:(nl+1)*C,ks]; es=esc[(nl+1)*C:(nl+2)*C,ks]
        stb=st_ref[0,h]
        ds=dstate[h]; dsb=ds.astype(BF)
        qe=(q*ec*keep).astype(BF); ke=(k*es*tail).astype(BF)
        dq=dd*k+dot(do,stb)*(ec*keep)
        dk=dd*q+dot(v,dsb)*(es*tail)
        for l,hs in enumerate(LEVELS):
            e=esc[l*C:(l+1)*C,ks]
            sec=(row&hs)!=0
            x=(jnp.where(sec,q,k)*e).astype(BF)
            sx=dot_nt(x,x)
            at=jnp.where((lvu>=hs)&(lvu<2*hs),sx,at)
            gl=jnp.where((lv>=hs)&(lv<2*hs),das,0.0).astype(BF)
            tt=dot(gl,x)*e
            dq=dq+jnp.where(sec,tt,0.0)
            dk=dk+jnp.where(sec,0.0,tt)
        dv_ref[:,vs]=(dot(at.astype(BF),do)+dot_nt(ke,dsb)).astype(BF)
        dq_ref[:,ks]=(dq*SCALE).astype(BF)
        dk_ref[:,ks]=dk.astype(BF)
        dsn=ds*(ec[C-1:C,:]*stay)+dot_tn(do,qe)
        dstate[h]=dsn
        dc=q*dq-k*dk
        hi=dc.astype(BF)
        dcs[:,ks]=hi; dcs[:,HEADS*KH+h*KH:HEADS*KH+(h+1)*KH]=(dc-hi.astype(F32)).astype(BF)
        rold=rcar[:,ks]
        rcar[:,ks]=jnp.sum(stb.astype(F32)*dsn,axis=0,keepdims=True)
        dcs2=rold
        um=jnp.where((lv>=0)&(t<=s),1.0,0.0).astype(BF)
        df=dot(um,dcs[:,ks])+dot(um,dcs[:,HEADS*KH+h*KH:HEADS*KH+(h+1)*KH])+tail*dcs2
        dp=jnp.where(start,0.0,df)*(jax.nn.sigmoid(-zb[:,ks])*(1.0/16.0))
        dz_ref[:,ks]=dp.astype(BF)
        gb_ref[:,ks]+=jnp.sum(dp,axis=0,keepdims=True)
    gg_ref[...]+=ggacc

def seg_rows(segments):
    b,l=segments.shape
    seg=segments if b==1 else segments+8*lax.broadcasted_iota(jnp.int32,(b,l),0)
    return seg.reshape(-1,1,C)


MESH = pl.DeviceIdType.MESH
TILE = 256
EARLY = 3


class Place:
    def __init__(self, n, reps):
        self.n, self.z = n, reps // 2
        self.rep = lax.axis_index("rep")
        self.me = lax.axis_index("shard")
        self.core = lax.rem(self.rep, 2)
        self.chip = self.rep // 2
        self.sib = (self.rep + 1 - 2 * self.core, self.me)

    def peer(self, step):
        return lax.rem(self.me + step, self.n)

    def flip(self, bit):
        if bit == 1:
            return self.me + 1 - 2 * lax.rem(self.me, 2)
        return lax.rem(self.me + 2, 4)

    def first(self):
        return jnp.where(self.core == 0, self.flip(1), self.flip(2))

    def second(self):
        return jnp.where(self.core == 0, self.flip(2), self.flip(1))


def greet(ids):
    barrier = pltpu.get_barrier_semaphore()
    for d in ids:
        pl.semaphore_signal(barrier, inc=1, device_id=d, device_id_type=MESH)
    pl.semaphore_wait(barrier, len(ids))


def remote(src, dst, ssem, rsem, device):
    return pltpu.make_async_remote_copy(
        src_ref=src, dst_ref=dst, send_sem=ssem, recv_sem=rsem, device_id=device, device_id_type=MESH
    )


def gather_sems(n, count):
    kinds = 2 * (n - 1) + 1
    return [pltpu.SemaphoreType.DMA((count, kinds)), pltpu.SemaphoreType.DMA((count, kinds))]


class Gather:
    def __init__(self, place, owns, fulls, sems):
        self.p, self.owns, self.fulls = place, owns, fulls
        self.ssem, self.rsem = sems

    def peers(self):
        p = self.p
        return [(p.rep, p.peer(j)) for j in range(1, p.n)] + [p.sib]

    def same(self, i):
        kind = 2 * (self.p.n - 1)
        return remote(
            self.owns[i], self.fulls[i].at[self.p.me], self.ssem[i].at[kind], self.rsem[i].at[kind], self.p.sib
        )

    def direct(self, i, kind, target):
        p = self.p
        return remote(
            self.owns[i].at[p.core],
            self.fulls[i].at[p.me, p.core],
            self.ssem[i].at[kind],
            self.rsem[i].at[kind],
            (p.rep, target),
        )

    def onward(self, i, kind, block, device):
        p = self.p
        view = self.fulls[i].at[block, p.core]
        return remote(view, view, self.ssem[i].at[kind], self.rsem[i].at[kind], device)

    def start(self, i):
        p = self.p
        if p.n == 4:
            self.direct(i, 0, p.first()).start()
            self.direct(i, 1, p.second()).start()
        else:
            for j in range(1, p.n):
                self.direct(i, j - 1, p.peer(j)).start()
        self.same(i).start()

    def blocks(self):
        p = self.p
        if p.n == 4:
            return [p.first(), p.second(), 3 - p.me]
        return [p.peer(p.n - j) for j in range(1, p.n)]

    def relay(self, i):
        p, blocks, last = self.p, self.blocks(), self.p.n - 1
        if p.n == 4:
            self.direct(i, 1, blocks[1]).wait_recv()
            self.onward(i, 2, blocks[1], (p.rep, blocks[0])).start()
            self.onward(i, last + 1, blocks[1], p.sib).start()
            self.direct(i, 0, blocks[0]).wait_recv()
            self.onward(i, last, blocks[0], p.sib).start()
        else:
            for j in range(last):
                self.direct(i, j, p.me).wait_recv()
                self.onward(i, last + j, blocks[j], p.sib).start()

    def pass_on(self, i):
        p, blocks, last = self.p, self.blocks(), self.p.n - 1
        if p.n == 4:
            self.onward(i, 2, blocks[2], (p.rep, blocks[0])).wait_recv()
            self.onward(i, last + 2, blocks[2], p.sib).start()

    def done(self, i):
        p, blocks, last = self.p, self.blocks(), self.p.n - 1
        self.same(i).wait()
        for j in range(last):
            self.direct(i, j, p.me).wait_send()
            arrival = self.onward(i, last + j, blocks[j], p.sib)
            arrival.wait_send()
            arrival.wait_recv()


def halves(w):
    return w.reshape(2, w.shape[0] // 2, w.shape[1])


def add_rows(dst, a, b):
    rows = dst.shape[0]
    slab = 32 if rows % 32 == 0 else 16

    def step(j, _):
        at = pl.ds(pl.multiple_of(j * slab, slab), slab)
        dst[at, :] = a[at, :] + b[at, :]
        return 0

    lax.fori_loop(0, rows // slab, step, 0)


class Reduce:
    STAGES = 7

    def __init__(self, place, out, bufs, sems, mine=None, give=None, part=None):
        self.p, self.out = place, out
        self.part = part
        self.square = place.n == 4
        self.line = place.z == 4
        bufs = list(bufs)
        if part is not None:
            mine, give = bufs.pop(0), part.at[:, 1 - place.core]
        self.mine, self.give = mine, give
        self.other, self.group, self.ring = bufs
        self.own = mine.at[place.me]
        self.rest = mine.at[place.second()] if self.square else None
        self.ssem, self.rsem, self.lsem = sems
        self.zbase = place.n
        self.end = self.zbase + (3 if self.line else place.z - 1)
        self.total = self.ring.at[2] if self.line else self.group.at[0]

    def copy(self, kind, src, dst, device):
        return remote(src, dst, self.ssem.at[kind], self.rsem.at[kind], device)

    def load(self):
        return pltpu.make_async_copy(self.part.at[:, self.p.core], self.mine, self.lsem.at[0])

    def swap(self):
        return self.copy(0, self.give, self.other, self.p.sib)

    def start(self):
        self.swap().start()
        if self.part is not None:
            self.load().start()

    def group_sends(self):
        p = self.p
        if self.square:
            to = (p.rep, p.first())
            return [
                self.copy(1, self.mine.at[p.first()], self.group.at[0], to),
                self.copy(2, self.mine.at[3 - p.me], self.group.at[1], to),
            ]
        return [
            self.copy(j, self.mine.at[p.peer(j)], self.group.at[j - 1], (p.rep, p.peer(j))) for j in range(1, p.n)
        ]

    def second_send(self):
        p = self.p
        return self.copy(3, self.rest, self.group.at[2], (p.rep, p.second()))

    def line_send(self, step):
        p = self.p
        if step == 0:
            to = jnp.where(p.chip == 0, p.rep + 2, p.rep - 2)
            return self.copy(self.zbase, self.own, self.ring.at[0], (to, p.me))
        if step == 1:
            to = jnp.where(p.chip == 1, p.rep + 2, p.rep - 2)
            return self.copy(self.zbase + 1, self.own, self.ring.at[1], (to, p.me))
        to = jnp.where(p.chip == 1, p.rep - 2, p.rep + 2)
        return self.copy(self.zbase + 2, self.total, self.total, (to, p.me))

    def ring_sends(self):
        p = self.p
        return [
            self.copy(self.zbase + j - 1, self.own, self.ring.at[p.chip], (lax.rem(p.rep + 2 * j, 2 * p.z), p.me))
            for j in range(1, p.z)
        ]

    def last_swaps(self):
        return [
            self.copy(self.end + j, self.total.at[:, lanes], half(self.p.core), self.p.sib)
            for j, (half, lanes) in enumerate(self.out)
        ]

    def stores(self):
        return [
            pltpu.make_async_copy(self.total.at[:, lanes], half(self.p.core), self.lsem.at[2 + j])
            for j, (half, lanes) in enumerate(self.out)
        ]

    def stage(self, k):
        p = self.p
        outer = (p.chip == 0) | (p.chip == 3)
        if k == 0:
            if self.part is not None:
                self.load().wait()
            self.swap().wait_recv()
            for b in range(p.n):
                add_rows(self.mine.at[b], self.mine.at[b], self.other.at[b])
            for c in self.group_sends():
                c.start()
        elif k == 1:
            for c in self.group_sends():
                c.wait_recv()
            add_rows(self.own, self.own, self.group.at[0])
            if self.square:
                add_rows(self.rest, self.rest, self.group.at[1])
                self.second_send().start()
            else:
                for j in range(1, p.n - 1):
                    add_rows(self.own, self.own, self.group.at[j])
        elif k == 2:
            if self.square:
                self.second_send().wait_recv()
                add_rows(self.own, self.own, self.group.at[2])
            if self.line:

                @pl.when(outer)
                def _():
                    self.line_send(0).start()

            else:
                for c in self.ring_sends():
                    c.start()
        elif k == 3:
            if self.line:

                @pl.when(jnp.logical_not(outer))
                def _():
                    self.line_send(0).wait_recv()
                    add_rows(self.own, self.own, self.ring.at[0])
                    self.line_send(1).start()

            else:
                for c in self.ring_sends():
                    c.wait_recv()
                self.ring[p.chip] = self.own[...]
                add_rows(self.total, self.ring.at[0], self.ring.at[1])
                for j in range(2, p.z):
                    add_rows(self.total, self.total, self.ring.at[j])
        elif k == 4:
            if self.line:

                @pl.when(jnp.logical_not(outer))
                def _():
                    self.line_send(1).wait_recv()
                    add_rows(self.total, self.own, self.ring.at[1])
                    self.line_send(2).start()

        elif k == 5:
            if self.line:

                @pl.when(outer)
                def _():
                    self.line_send(2).wait_recv()

            for c in self.last_swaps() + self.stores():
                c.start()
        else:
            for c in self.last_swaps():
                c.wait_recv()
            for c in self.stores():
                c.wait()

    def settle(self):
        p = self.p
        outer = (p.chip == 0) | (p.chip == 3)
        self.swap().wait_send()
        for c in self.group_sends():
            c.wait_send()
        if self.square:
            self.second_send().wait_send()
        if self.line:

            @pl.when(outer)
            def _():
                self.line_send(0).wait_send()

            @pl.when(jnp.logical_not(outer))
            def _():
                self.line_send(1).wait_send()
                self.line_send(2).wait_send()

        else:
            for c in self.ring_sends():
                c.wait_send()
        for c in self.last_swaps():
            c.wait_send()

    @staticmethod
    def peers(p):
        group = [(p.rep, p.peer(j)) for j in range(1, p.n)]
        along = [(lax.rem(p.rep + 2 * j, 2 * p.z), p.me) for j in range(1, p.z)]
        return group + along + [p.sib]

    @staticmethod
    def kinds(n, z):
        return n + (3 if z == 4 else z - 1) + 2

    @staticmethod
    def scratch(n, z, half, width, loaded, lead=()):
        lead = tuple(lead)
        kinds = Reduce.kinds(n, z)
        return ([pltpu.VMEM(lead + (n, half, width), BF)] if loaded else []) + [
            pltpu.VMEM(lead + (n, half, width), BF),
            pltpu.VMEM(lead + (n - 1, half, width), BF),
            pltpu.VMEM(lead + (3 if z == 4 else z, half, width), BF),
            pltpu.SemaphoreType.DMA(lead + (kinds,)),
            pltpu.SemaphoreType.DMA(lead + (kinds,)),
            pltpu.SemaphoreType.DMA(lead + (4,)),
        ]


class Small:
    def __init__(self, place, part, out, bufs, sems):
        self.p, self.part, self.out = place, part, out
        self.pair, self.other, self.group, self.ring = bufs
        self.ssem, self.rsem = sems

    def copy(self, kind, src, dst, device):
        return remote(src, dst, self.ssem.at[kind], self.rsem.at[kind], device)

    def swap(self):
        return self.copy(0, self.part, self.other, self.p.sib)

    def sends(self):
        p = self.p
        return [
            self.copy(j, self.pair.at[p.peer(j)], self.group.at[j - 1], (p.rep, p.peer(j))) for j in range(1, p.n)
        ]

    def along(self):
        p = self.p
        return [
            self.copy(p.n + j - 1, self.pair.at[p.me], self.ring.at[p.chip], (lax.rem(p.rep + 2 * j, 2 * p.z), p.me))
            for j in range(1, p.z)
        ]

    def stage(self, k):
        p = self.p
        if k == 0:
            self.swap().wait_recv()
            self.pair[...] = self.part[...] + self.other[...]
            for c in self.sends():
                c.start()
        elif k == 1:
            for c in self.sends():
                c.wait_recv()
            own = self.pair[p.me]
            for j in range(p.n - 1):
                own = own + self.group[j]
            self.pair[p.me] = own
            self.ring[p.chip] = own
            for c in self.along():
                c.start()
        else:
            for c in self.along():
                c.wait_recv()
            own = self.ring[0]
            for j in range(1, p.z):
                own = own + self.ring[j]
            self.out[...] = own

    def settle(self):
        self.swap().wait_send()
        for c in self.sends() + self.along():
            c.wait_send()

    @staticmethod
    def scratch(n, z, rows, width):
        return [
            pltpu.VMEM((n, rows, width), F32),
            pltpu.VMEM((n, rows, width), F32),
            pltpu.VMEM((n - 1, rows, width), F32),
            pltpu.VMEM((z, rows, width), F32),
            pltpu.SemaphoreType.DMA((n + z - 1,)),
            pltpu.SemaphoreType.DMA((n + z - 1,)),
        ]


def feed_kernel(n, reps, half, tile, *refs):
    b_ref, e_ref, x_ref, gain_ref, wd_ref = refs[:5]
    first, owns = refs[5:7], refs[7:9]
    res_out, dx_out, dm_out, norm_ref, down_out, gate_out, up_out, *late = refs[9:18]
    bt, acc, hid, dgate, dup, both, other, group, ring, ssem, rsem, lsem = refs[18:30]
    xs, res_ref, dx_ref, dm_ref, down_ref, moved, gsend, grecv, wbuf, wsem = refs[30:]
    step, tiles = pl.program_id(0), pl.num_programs(0) - 1
    p = Place(n, reps)
    total = b_ref.shape[0]
    rs = 2 * half
    rows_at = lambda j, size: pl.ds(pl.multiple_of(j * size, size), size)

    def fetch():
        return pltpu.make_async_copy(x_ref, xs, moved.at[0])

    def write(k, ref, out, rows):
        return pltpu.make_async_copy(ref.at[rows], out.at[rows], moved.at[k])

    def tile_gather(j):
        at = pl.ds(pl.multiple_of(j * tile, tile), tile)
        to = pl.ds(pl.multiple_of((j - EARLY) * tile, tile), tile)
        return Gather(
            p,
            [own.at[:, :, at] for own in owns],
            [full.at[:, :, :, to] for full in late],
            [[sem.at[j - EARLY, i] for i in range(2)] for sem in (gsend, grecv)],
        )

    def weights(j, begin):
        buf = lax.rem(j, 2)

        def one(source, at):
            for i in range(2):
                c = pltpu.make_async_copy(
                    source[i].at[:, :, :, pl.ds(pl.multiple_of(at * tile, tile), tile)], wbuf.at[buf, i], wsem.at[buf, i]
                )
                c.start() if begin else c.wait()

        @pl.when(j < EARLY)
        def _():
            one(first, j)

        @pl.when(j >= EARLY)
        def _():
            one(late, j - EARLY)

    def ahead(lead, run):
        @pl.when((step + lead >= EARLY) & (step + lead < tiles))
        def _():
            for i in range(2):
                run(tile_gather(step + lead), i)

    def item(j):
        cols = pl.ds(pl.multiple_of(j * tile, tile), tile)
        out = [
            (lambda c: gate_out.at[c, :, cols], pl.ds(0, tile)),
            (lambda c: up_out.at[c, :, cols], pl.ds(tile, tile)),
        ]
        return Reduce(
            p,
            out,
            [other.at[j], group.at[j], ring.at[j]],
            [ssem.at[j], rsem.at[j], lsem.at[j]],
            mine=both.at[j, 0],
            give=both.at[j, 1],
        )

    def slot(t):
        for k in range(Reduce.STAGES):

            @pl.when((t >= k) & (t - k < tiles))
            def _():
                item(t - k).stage(k)

    @pl.when(step == 0)
    def _():
        greet(Reduce.peers(p))
        fetch().start()
        weights(0, True)
        for j in range(EARLY, min(EARLY + 1, tiles)):
            for i in range(2):
                tile_gather(j).start(i)
        acc[...] = jnp.zeros_like(acc)
        dx_ref[...] = jnp.zeros_like(dx_ref)

        def turn(j, _):
            rows = rows_at(j, 128)
            bt[:, rows] = jnp.transpose(b_ref[rows, :])
            return 0

        lax.fori_loop(0, total // 128, turn, 0)

    @pl.when(step < tiles)
    def _():
        ahead(EARLY + 1, lambda g, i: g.start(i))
        weights(step, False)
        wg = wbuf[lax.rem(step, 2), 0].reshape(-1, tile)
        wu = wbuf[lax.rem(step, 2), 1].reshape(-1, tile)

        def rows_step(j, _):
            rows = rows_at(j, 512)
            b, e = b_ref[rows, :], e_ref[rows, :]
            gate = dot(b, wg)
            up = dot(b, wu)
            dh = dot_nt(e, wd_ref[...])
            sig = jax.nn.sigmoid(gate)
            swish = gate * sig
            h = (swish * up).astype(BF)
            dg = (dh * up * (sig * (1.0 + gate * (1.0 - sig)))).astype(BF)
            du = (dh * swish).astype(BF)
            down_ref[rows_at(step, tile), rows] = jnp.transpose(h)
            hid[rows, :] = h
            dgate[rows, :] = dg
            dup[rows, :] = du
            return 0

        def sums_step(j, _):
            rows = rows_at(j, 512)
            acc[rows, :] += dot(hid[rows, :], wd_ref[...])
            dx_ref[rows, :] += dot_nt(dgate[rows, :], wg) + dot_nt(dup[rows, :], wu)
            return 0

        lax.fori_loop(0, total // 512, rows_step, 0)

        ahead(EARLY, lambda g, i: g.relay(i))
        ahead(EARLY - 1, lambda g, i: g.pass_on(i))
        ahead(1, lambda g, i: g.done(i))

        @pl.when(step + 1 < tiles)
        def _():
            weights(step + 1, True)

        @pl.when(step > 0)
        def _():
            slot(step - 1)

        for at, d in ((0, dgate), (tile, dup)):
            w = dot(bt[...], d[...]).astype(BF)
            for s in range(n):
                both[step, p.core, s, :, at : at + tile] = w[s * rs : s * rs + half]
                both[step, 1 - p.core, s, :, at : at + tile] = w[s * rs + half : (s + 1) * rs]
        item(step).start()
        lax.fori_loop(0, total // 512, sums_step, 0)

    @pl.when(step == tiles)
    def _():
        norm_ref[...] = jnp.zeros_like(norm_ref)

        def finish(j, _):
            rows = rows_at(j, 128)
            x = xs[rows, :]
            res_ref[rows, :] = (x + acc[rows, :]).astype(BF)
            inv = lax.rsqrt(jnp.mean(x * x, axis=-1, keepdims=True) + 1e-5)
            xn = x * inv
            db = dx_ref[rows, :]
            norm_ref[...] += jnp.sum(db * xn, axis=0, keepdims=True)
            dbg = db * gain_ref[1:2, :]
            dx = e_ref[rows, :].astype(F32) + inv * (dbg - xn * jnp.mean(dbg * xn, axis=-1, keepdims=True))
            dx_ref[rows, :] = dx
            dm_ref[rows, :] = dx.astype(BF)
            return 0

        fetch().wait()

        def turn_down(j, _):
            slot(tiles - 1 + j)
            rows = rows_at(j, down_ref.shape[0] // 4)
            down_ref[rows, :] = dot(down_ref[rows, :], e_ref[...]).astype(BF)
            write(1 + j, down_ref, down_out, rows).start()
            return 0

        lax.fori_loop(0, 4, turn_down, 0)
        slot(tiles + 3)
        lax.fori_loop(0, total // 128, finish, 0)
        every = pl.ds(0, total)
        results = [
            write(5, res_ref, res_out, every),
            write(6, dx_ref, dx_out, every),
            write(7, dm_ref, dm_out, every),
        ]
        for c in results:
            c.start()

        def tail(t, _):
            slot(t)
            return 0

        lax.fori_loop(tiles + 4, tiles + Reduce.STAGES - 1, tail, 0)

        def settle(j, _):
            item(j).settle()
            return 0

        lax.fori_loop(0, tiles, settle, 0)
        for j in range(4):
            write(1 + j, down_ref, down_out, rows_at(j, down_ref.shape[0] // 4)).wait()
        for c in results:
            c.wait()


def feed(n, reps, b, e, x2, gain, wd, first, owns):
    total, width = b.shape
    owns = [halves(w) for w in owns]
    ff = wd.shape[0]
    tile, z = TILE, reps // 2
    tiles, half = ff // tile, width // (2 * n)
    once = lambda *sh: pl.BlockSpec(sh, lambda j: (0,) * len(sh), pipeline_mode=pl.Buffered(1))
    row = lambda: pl.BlockSpec((tile, width), lambda j: (jnp.minimum(j, tiles - 1), 0))
    anywhere = pl.BlockSpec(memory_space=pl.ANY)
    sd = jax.ShapeDtypeStruct
    return pl.pallas_call(
        functools.partial(feed_kernel, n, reps, half, tile),
        grid=(tiles + 1,),
        in_specs=[once(total, width)] * 2 + [anywhere, once(8, width), row()] + [anywhere] * 4,
        out_specs=[anywhere] * 3 + [once(1, width)] + [anywhere] * 5,
        out_shape=[
            sd((total, width), BF),
            sd((total, width), F32),
            sd((total, width), BF),
            sd((1, width), F32),
            sd((ff, total), BF),
            sd((2, half, ff), BF),
            sd((2, half, ff), BF),
            sd((n, 2, half, ff - EARLY * tile), BF),
            sd((n, 2, half, ff - EARLY * tile), BF),
        ],
        scratch_shapes=[
            pltpu.VMEM((width, total), BF),
            pltpu.VMEM((total, width), F32),
            pltpu.VMEM((total, tile), BF),
            pltpu.VMEM((total, tile), BF),
            pltpu.VMEM((total, tile), BF),
            pltpu.VMEM((tiles, 2, n, half, 2 * tile), BF),
        ]
        + Reduce.scratch(n, z, half, 2 * tile, False, (tiles,))
        + [
            pltpu.VMEM((total, width), F32),
            pltpu.VMEM((total, width), BF),
            pltpu.VMEM((total, width), F32),
            pltpu.VMEM((total, width), BF),
            pltpu.VMEM((ff, total), BF),
            pltpu.SemaphoreType.DMA((8,)),
            pltpu.SemaphoreType.DMA((tiles - EARLY, 2, 2 * (n - 1) + 1)),
            pltpu.SemaphoreType.DMA((tiles - EARLY, 2, 2 * (n - 1) + 1)),
            pltpu.VMEM((2, 2, n, 2, half, tile), BF),
            pltpu.SemaphoreType.DMA((2, 2)),
        ],
        compiler_params=pltpu.CompilerParams(collective_id=1, has_side_effects=True, vmem_limit_bytes=63 << 20),
        name="feed_forward",
    )(b, e, x2, gain, wd, *first, *owns)[:7]


def forward_kernel(n, reps, width, *refs):
    x_ref, segr_ref, m_ref, vec_ref, high_ref, low_ref = refs[:6]
    owns = refs[6:14]
    a_ref, q_ref, k_ref, v_ref, g_ref, r_ref, y_ref, o_ref, st_ref = refs[14:23]
    x2_ref, b_ref, vec_out, high_out, low_out = refs[23:28]
    outs = refs[28:36]
    state, esc, xs, ys, vecs, highs, lows = refs[36:43]
    kept = refs[43:48]
    small_send, small_recv, ssem, rsem, lsem = refs[48:]
    step, nc = pl.program_id(0), pl.num_programs(0) - 1
    p = Place(n, reps)
    early = outs[6].shape[3]
    owns = list(owns[:6]) + [own.at[:, :, 0:early] for own in owns[6:]]
    gather = Gather(
        p, owns, list(kept) + list(outs[5:]), [[sem.at[i] for i in range(8)] for sem in (ssem, rsem)]
    )
    smalls = [(vec_ref, vecs), (high_ref, highs), (low_ref, lows)]

    def small(k, j):
        src, dst = smalls[k]
        return remote(src, dst.at[p.me], small_send.at[k, j - 1], small_recv.at[k, j - 1], (p.rep, p.peer(j)))

    def keep(i):
        return pltpu.make_async_copy(kept[i], outs[i], lsem.at[i])

    def whole(i):
        w = kept[i][...]
        return w.reshape(-1, w.shape[-1])

    @pl.when(step == 0)
    def _():
        greet(gather.peers())
        for i in range(4):
            gather.start(i)
        for k in range(3):
            for j in range(1, n):
                small(k, j).start()
            src, dst = smalls[k]
            dst[p.me] = src[...]
        for i in range(4):
            gather.relay(i)
        for i in range(4, 8):
            gather.start(i)
        for k in range(3):
            for j in range(1, n):
                small(k, j).wait()
        rs = low_ref.shape[1]
        for s in range(n):
            at = slice(s * rs, (s + 1) * rs)
            vec_out[0:1, at] = vecs[s, :, 0:rs]
            vec_out[1:2, at] = vecs[s, :, rs : 2 * rs]
            low_out[:, at] = lows[s]

        def spread(part, out_width):
            own = part(0).shape[1]
            total = None
            for s in range(n):
                col = lax.broadcasted_iota(jnp.int32, (own, out_width), 1)
                row = lax.broadcasted_iota(jnp.int32, (own, out_width), 0)
                piece = dot(part(s), (col == row + s * own).astype(F32).astype(BF))
                total = piece if total is None else total + piece
            return total

        nb, ng = 512 // n, VH // n
        vec_out[2:3, 0:512] = spread(lambda s: vecs[s, :, 2 * rs : 2 * rs + nb].astype(BF), 512)
        vec_out[3:4, 0:VH] = spread(lambda s: vecs[s, :, -128:][:, 0:ng].astype(BF), VH)
        high_out[...] = spread(lambda s: highs[s], 512).astype(BF)
        for i in range(4):
            gather.pass_on(i)
        for i in range(4):
            gather.done(i)
            keep(i).start()
        state[...] = jnp.zeros_like(state)

    @pl.when(step < nc)
    def _():
        rows = pl.ds(pl.multiple_of(step * C, C), C)
        xb = x_ref[...]
        xs[rows, :] = xb
        x = xb.astype(F32)
        inv = lax.rsqrt(jnp.mean(x * x, axis=-1, keepdims=True) + 1e-5)
        a = (x * inv * vec_out[0:1, :]).astype(BF)
        a_ref[...] = a
        q_ref[...] = dot(a, whole(0)).astype(BF)
        k_ref[...] = dot(a, whole(1)).astype(BF)
        v_ref[...] = dot(a, whole(2)).astype(BF)
        g_ref[...] = dot(a, whole(3)).astype(BF)
        r_ref[...] = dot_nt(a, low_out[...]).astype(BF)
        fwd_chunk(
            step, q_ref, k_ref, v_ref, g_ref, r_ref, high_out, vec_out.at[2:3, 0:512], vec_out.at[3:4, 0:VH],
            segr_ref, m_ref, y_ref, o_ref, st_ref, state, esc,
        )
        ys[rows, :] = y_ref[...]

    @pl.when(step == 2)
    def _():
        gather.relay(4)

    @pl.when(step == 4)
    def _():
        gather.pass_on(4)

    @pl.when(step == nc)
    def _():
        gather.relay(5)
        gather.done(4)
        keep(4).start()

        def join(j, _):
            rows = pl.ds(pl.multiple_of(j * 256, 256), 256)
            x2 = xs[rows, :].astype(F32) + dot(ys[rows, :], whole(4))
            x2_ref[rows, :] = x2
            inv = lax.rsqrt(jnp.mean(x2 * x2, axis=-1, keepdims=True) + 1e-5)
            b_ref[rows, :] = (x2 * inv * vec_out[1:2, :]).astype(BF)
            return 0

        lax.fori_loop(0, xs.shape[0] // 256, join, 0)
        gather.pass_on(5)
        gather.relay(6)
        gather.pass_on(6)
        gather.relay(7)
        gather.pass_on(7)
        for i in range(5, 8):
            gather.done(i)
        for i in range(5):
            keep(i).wait()


def forward(n, reps, x, segr, vec, high, low, weights):
    T, width = x.shape
    nc = T // C
    M = jnp.asarray(level_sums(), BF)
    nr = M.shape[0]
    owns = [halves(w) for w in weights]
    last = lambda i: jnp.minimum(i, nc - 1)
    blk = lambda w: pl.BlockSpec((C, w), lambda i: (last(i), 0))
    full = lambda *sh: pl.BlockSpec(sh, lambda i: (0,) * len(sh), pipeline_mode=pl.Buffered(1))
    anywhere = pl.BlockSpec(memory_space=pl.ANY)
    sd = jax.ShapeDtypeStruct
    shapes = [(n,) + o.shape for o in owns[:6]] + [(n,) + o.shape[:2] + (EARLY * TILE,) for o in owns[6:]]
    kinds = 2 * (n - 1) + 1
    res = pl.pallas_call(
        functools.partial(forward_kernel, n, reps, width),
        grid=(nc + 1,),
        in_specs=[blk(width), full(nc, 1, C), full(nr, C), full(*vec.shape), full(*high.shape), full(*low.shape)]
        + [anywhere] * 8,
        out_specs=[blk(w) for w in (width, 512, 512, 1024, 1024, 16, 1024, 1024)]
        + [pl.BlockSpec((1, HEADS, VH, KH), lambda i: (last(i), 0, 0, 0))]
        + [full(T, width), full(T, width), full(8, width), full(16, 512), full(16, width)]
        + [anywhere] * 8,
        out_shape=[sd((T, w), BF) for w in (width, 512, 512, 1024, 1024, 16, 1024, 1024)]
        + [
            sd((nc, HEADS, VH, KH), BF),
            sd((T, width), F32),
            sd((T, width), BF),
            sd((8, width), F32),
            sd((16, 512), BF),
            sd((16, width), BF),
        ]
        + [sd(shape, BF) for shape in shapes],
        scratch_shapes=[
            pltpu.VMEM((HEADS, VH, KH), F32),
            pltpu.VMEM((nr, 512), F32),
            pltpu.VMEM((T, width), BF),
            pltpu.VMEM((T, 1024), BF),
            pltpu.VMEM((n,) + vec.shape, F32),
            pltpu.VMEM((n,) + high.shape, BF),
            pltpu.VMEM((n,) + low.shape, BF),
        ]
        + [pltpu.VMEM(shape, BF) for shape in shapes[:5]]
        + [
            pltpu.SemaphoreType.DMA((3, n - 1)),
            pltpu.SemaphoreType.DMA((3, n - 1)),
            pltpu.SemaphoreType.DMA((8, kinds)),
            pltpu.SemaphoreType.DMA((8, kinds)),
            pltpu.SemaphoreType.DMA((5,)),
        ],
        compiler_params=pltpu.CompilerParams(collective_id=0, has_side_effects=True, vmem_limit_bytes=60 << 20),
        name="gla_fwd_gather",
    )(x, segr, M, vec, high, low, *owns)
    return res[:14], [o.reshape(-1, o.shape[-1]) for o in res[14:20]] + list(res[20:])


def backward_kernel(n,reps,plan,half,*refs):
    (q_ref,k_ref,v_ref,g_ref,r_ref,o_ref,st_ref,dy_ref,a_ref,x_ref,dx_ref,
     wh_ref,vec_ref,nmlp_ref,segr_ref,m_ref,wq_ref,wk_ref,wv_ref,wg_ref,wl_ref)=refs[:21]
    bias_ref,gain_ref=vec_ref.at[2:3,0:512],vec_ref.at[3:4,0:VH]
    parts=refs[21:23]
    gt_ref,small_ref=refs[23:25]
    outs=refs[25:31]
    dstate,rcar,esc,dcs,dall,at_ref,dz_ref,low_acc,high_acc,gb_ref,gg_ref,smb,both,drs=refs[31:45]
    rest=refs[45:]
    step=pl.program_id(0); nc=(pl.num_programs(0)-1)//2
    p=Place(n,reps)
    items=[]
    for which,at,width,source in plan:
        count=7 if source is None else 6
        mem,rest=rest[:count],rest[count:]
        cols=pl.ds(at,width)
        out=[(lambda c,which=which,cols=cols: outs[which].at[c,:,cols],pl.ds(0,width))]
        if source is None:
            items.append(Reduce(p,out,mem[:4],mem[4:],part=parts[which].at[:,:,:,cols]))
        else:
            cols=pl.ds(source,width)
            items.append(Reduce(p,out,mem[:3],mem[3:],mine=both.at[0,:,:,cols],give=both.at[1,:,:,cols]))
    mem=rest
    small=Small(p,smb,small_ref,mem[:4],mem[4:])
    ready=[it for it in items if it.part is not None]
    fresh=[it for it in items if it.part is None]

    plan_at={}
    def book(it,times):
        for stage,t in enumerate(times): plan_at.setdefault(t,[]).append((stage,it))
    for j,it in enumerate(ready): book(it,(j//2,2+j,4+j,6+j,7+j,8+j,9+j))
    for j,it in enumerate(fresh): book(it,[8+j+s for s in range(Reduce.STAGES)])
    last=max(plan_at)+1

    def slot(t):
        for stage,it in sorted(plan_at.get(t,[]),key=lambda pair: pair[0]): it.stage(stage)

    @pl.when(step==0)
    def _():
        greet(Reduce.peers(p))
        for it in ready: it.start()
        for ref in (dstate,rcar,gb_ref,gg_ref,low_acc,high_acc,smb): ref[...]=jnp.zeros_like(ref)

    @pl.when(step<nc)
    def _():
        i=nc-1-step
        rows=pl.ds(pl.multiple_of(i*C,C),C)
        bwd_chunk(i,q_ref,k_ref,v_ref,g_ref,r_ref,o_ref,st_ref,dy_ref,wh_ref,bias_ref,gain_ref,segr_ref,m_ref,
                  dall.at[rows,0:512],dall.at[rows,512:1024],dall.at[rows,1024:2048],dall.at[rows,2048:3072],dz_ref,gb_ref,gg_ref,dstate,rcar,esc,dcs)
        dz=dz_ref[...]; a=a_ref[...]
        dr=dot_nt(dz,wh_ref[...]).astype(BF)
        drs[rows,:]=dr
        high_acc[...]+=dot_tn(r_ref[...],dz)
        low_acc[...]+=dot_tn(dr,a)
        at_ref[:,rows]=jnp.transpose(a)

    @pl.when(step>nc)
    def _():
        rows=pl.ds(pl.multiple_of((step-nc-1)*C,C),C)
        da=dot_nt(dall[rows,0:512],wq_ref[...])+dot_nt(dall[rows,512:1024],wk_ref[...])
        da=da+dot_nt(dall[rows,1024:2048],wv_ref[...])+dot_nt(dall[rows,2048:3072],wg_ref[...])+dot(drs[rows,:],wl_ref[...])
        x=x_ref[...].astype(F32)
        n1=lax.rsqrt(jnp.mean(x*x,axis=-1,keepdims=True)+1e-5)
        xn=x*n1
        dm=da*vec_ref[0:1,:]
        gt_ref[...]=dx_ref[...]+n1*(dm-xn*jnp.mean(dm*xn,axis=-1,keepdims=True))

    for t in range(8):
        @pl.when(step==t)
        def _(): slot(t)

    rs=2*half

    @pl.when(step==nc)
    def _():
        def product(at,width):
            cols=slice(at,at+width)
            w=dot(at_ref[...],dall[:,cols]).astype(BF)
            for s in range(n):
                both[p.core,s,:,cols]=w[s*rs:s*rs+half]
                both[1-p.core,s,:,cols]=w[s*rs+half:(s+1)*rs]

        smb[:,16:32,:]=jnp.broadcast_to(high_acc[...][None],(n,16,512))
        smb[:,32:33,:]=jnp.broadcast_to(gb_ref[...][None],(n,1,512))
        smb[:,33:34,0:256]=jnp.broadcast_to(gg_ref[...][None],(n,1,256))
        for s in range(n):
            at=slice(s*rs,(s+1)*rs)
            smb[s,0:16,0:rs]=low_acc[:,at]
            smb[s,35:36,0:rs]=nmlp_ref[:,at]
        for j,at in enumerate((2048,2560,1024,1536,0,512)):
            product(at,512)
            fresh[j].start()
            if j==1: small.swap().start()
            if j%2==1: slot(8+j//2)
            if j==5: small.stage(0)

    for t in range(11,19):
        @pl.when(step==t-11+nc+1)
        def _():
            slot(t)
            if t in (13,16): small.stage((t-10)//3)

    @pl.when(step==2*nc)
    def _():
        for t in range(19,last): slot(t)
        for it in items: it.settle()
        small.settle()

def backward(n,reps,q,k,v,g,r,o,st,dy,first,tokens,dx2,wh,vecs,nmlp,segr,weights,partials):
    T=q.shape[0]; nc=T//C; z=reps//2
    assert nc==8
    M=jnp.asarray(level_sums(),BF); nr=M.shape[0]
    blk=lambda w: pl.BlockSpec((C,w),lambda i:(jnp.maximum(nc-1-i,0),0))
    late=lambda w: pl.BlockSpec((C,w),lambda i:(jnp.clip(i-nc-1,0,nc-1),0))
    full=lambda *sh: pl.BlockSpec(sh,lambda i:(0,)*len(sh),pipeline_mode=pl.Buffered(1))
    sd=jax.ShapeDtypeStruct
    anywhere=pl.BlockSpec(memory_space=pl.ANY)
    half=first.shape[1]//(2*n)
    pairs=[q.reshape(n,2,q.shape[0]//(2*n),q.shape[1]) for q in partials]
    plan,scratch=[],[]
    for which,(pair,cut) in enumerate(zip(pairs,(4,2))):
        tiles=pair.shape[3]//128
        edges=[128*(tiles*j//cut) for j in range(cut+1)]
        for at,end in zip(edges[:-1],edges[1:]):
            plan.append((which,at,end-at,None)); scratch+=Reduce.scratch(n,z,pair.shape[2],end-at,True)
    for which,at,width,source in ((5,0,512,2048),(5,512,512,2560),(4,0,512,1024),(4,512,512,1536),(2,0,512,0),(3,0,512,512)):
        plan.append((which,at,width,source)); scratch+=Reduce.scratch(n,z,half,width,False)
    scratch+=Small.scratch(n,z,40,512)
    out=lambda h,w: sd((2,h,w),BF)
    res=pl.pallas_call(functools.partial(backward_kernel,n,reps,tuple(plan),half),grid=(2*nc+1,),
        in_specs=[blk(512),blk(512),blk(1024),blk(1024),blk(16),blk(1024),pl.BlockSpec((1,HEADS,VH,KH),lambda i:(jnp.maximum(nc-1-i,0),0,0,0)),blk(1024),
                  blk(1024),late(1024),late(1024),
                  full(16,512),full(8,1024),full(1,1024),full(nc,1,C),full(nr,C),
                  full(1024,512),full(1024,512),full(1024,1024),full(1024,1024),full(16,1024)]+[anywhere]*2,
        out_specs=[late(1024),pl.BlockSpec((40,512),lambda i:(0,0))]+[anywhere]*6,
        out_shape=[sd((T,1024),F32),sd((40,512),F32)]+[out(q.shape[2],q.shape[3]) for q in pairs]+[out(half,512),out(half,512),out(half,1024),out(half,1024)],
        scratch_shapes=[pltpu.VMEM((HEADS,VH,KH),F32),pltpu.VMEM((1,512),F32),pltpu.VMEM((nr,512),F32),pltpu.VMEM((C,1024),BF),
                        pltpu.VMEM((T,3072),BF),pltpu.VMEM((1024,T),BF),pltpu.VMEM((C,512),BF),pltpu.VMEM((16,1024),F32),pltpu.VMEM((16,512),F32),
                        pltpu.VMEM((1,512),F32),pltpu.VMEM((1,256),F32),pltpu.VMEM((n,40,512),F32),
                        pltpu.VMEM((2,n,half,3072),BF),pltpu.VMEM((T,16),BF)]+scratch,
        compiler_params=pltpu.CompilerParams(collective_id=2,has_side_effects=True,vmem_limit_bytes=63<<20),
        name="gla_bwd_reduce")(q,k,v,g,r,o,st,dy,first,tokens,dx2,wh,vecs,nmlp,segr,M,*weights,*pairs)
    return res[0],res[1],[x.reshape(-1,x.shape[2]) for x in res[2:]]


def matmul(left, right):
    return jnp.dot(left, right, preferred_element_type=F32)


def local(
    shards,
    reps,
    tokens,
    segments,
    cotangent,
    norm_mix,
    w_query,
    w_key,
    w_value,
    w_outgate,
    w_low,
    w_high,
    decay_bias,
    head_gain,
    w_out,
    norm_mlp,
    w_gate,
    w_up,
    w_down,
):
    total = tokens.shape[0] * tokens.shape[1]
    width = tokens.shape[2]
    segr = seg_rows(segments)
    pads = [-v.shape[0] % 128 for v in (decay_bias, head_gain)]
    zeros = [jnp.zeros((pad,), BF) for pad in pads]
    vec = jnp.concatenate([norm_mix, norm_mlp, decay_bias, zeros[0], head_gain, zeros[1]]).astype(F32)[None]
    (
        (first, query, keys, values, outgate, lowrank, mixed, heads, states, resid, second, vecs, high_w, low_w),
        (query_w, key_w, value_w, outgate_w, out_w, down_w, gate_w, up_w),
    ) = forward(
        shards,
        reps,
        tokens.reshape(total, width),
        segr,
        vec,
        w_high,
        w_low.T,
        (w_query, w_key, w_value, w_outgate, w_out, w_down, w_gate, w_up),
    )
    grad_out = cotangent.reshape(total, width)
    result, grad_resid, branch, part_norm_mlp, part_down, sum_gate, sum_up = feed(
        shards, reps, second, grad_out, resid, vecs, down_w, (gate_w, up_w), (w_gate, w_up)
    )
    part_out = dot_tn(mixed, branch)
    grad_mixed = dot_nt(branch, out_w).astype(BF)
    grad_inputs, small_sums, sums = backward(
        shards,
        reps,
        query,
        keys,
        values,
        outgate,
        lowrank,
        heads,
        states,
        grad_mixed,
        first,
        tokens.reshape(total, width),
        grad_resid,
        high_w,
        vecs,
        part_norm_mlp,
        segr,
        (query_w, key_w, value_w, outgate_w, low_w),
        (part_down, part_out.astype(BF)),
    )
    sum_gate, sum_up = [s.reshape(-1, s.shape[2]).astype(F32) for s in (sum_gate, sum_up)]
    sum_down, sum_out, sum_query, sum_key, sum_value, sum_outgate = [s.astype(F32) for s in sums]
    me = lax.axis_index("shard")
    rs = w_low.shape[0]

    def across(block, width):
        return lax.dynamic_slice_in_dim(block, me * width, width, axis=1)

    grad_low_w = small_sums[:16, :rs].T
    mixer = (
        (w_query, sum_query),
        (w_key, sum_key),
        (w_value, sum_value),
        (w_outgate, sum_outgate),
        (w_low, grad_low_w),
    )
    own = (
        sum(jnp.sum(w.astype(F32) * g, axis=1) for w, g in mixer) / norm_mix.astype(F32),
        small_sums[35, :rs],
        across(small_sums[32:33], decay_bias.shape[0]).reshape(-1),
        across(small_sums[33:34, :VH], head_gain.shape[0]).reshape(-1),
        grad_low_w,
        across(small_sums[16:32], w_high.shape[1]),
    )
    return (
        result.reshape(tokens.shape),
        grad_inputs.reshape(tokens.shape),
        own[0],
        sum_query,
        sum_key,
        sum_value,
        sum_outgate,
        own[4],
        own[5],
        own[2],
        own[3],
        sum_out,
        own[1],
        sum_gate,
        sum_up,
        sum_down,
    )


def solution(mesh):
    in_specs = (
        P(("rep", "shard"), None, None),
        P(("rep", "shard"), None),
        P(("rep", "shard"), None, None),
        P("shard"),
        P("shard", None),
        P("shard", None),
        P("shard", None),
        P("shard", None),
        P("shard", None),
        P(None, "shard"),
        P("shard"),
        P("shard"),
        P("shard", None),
        P("shard"),
        P("shard", None),
        P("shard", None),
        P("shard", None),
    )
    out_specs = (
        P(("rep", "shard"), None, None),
        P(("rep", "shard"), None, None),
        P("shard"),
        P("shard", None),
        P("shard", None),
        P("shard", None),
        P("shard", None),
        P("shard", None),
        P(None, "shard"),
        P("shard"),
        P("shard"),
        P("shard", None),
        P("shard"),
        P("shard", None),
        P("shard", None),
        P("shard", None),
    )
    return jax.shard_map(
        functools.partial(local, mesh.shape["shard"], mesh.shape["rep"]), mesh=mesh, in_specs=in_specs, out_specs=out_specs, check_vma=False)
```

```python
import functools
import numpy as np
import jax, jax.numpy as jnp
from jax import lax
from jax.experimental import pallas as pl
from jax.experimental.pallas import tpu as pltpu
from jax.sharding import PartitionSpec as P
HEADS=4; KH=128; VH=256; C=128
SCALE=KH**-0.5
LEVELS=(64,32,16,8,4,2,1)
F32=jnp.float32; BF=jnp.bfloat16

def level_sums():
    t=np.arange(C)[:,None]; u=np.arange(C)[None,:]
    rows=[]
    for h in LEVELS:
        ref=(t//(2*h))*(2*h)+h-1
        second=t>ref
        rows.append(np.where(second,(u>ref)&(u<=t),(u>t)&(u<=ref)))
    rows.append(u<=t); rows.append(u>t)
    return np.concatenate(rows,0).astype(np.float32)

def dot(a,b): return lax.dot_general(a,b,(((1,),(0,)),((),())),preferred_element_type=F32)
def dot_nt(a,b): return lax.dot_general(a,b,(((1,),(1,)),((),())),preferred_element_type=F32)
def dot_tn(a,b): return lax.dot_general(a,b,(((0,),(0,)),((),())),preferred_element_type=F32)

def gate_in(r_ref,wh_ref,bias_ref):
    return dot(r_ref[...],wh_ref[...])+bias_ref[...]

def log_rate(zb):
    return (jnp.minimum(zb,0.0)-jnp.log1p(jnp.exp(-jnp.abs(zb))))*(1.0/16.0)

def level_map(i,segr_ref):
    t=lax.broadcasted_iota(jnp.int32,(C,C),0); s=lax.broadcasted_iota(jnp.int32,(C,C),1)
    segr=segr_ref[i].astype(F32)
    prev=jnp.where(i==0,-1.0,segr_ref[jnp.maximum(i-1,0)][:,C-1:C].astype(F32))
    segc=jnp.sum(jnp.where(t==s,segr,0.0),axis=1,keepdims=True)
    before=jnp.sum(jnp.where(t==s+1,segr,0.0),axis=1,keepdims=True)
    first=lax.broadcasted_iota(jnp.int32,(C,1),0)==0
    start=jnp.where(first,prev,before)!=segc
    last=segr[:,C-1:C]
    lv=jnp.where(segc==segr,t^s,-1)
    return lv,t,s,(segc==prev).astype(F32),(segc==last).astype(F32),(prev==last).astype(F32),start

def fwd_chunk(i,q_ref,k_ref,v_ref,g_ref,r_ref,wh_ref,bias_ref,gain_ref,segr_ref,m_ref,y_ref,o_ref,st_ref,state,esc):
    f=log_rate(gate_in(r_ref,wh_ref,bias_ref)).astype(BF)
    esc[...]=jnp.exp(dot(m_ref[...],f))
    lv,t,s,keep,tail,stay,start=level_map(i,segr_ref)
    lv=jnp.where(t>=s,lv,-1)
    row=lax.broadcasted_iota(jnp.int32,(C,KH),0)
    nl=len(LEVELS)
    for h in range(HEADS):
        ks=slice(h*KH,(h+1)*KH); vs=slice(h*VH,(h+1)*VH)
        q=q_ref[:,ks].astype(F32)*SCALE; k=k_ref[:,ks].astype(F32); v=v_ref[:,vs]
        a=jnp.where(lv==0,dot_nt(q.astype(BF),k_ref[:,ks]),0.0)
        for l,hs in enumerate(LEVELS):
            x=(jnp.where((row&hs)!=0,q,k)*esc[l*C:(l+1)*C,ks]).astype(BF)
            a=jnp.where((lv>=hs)&(lv<2*hs),dot_nt(x,x),a)
        ec=esc[nl*C:(nl+1)*C,ks]; es=esc[(nl+1)*C:(nl+2)*C,ks]
        st=state[h]
        stb=st.astype(BF)
        st_ref[0,h]=stb
        o=dot(a.astype(BF),v)+dot_nt((q*ec*keep).astype(BF),stb)
        state[h]=st*(ec[C-1:C,:]*stay)+dot_tn(v,(k*es*tail).astype(BF))
        o_ref[:,vs]=o.astype(BF)
        m=lax.rsqrt(jnp.mean(o*o,axis=-1,keepdims=True)+1.0)
        g=g_ref[:,vs].astype(F32)
        y_ref[:,vs]=(o*m*gain_ref[...]*(g*jax.nn.sigmoid(g))).astype(BF)

def bwd_chunk(i,q_ref,k_ref,v_ref,g_ref,r_ref,o_ref,st_ref,dy_ref,wh_ref,bias_ref,gain_ref,segr_ref,m_ref,
             dq_ref,dk_ref,dv_ref,dg_ref,dz_ref,gb_ref,gg_ref,dstate,rcar,esc,dcs):
    zb=gate_in(r_ref,wh_ref,bias_ref)
    f=log_rate(zb).astype(BF)
    esc[...]=jnp.exp(dot(m_ref[...],f))
    lv,t,s,keep,tail,stay,start=level_map(i,segr_ref)
    lvu=jnp.where(t<=s,lv,-1)
    lower=t>=s
    row=lax.broadcasted_iota(jnp.int32,(C,KH),0)
    nl=len(LEVELS)
    gain=gain_ref[...]
    ggacc=jnp.zeros((1,VH),F32)
    for h in range(HEADS):
        ks=slice(h*KH,(h+1)*KH); vs=slice(h*VH,(h+1)*VH)
        o=o_ref[:,vs].astype(F32); g=g_ref[:,vs].astype(F32); dy=dy_ref[:,vs].astype(F32)
        m=lax.rsqrt(jnp.mean(o*o,axis=-1,keepdims=True)+1.0)
        sg=jax.nn.sigmoid(g); om=o*m
        u=dy*(g*sg)
        dg_ref[:,vs]=(dy*om*gain*(sg*(1.0+g*(1.0-sg)))).astype(BF)
        ggacc=ggacc+jnp.sum(u*om,axis=0,keepdims=True)
        ug=u*gain
        do=(m*ug-om*(m*m)*jnp.mean(ug*o,axis=-1,keepdims=True)).astype(BF)
        q=q_ref[:,ks].astype(F32)*SCALE; k=k_ref[:,ks].astype(F32); v=v_ref[:,vs]
        qb=q.astype(BF); kb=k_ref[:,ks]
        das=jnp.where(lower,dot_nt(do,v),dot_nt(v,do))
        dd=jnp.sum(jnp.where(t==s,das,0.0),axis=1,keepdims=True)
        at=jnp.where(lvu==0,dot_nt(kb,qb),0.0)
        ec=esc[nl*C:(nl+1)*C,ks]; es=esc[(nl+1)*C:(nl+2)*C,ks]
        stb=st_ref[0,h]
        ds=dstate[h]; dsb=ds.astype(BF)
        qe=(q*ec*keep).astype(BF); ke=(k*es*tail).astype(BF)
        dq=dd*k+dot(do,stb)*(ec*keep)
        dk=dd*q+dot(v,dsb)*(es*tail)
        for l,hs in enumerate(LEVELS):
            e=esc[l*C:(l+1)*C,ks]
            sec=(row&hs)!=0
            x=(jnp.where(sec,q,k)*e).astype(BF)
            sx=dot_nt(x,x)
            at=jnp.where((lvu>=hs)&(lvu<2*hs),sx,at)
            gl=jnp.where((lv>=hs)&(lv<2*hs),das,0.0).astype(BF)
            tt=dot(gl,x)*e
            dq=dq+jnp.where(sec,tt,0.0)
            dk=dk+jnp.where(sec,0.0,tt)
        dv_ref[:,vs]=(dot(at.astype(BF),do)+dot_nt(ke,dsb)).astype(BF)
        dq_ref[:,ks]=(dq*SCALE).astype(BF)
        dk_ref[:,ks]=dk.astype(BF)
        dsn=ds*(ec[C-1:C,:]*stay)+dot_tn(do,qe)
        dstate[h]=dsn
        dc=q*dq-k*dk
        hi=dc.astype(BF)
        dcs[:,ks]=hi; dcs[:,HEADS*KH+h*KH:HEADS*KH+(h+1)*KH]=(dc-hi.astype(F32)).astype(BF)
        rold=rcar[:,ks]
        rcar[:,ks]=jnp.sum(stb.astype(F32)*dsn,axis=0,keepdims=True)
        dcs2=rold
        um=jnp.where((lv>=0)&(t<=s),1.0,0.0).astype(BF)
        df=dot(um,dcs[:,ks])+dot(um,dcs[:,HEADS*KH+h*KH:HEADS*KH+(h+1)*KH])+tail*dcs2
        dp=jnp.where(start,0.0,df)*(jax.nn.sigmoid(-zb[:,ks])*(1.0/16.0))
        dz_ref[:,ks]=dp.astype(BF)
        gb_ref[:,ks]+=jnp.sum(dp,axis=0,keepdims=True)
    gg_ref[...]+=ggacc

def seg_rows(segments):
    b,l=segments.shape
    seg=segments if b==1 else segments+8*lax.broadcasted_iota(jnp.int32,(b,l),0)
    return seg.reshape(-1,1,C)


MESH = pl.DeviceIdType.MESH
TILE = 256
EARLY = 3


class Place:
    def __init__(self, n, reps):
        self.n, self.z = n, reps // 2
        self.rep = lax.axis_index("rep")
        self.me = lax.axis_index("shard")
        self.core = lax.rem(self.rep, 2)
        self.chip = self.rep // 2
        self.sib = (self.rep + 1 - 2 * self.core, self.me)

    def peer(self, step):
        return lax.rem(self.me + step, self.n)

    def flip(self, bit):
        if bit == 1:
            return self.me + 1 - 2 * lax.rem(self.me, 2)
        return lax.rem(self.me + 2, 4)

    def first(self):
        return jnp.where(self.core == 0, self.flip(1), self.flip(2))

    def second(self):
        return jnp.where(self.core == 0, self.flip(2), self.flip(1))


def greet(ids):
    barrier = pltpu.get_barrier_semaphore()
    for d in ids:
        pl.semaphore_signal(barrier, inc=1, device_id=d, device_id_type=MESH)
    pl.semaphore_wait(barrier, len(ids))


def remote(src, dst, ssem, rsem, device):
    return pltpu.make_async_remote_copy(
        src_ref=src, dst_ref=dst, send_sem=ssem, recv_sem=rsem, device_id=device, device_id_type=MESH
    )


def gather_sems(n, count):
    kinds = 2 * (n - 1) + 1
    return [pltpu.SemaphoreType.DMA((count, kinds)), pltpu.SemaphoreType.DMA((count, kinds))]


class Gather:
    def __init__(self, place, owns, fulls, sems):
        self.p, self.owns, self.fulls = place, owns, fulls
        self.ssem, self.rsem = sems

    def peers(self):
        p = self.p
        return [(p.rep, p.peer(j)) for j in range(1, p.n)] + [p.sib]

    def same(self, i):
        kind = 2 * (self.p.n - 1)
        return remote(
            self.owns[i], self.fulls[i].at[self.p.me], self.ssem[i].at[kind], self.rsem[i].at[kind], self.p.sib
        )

    def direct(self, i, kind, target):
        p = self.p
        return remote(
            self.owns[i].at[p.core],
            self.fulls[i].at[p.me, p.core],
            self.ssem[i].at[kind],
            self.rsem[i].at[kind],
            (p.rep, target),
        )

    def onward(self, i, kind, block, device):
        p = self.p
        view = self.fulls[i].at[block, p.core]
        return remote(view, view, self.ssem[i].at[kind], self.rsem[i].at[kind], device)

    def start(self, i):
        p = self.p
        if p.n == 4:
            self.direct(i, 0, p.first()).start()
            self.direct(i, 1, p.second()).start()
        else:
            for j in range(1, p.n):
                self.direct(i, j - 1, p.peer(j)).start()
        self.same(i).start()

    def blocks(self):
        p = self.p
        if p.n == 4:
            return [p.first(), p.second(), 3 - p.me]
        return [p.peer(p.n - j) for j in range(1, p.n)]

    def relay(self, i):
        p, blocks, last = self.p, self.blocks(), self.p.n - 1
        if p.n == 4:
            self.direct(i, 1, blocks[1]).wait_recv()
            self.onward(i, 2, blocks[1], (p.rep, blocks[0])).start()
            self.onward(i, last + 1, blocks[1], p.sib).start()
            self.direct(i, 0, blocks[0]).wait_recv()
            self.onward(i, last, blocks[0], p.sib).start()
        else:
            for j in range(last):
                self.direct(i, j, p.me).wait_recv()
                self.onward(i, last + j, blocks[j], p.sib).start()

    def pass_on(self, i):
        p, blocks, last = self.p, self.blocks(), self.p.n - 1
        if p.n == 4:
            self.onward(i, 2, blocks[2], (p.rep, blocks[0])).wait_recv()
            self.onward(i, last + 2, blocks[2], p.sib).start()

    def done(self, i):
        p, blocks, last = self.p, self.blocks(), self.p.n - 1
        self.same(i).wait()
        for j in range(last):
            self.direct(i, j, p.me).wait_send()
            arrival = self.onward(i, last + j, blocks[j], p.sib)
            arrival.wait_send()
            arrival.wait_recv()


def halves(w):
    return w.reshape(2, w.shape[0] // 2, w.shape[1])


def add_rows(dst, a, b):
    rows = dst.shape[0]
    slab = 32 if rows % 32 == 0 else 16

    def step(j, _):
        at = pl.ds(pl.multiple_of(j * slab, slab), slab)
        dst[at, :] = a[at, :] + b[at, :]
        return 0

    lax.fori_loop(0, rows // slab, step, 0)


class Reduce:
    STAGES = 7

    def __init__(self, place, out, bufs, sems, mine=None, give=None, part=None):
        self.p, self.out = place, out
        self.part = part
        self.square = place.n == 4
        self.line = place.z == 4
        bufs = list(bufs)
        if part is not None:
            mine, give = bufs.pop(0), part.at[:, 1 - place.core]
        self.mine, self.give = mine, give
        self.other, self.group, self.ring = bufs
        self.own = mine.at[place.me]
        self.rest = mine.at[place.second()] if self.square else None
        self.ssem, self.rsem, self.lsem = sems
        self.zbase = place.n
        self.end = self.zbase + (3 if self.line else place.z - 1)
        self.total = self.ring.at[2] if self.line else self.group.at[0]

    def copy(self, kind, src, dst, device):
        return remote(src, dst, self.ssem.at[kind], self.rsem.at[kind], device)

    def load(self):
        return pltpu.make_async_copy(self.part.at[:, self.p.core], self.mine, self.lsem.at[0])

    def swap(self):
        return self.copy(0, self.give, self.other, self.p.sib)

    def start(self):
        self.swap().start()
        if self.part is not None:
            self.load().start()

    def group_sends(self):
        p = self.p
        if self.square:
            to = (p.rep, p.first())
            return [
                self.copy(1, self.mine.at[p.first()], self.group.at[0], to),
                self.copy(2, self.mine.at[3 - p.me], self.group.at[1], to),
            ]
        return [
            self.copy(j, self.mine.at[p.peer(j)], self.group.at[j - 1], (p.rep, p.peer(j))) for j in range(1, p.n)
        ]

    def second_send(self):
        p = self.p
        return self.copy(3, self.rest, self.group.at[2], (p.rep, p.second()))

    def line_send(self, step):
        p = self.p
        if step == 0:
            to = jnp.where(p.chip == 0, p.rep + 2, p.rep - 2)
            return self.copy(self.zbase, self.own, self.ring.at[0], (to, p.me))
        if step == 1:
            to = jnp.where(p.chip == 1, p.rep + 2, p.rep - 2)
            return self.copy(self.zbase + 1, self.own, self.ring.at[1], (to, p.me))
        to = jnp.where(p.chip == 1, p.rep - 2, p.rep + 2)
        return self.copy(self.zbase + 2, self.total, self.total, (to, p.me))

    def ring_sends(self):
        p = self.p
        return [
            self.copy(self.zbase + j - 1, self.own, self.ring.at[p.chip], (lax.rem(p.rep + 2 * j, 2 * p.z), p.me))
            for j in range(1, p.z)
        ]

    def last_swaps(self):
        return [
            self.copy(self.end + j, self.total.at[:, lanes], half(self.p.core), self.p.sib)
            for j, (half, lanes) in enumerate(self.out)
        ]

    def stores(self):
        return [
            pltpu.make_async_copy(self.total.at[:, lanes], half(self.p.core), self.lsem.at[2 + j])
            for j, (half, lanes) in enumerate(self.out)
        ]

    def stage(self, k):
        p = self.p
        outer = (p.chip == 0) | (p.chip == 3)
        if k == 0:
            if self.part is not None:
                self.load().wait()
            self.swap().wait_recv()
            for b in range(p.n):
                add_rows(self.mine.at[b], self.mine.at[b], self.other.at[b])
            for c in self.group_sends():
                c.start()
        elif k == 1:
            for c in self.group_sends():
                c.wait_recv()
            add_rows(self.own, self.own, self.group.at[0])
            if self.square:
                add_rows(self.rest, self.rest, self.group.at[1])
                self.second_send().start()
            else:
                for j in range(1, p.n - 1):
                    add_rows(self.own, self.own, self.group.at[j])
        elif k == 2:
            if self.square:
                self.second_send().wait_recv()
                add_rows(self.own, self.own, self.group.at[2])
            if self.line:

                @pl.when(outer)
                def _():
                    self.line_send(0).start()

            else:
                for c in self.ring_sends():
                    c.start()
        elif k == 3:
            if self.line:

                @pl.when(jnp.logical_not(outer))
                def _():
                    self.line_send(0).wait_recv()
                    add_rows(self.own, self.own, self.ring.at[0])
                    self.line_send(1).start()

            else:
                for c in self.ring_sends():
                    c.wait_recv()
                self.ring[p.chip] = self.own[...]
                add_rows(self.total, self.ring.at[0], self.ring.at[1])
                for j in range(2, p.z):
                    add_rows(self.total, self.total, self.ring.at[j])
        elif k == 4:
            if self.line:

                @pl.when(jnp.logical_not(outer))
                def _():
                    self.line_send(1).wait_recv()
                    add_rows(self.total, self.own, self.ring.at[1])
                    self.line_send(2).start()

        elif k == 5:
            if self.line:

                @pl.when(outer)
                def _():
                    self.line_send(2).wait_recv()

            for c in self.last_swaps() + self.stores():
                c.start()
        else:
            for c in self.last_swaps():
                c.wait_recv()
            for c in self.stores():
                c.wait()

    def settle(self):
        p = self.p
        outer = (p.chip == 0) | (p.chip == 3)
        self.swap().wait_send()
        for c in self.group_sends():
            c.wait_send()
        if self.square:
            self.second_send().wait_send()
        if self.line:

            @pl.when(outer)
            def _():
                self.line_send(0).wait_send()

            @pl.when(jnp.logical_not(outer))
            def _():
                self.line_send(1).wait_send()
                self.line_send(2).wait_send()

        else:
            for c in self.ring_sends():
                c.wait_send()
        for c in self.last_swaps():
            c.wait_send()

    @staticmethod
    def peers(p):
        group = [(p.rep, p.peer(j)) for j in range(1, p.n)]
        along = [(lax.rem(p.rep + 2 * j, 2 * p.z), p.me) for j in range(1, p.z)]
        return group + along + [p.sib]

    @staticmethod
    def kinds(n, z):
        return n + (3 if z == 4 else z - 1) + 2

    @staticmethod
    def scratch(n, z, half, width, loaded, lead=()):
        lead = tuple(lead)
        kinds = Reduce.kinds(n, z)
        return ([pltpu.VMEM(lead + (n, half, width), BF)] if loaded else []) + [
            pltpu.VMEM(lead + (n, half, width), BF),
            pltpu.VMEM(lead + (n - 1, half, width), BF),
            pltpu.VMEM(lead + (3 if z == 4 else z, half, width), BF),
            pltpu.SemaphoreType.DMA(lead + (kinds,)),
            pltpu.SemaphoreType.DMA(lead + (kinds,)),
            pltpu.SemaphoreType.DMA(lead + (4,)),
        ]


class Small:
    def __init__(self, place, part, out, bufs, sems):
        self.p, self.part, self.out = place, part, out
        self.pair, self.other, self.group, self.ring = bufs
        self.ssem, self.rsem = sems

    def copy(self, kind, src, dst, device):
        return remote(src, dst, self.ssem.at[kind], self.rsem.at[kind], device)

    def swap(self):
        return self.copy(0, self.part, self.other, self.p.sib)

    def sends(self):
        p = self.p
        return [
            self.copy(j, self.pair.at[p.peer(j)], self.group.at[j - 1], (p.rep, p.peer(j))) for j in range(1, p.n)
        ]

    def along(self):
        p = self.p
        return [
            self.copy(p.n + j - 1, self.pair.at[p.me], self.ring.at[p.chip], (lax.rem(p.rep + 2 * j, 2 * p.z), p.me))
            for j in range(1, p.z)
        ]

    def stage(self, k):
        p = self.p
        if k == 0:
            self.swap().wait_recv()
            self.pair[...] = self.part[...] + self.other[...]
            for c in self.sends():
                c.start()
        elif k == 1:
            for c in self.sends():
                c.wait_recv()
            own = self.pair[p.me]
            for j in range(p.n - 1):
                own = own + self.group[j]
            self.pair[p.me] = own
            self.ring[p.chip] = own
            for c in self.along():
                c.start()
        else:
            for c in self.along():
                c.wait_recv()
            own = self.ring[0]
            for j in range(1, p.z):
                own = own + self.ring[j]
            self.out[...] = own

    def settle(self):
        self.swap().wait_send()
        for c in self.sends() + self.along():
            c.wait_send()

    @staticmethod
    def scratch(n, z, rows, width):
        return [
            pltpu.VMEM((n, rows, width), F32),
            pltpu.VMEM((n, rows, width), F32),
            pltpu.VMEM((n - 1, rows, width), F32),
            pltpu.VMEM((z, rows, width), F32),
            pltpu.SemaphoreType.DMA((n + z - 1,)),
            pltpu.SemaphoreType.DMA((n + z - 1,)),
        ]


def feed_kernel(n, reps, half, tile, *refs):
    b_ref, e_ref, x_ref, gain_ref, wd_ref = refs[:5]
    first, owns = refs[5:7], refs[7:9]
    res_out, dx_out, dm_out, norm_ref, down_out, gate_out, up_out, *late = refs[9:18]
    bt, acc, hid, dgate, dup, both, other, group, ring, ssem, rsem, lsem = refs[18:30]
    xs, res_ref, dx_ref, dm_ref, down_ref, moved, gsend, grecv, wbuf, wsem = refs[30:]
    step, tiles = pl.program_id(0), pl.num_programs(0) - 1
    p = Place(n, reps)
    total = b_ref.shape[0]
    rs = 2 * half
    rows_at = lambda j, size: pl.ds(pl.multiple_of(j * size, size), size)

    def fetch():
        return pltpu.make_async_copy(x_ref, xs, moved.at[0])

    def write(k, ref, out, rows):
        return pltpu.make_async_copy(ref.at[rows], out.at[rows], moved.at[k])

    def tile_gather(j):
        at = pl.ds(pl.multiple_of(j * tile, tile), tile)
        to = pl.ds(pl.multiple_of((j - EARLY) * tile, tile), tile)
        return Gather(
            p,
            [own.at[:, :, at] for own in owns],
            [full.at[:, :, :, to] for full in late],
            [[sem.at[j - EARLY, i] for i in range(2)] for sem in (gsend, grecv)],
        )

    def weights(j, begin):
        buf = lax.rem(j, 2)

        def one(source, at):
            for i in range(2):
                c = pltpu.make_async_copy(
                    source[i].at[:, :, :, pl.ds(pl.multiple_of(at * tile, tile), tile)], wbuf.at[buf, i], wsem.at[buf, i]
                )
                c.start() if begin else c.wait()

        @pl.when(j < EARLY)
        def _():
            one(first, j)

        @pl.when(j >= EARLY)
        def _():
            one(late, j - EARLY)

    def ahead(lead, run):
        @pl.when((step + lead >= EARLY) & (step + lead < tiles))
        def _():
            for i in range(2):
                run(tile_gather(step + lead), i)

    def item(j):
        cols = pl.ds(pl.multiple_of(j * tile, tile), tile)
        out = [
            (lambda c: gate_out.at[c, :, cols], pl.ds(0, tile)),
            (lambda c: up_out.at[c, :, cols], pl.ds(tile, tile)),
        ]
        return Reduce(
            p,
            out,
            [other.at[j], group.at[j], ring.at[j]],
            [ssem.at[j], rsem.at[j], lsem.at[j]],
            mine=both.at[j, 0],
            give=both.at[j, 1],
        )

    def slot(t):
        for k in range(Reduce.STAGES):

            @pl.when((t >= k) & (t - k < tiles))
            def _():
                item(t - k).stage(k)

    @pl.when(step == 0)
    def _():
        greet(Reduce.peers(p))
        fetch().start()
        weights(0, True)
        for j in range(EARLY, min(EARLY + 1, tiles)):
            for i in range(2):
                tile_gather(j).start(i)
        acc[...] = jnp.zeros_like(acc)
        dx_ref[...] = jnp.zeros_like(dx_ref)

        def turn(j, _):
            rows = rows_at(j, 128)
            bt[:, rows] = jnp.transpose(b_ref[rows, :])
            return 0

        lax.fori_loop(0, total // 128, turn, 0)

    @pl.when(step < tiles)
    def _():
        ahead(EARLY + 1, lambda g, i: g.start(i))
        weights(step, False)
        wg = wbuf[lax.rem(step, 2), 0].reshape(-1, tile)
        wu = wbuf[lax.rem(step, 2), 1].reshape(-1, tile)

        def rows_step(j, _):
            rows = rows_at(j, 512)
            b, e = b_ref[rows, :], e_ref[rows, :]
            gate = dot(b, wg)
            up = dot(b, wu)
            dh = dot_nt(e, wd_ref[...])
            sig = jax.nn.sigmoid(gate)
            swish = gate * sig
            h = (swish * up).astype(BF)
            dg = (dh * up * (sig * (1.0 + gate * (1.0 - sig)))).astype(BF)
            du = (dh * swish).astype(BF)
            down_ref[rows_at(step, tile), rows] = jnp.transpose(h)
            hid[rows, :] = h
            dgate[rows, :] = dg
            dup[rows, :] = du
            return 0

        def sums_step(j, _):
            rows = rows_at(j, 512)
            acc[rows, :] += dot(hid[rows, :], wd_ref[...])
            dx_ref[rows, :] += dot_nt(dgate[rows, :], wg) + dot_nt(dup[rows, :], wu)
            return 0

        lax.fori_loop(0, total // 512, rows_step, 0)

        ahead(EARLY, lambda g, i: g.relay(i))
        ahead(EARLY - 1, lambda g, i: g.pass_on(i))
        ahead(1, lambda g, i: g.done(i))

        @pl.when(step + 1 < tiles)
        def _():
            weights(step + 1, True)

        @pl.when(step > 0)
        def _():
            slot(step - 1)

        for at, d in ((0, dgate), (tile, dup)):
            w = dot(bt[...], d[...]).astype(BF)
            for s in range(n):
                both[step, p.core, s, :, at : at + tile] = w[s * rs : s * rs + half]
                both[step, 1 - p.core, s, :, at : at + tile] = w[s * rs + half : (s + 1) * rs]
        item(step).start()
        lax.fori_loop(0, total // 512, sums_step, 0)

    @pl.when(step == tiles)
    def _():
        norm_ref[...] = jnp.zeros_like(norm_ref)

        def finish(j, _):
            rows = rows_at(j, 128)
            x = xs[rows, :]
            res_ref[rows, :] = (x + acc[rows, :]).astype(BF)
            inv = lax.rsqrt(jnp.mean(x * x, axis=-1, keepdims=True) + 1e-5)
            xn = x * inv
            db = dx_ref[rows, :]
            norm_ref[...] += jnp.sum(db * xn, axis=0, keepdims=True)
            dbg = db * gain_ref[1:2, :]
            dx = e_ref[rows, :].astype(F32) + inv * (dbg - xn * jnp.mean(dbg * xn, axis=-1, keepdims=True))
            dx_ref[rows, :] = dx
            dm_ref[rows, :] = dx.astype(BF)
            return 0

        fetch().wait()

        def turn_down(j, _):
            slot(tiles - 1 + j)
            rows = rows_at(j, down_ref.shape[0] // 4)
            down_ref[rows, :] = dot(down_ref[rows, :], e_ref[...]).astype(BF)
            write(1 + j, down_ref, down_out, rows).start()
            return 0

        lax.fori_loop(0, 4, turn_down, 0)
        slot(tiles + 3)
        lax.fori_loop(0, total // 128, finish, 0)
        every = pl.ds(0, total)
        results = [
            write(5, res_ref, res_out, every),
            write(6, dx_ref, dx_out, every),
            write(7, dm_ref, dm_out, every),
        ]
        for c in results:
            c.start()

        def tail(t, _):
            slot(t)
            return 0

        lax.fori_loop(tiles + 4, tiles + Reduce.STAGES - 1, tail, 0)

        def settle(j, _):
            item(j).settle()
            return 0

        lax.fori_loop(0, tiles, settle, 0)
        for j in range(4):
            write(1 + j, down_ref, down_out, rows_at(j, down_ref.shape[0] // 4)).wait()
        for c in results:
            c.wait()


def feed(n, reps, b, e, x2, gain, wd, first, owns):
    total, width = b.shape
    owns = [halves(w) for w in owns]
    ff = wd.shape[0]
    tile, z = TILE, reps // 2
    tiles, half = ff // tile, width // (2 * n)
    once = lambda *sh: pl.BlockSpec(sh, lambda j: (0,) * len(sh), pipeline_mode=pl.Buffered(1))
    row = lambda: pl.BlockSpec((tile, width), lambda j: (jnp.minimum(j, tiles - 1), 0))
    anywhere = pl.BlockSpec(memory_space=pl.ANY)
    sd = jax.ShapeDtypeStruct
    return pl.pallas_call(
        functools.partial(feed_kernel, n, reps, half, tile),
        grid=(tiles + 1,),
        in_specs=[once(total, width)] * 2 + [anywhere, once(8, width), row()] + [anywhere] * 4,
        out_specs=[anywhere] * 3 + [once(1, width)] + [anywhere] * 5,
        out_shape=[
            sd((total, width), BF),
            sd((total, width), F32),
            sd((total, width), BF),
            sd((1, width), F32),
            sd((ff, total), BF),
            sd((2, half, ff), BF),
            sd((2, half, ff), BF),
            sd((n, 2, half, ff - EARLY * tile), BF),
            sd((n, 2, half, ff - EARLY * tile), BF),
        ],
        scratch_shapes=[
            pltpu.VMEM((width, total), BF),
            pltpu.VMEM((total, width), F32),
            pltpu.VMEM((total, tile), BF),
            pltpu.VMEM((total, tile), BF),
            pltpu.VMEM((total, tile), BF),
            pltpu.VMEM((tiles, 2, n, half, 2 * tile), BF),
        ]
        + Reduce.scratch(n, z, half, 2 * tile, False, (tiles,))
        + [
            pltpu.VMEM((total, width), F32),
            pltpu.VMEM((total, width), BF),
            pltpu.VMEM((total, width), F32),
            pltpu.VMEM((total, width), BF),
            pltpu.VMEM((ff, total), BF),
            pltpu.SemaphoreType.DMA((8,)),
            pltpu.SemaphoreType.DMA((tiles - EARLY, 2, 2 * (n - 1) + 1)),
            pltpu.SemaphoreType.DMA((tiles - EARLY, 2, 2 * (n - 1) + 1)),
            pltpu.VMEM((2, 2, n, 2, half, tile), BF),
            pltpu.SemaphoreType.DMA((2, 2)),
        ],
        compiler_params=pltpu.CompilerParams(collective_id=1, has_side_effects=True, vmem_limit_bytes=63 << 20),
        name="feed_forward",
    )(b, e, x2, gain, wd, *first, *owns)[:7]


def forward_kernel(n, reps, width, *refs):
    x_ref, segr_ref, m_ref, vec_ref, high_ref, low_ref = refs[:6]
    owns = refs[6:14]
    a_ref, q_ref, k_ref, v_ref, g_ref, r_ref, y_ref, o_ref, st_ref = refs[14:23]
    x2_ref, b_ref, vec_out, high_out, low_out = refs[23:28]
    outs = refs[28:36]
    state, esc, xs, ys, vecs, highs, lows = refs[36:43]
    kept = refs[43:48]
    small_send, small_recv, ssem, rsem, lsem = refs[48:]
    step, nc = pl.program_id(0), pl.num_programs(0) - 1
    p = Place(n, reps)
    early = outs[6].shape[3]
    owns = list(owns[:6]) + [own.at[:, :, 0:early] for own in owns[6:]]
    gather = Gather(
        p, owns, list(kept) + list(outs[5:]), [[sem.at[i] for i in range(8)] for sem in (ssem, rsem)]
    )
    smalls = [(vec_ref, vecs), (high_ref, highs), (low_ref, lows)]

    def small(k, j):
        src, dst = smalls[k]
        return remote(src, dst.at[p.me], small_send.at[k, j - 1], small_recv.at[k, j - 1], (p.rep, p.peer(j)))

    def keep(i):
        return pltpu.make_async_copy(kept[i], outs[i], lsem.at[i])

    def whole(i):
        w = kept[i][...]
        return w.reshape(-1, w.shape[-1])

    @pl.when(step == 0)
    def _():
        greet(gather.peers())
        for i in range(4):
            gather.start(i)
        for k in range(3):
            for j in range(1, n):
                small(k, j).start()
            src, dst = smalls[k]
            dst[p.me] = src[...]
        for i in range(4):
            gather.relay(i)
        for i in range(4, 8):
            gather.start(i)
        for k in range(3):
            for j in range(1, n):
                small(k, j).wait()
        rs = low_ref.shape[1]
        for s in range(n):
            at = slice(s * rs, (s + 1) * rs)
            vec_out[0:1, at] = vecs[s, :, 0:rs]
            vec_out[1:2, at] = vecs[s, :, rs : 2 * rs]
            low_out[:, at] = lows[s]

        def spread(part, out_width):
            own = part(0).shape[1]
            total = None
            for s in range(n):
                col = lax.broadcasted_iota(jnp.int32, (own, out_width), 1)
                row = lax.broadcasted_iota(jnp.int32, (own, out_width), 0)
                piece = dot(part(s), (col == row + s * own).astype(F32).astype(BF))
                total = piece if total is None else total + piece
            return total

        nb, ng = 512 // n, VH // n
        vec_out[2:3, 0:512] = spread(lambda s: vecs[s, :, 2 * rs : 2 * rs + nb].astype(BF), 512)
        vec_out[3:4, 0:VH] = spread(lambda s: vecs[s, :, -128:][:, 0:ng].astype(BF), VH)
        high_out[...] = spread(lambda s: highs[s], 512).astype(BF)
        for i in range(4):
            gather.pass_on(i)
        for i in range(4):
            gather.done(i)
            keep(i).start()
        state[...] = jnp.zeros_like(state)

    @pl.when(step < nc)
    def _():
        rows = pl.ds(pl.multiple_of(step * C, C), C)
        xb = x_ref[...]
        xs[rows, :] = xb
        x = xb.astype(F32)
        inv = lax.rsqrt(jnp.mean(x * x, axis=-1, keepdims=True) + 1e-5)
        a = (x * inv * vec_out[0:1, :]).astype(BF)
        a_ref[...] = a
        q_ref[...] = dot(a, whole(0)).astype(BF)
        k_ref[...] = dot(a, whole(1)).astype(BF)
        v_ref[...] = dot(a, whole(2)).astype(BF)
        g_ref[...] = dot(a, whole(3)).astype(BF)
        r_ref[...] = dot_nt(a, low_out[...]).astype(BF)
        fwd_chunk(
            step, q_ref, k_ref, v_ref, g_ref, r_ref, high_out, vec_out.at[2:3, 0:512], vec_out.at[3:4, 0:VH],
            segr_ref, m_ref, y_ref, o_ref, st_ref, state, esc,
        )
        ys[rows, :] = y_ref[...]

    for at, run in (
        (1, lambda: gather.relay(4)),
        (3, lambda: gather.pass_on(4)),
        (4, lambda: gather.relay(5)),
        (5, lambda: gather.relay(6)),
        (6, lambda: gather.relay(7)),
        (7, lambda: gather.pass_on(5)),
    ):
        pl.when(step == at)(run)

    @pl.when(step == nc)
    def _():
        gather.done(4)
        keep(4).start()

        def join(j, _):
            rows = pl.ds(pl.multiple_of(j * 256, 256), 256)
            x2 = xs[rows, :].astype(F32) + dot(ys[rows, :], whole(4))
            x2_ref[rows, :] = x2
            inv = lax.rsqrt(jnp.mean(x2 * x2, axis=-1, keepdims=True) + 1e-5)
            b_ref[rows, :] = (x2 * inv * vec_out[1:2, :]).astype(BF)
            return 0

        lax.fori_loop(0, xs.shape[0] // 256, join, 0)
        gather.pass_on(6)
        gather.pass_on(7)
        for i in range(5, 8):
            gather.done(i)
        for i in range(5):
            keep(i).wait()


def forward(n, reps, x, segr, vec, high, low, weights):
    T, width = x.shape
    nc = T // C
    M = jnp.asarray(level_sums(), BF)
    nr = M.shape[0]
    owns = [halves(w) for w in weights]
    last = lambda i: jnp.minimum(i, nc - 1)
    blk = lambda w: pl.BlockSpec((C, w), lambda i: (last(i), 0))
    full = lambda *sh: pl.BlockSpec(sh, lambda i: (0,) * len(sh), pipeline_mode=pl.Buffered(1))
    anywhere = pl.BlockSpec(memory_space=pl.ANY)
    sd = jax.ShapeDtypeStruct
    shapes = [(n,) + o.shape for o in owns[:6]] + [(n,) + o.shape[:2] + (EARLY * TILE,) for o in owns[6:]]
    kinds = 2 * (n - 1) + 1
    res = pl.pallas_call(
        functools.partial(forward_kernel, n, reps, width),
        grid=(nc + 1,),
        in_specs=[blk(width), full(nc, 1, C), full(nr, C), full(*vec.shape), full(*high.shape), full(*low.shape)]
        + [anywhere] * 8,
        out_specs=[blk(w) for w in (width, 512, 512, 1024, 1024, 16, 1024, 1024)]
        + [pl.BlockSpec((1, HEADS, VH, KH), lambda i: (last(i), 0, 0, 0))]
        + [full(T, width), full(T, width), full(8, width), full(16, 512), full(16, width)]
        + [anywhere] * 8,
        out_shape=[sd((T, w), BF) for w in (width, 512, 512, 1024, 1024, 16, 1024, 1024)]
        + [
            sd((nc, HEADS, VH, KH), BF),
            sd((T, width), F32),
            sd((T, width), BF),
            sd((8, width), F32),
            sd((16, 512), BF),
            sd((16, width), BF),
        ]
        + [sd(shape, BF) for shape in shapes],
        scratch_shapes=[
            pltpu.VMEM((HEADS, VH, KH), F32),
            pltpu.VMEM((nr, 512), F32),
            pltpu.VMEM((T, width), BF),
            pltpu.VMEM((T, 1024), BF),
            pltpu.VMEM((n,) + vec.shape, F32),
            pltpu.VMEM((n,) + high.shape, BF),
            pltpu.VMEM((n,) + low.shape, BF),
        ]
        + [pltpu.VMEM(shape, BF) for shape in shapes[:5]]
        + [
            pltpu.SemaphoreType.DMA((3, n - 1)),
            pltpu.SemaphoreType.DMA((3, n - 1)),
            pltpu.SemaphoreType.DMA((8, kinds)),
            pltpu.SemaphoreType.DMA((8, kinds)),
            pltpu.SemaphoreType.DMA((5,)),
        ],
        compiler_params=pltpu.CompilerParams(collective_id=0, has_side_effects=True, vmem_limit_bytes=60 << 20),
        name="gla_fwd_gather",
    )(x, segr, M, vec, high, low, *owns)
    return res[:14], [o.reshape(-1, o.shape[-1]) for o in res[14:20]] + list(res[20:])


def backward_kernel(n,reps,plan,half,*refs):
    (q_ref,k_ref,v_ref,g_ref,r_ref,o_ref,st_ref,dy_ref,a_ref,x_ref,dx_ref,
     wh_ref,vec_ref,nmlp_ref,segr_ref,m_ref,wq_ref,wk_ref,wv_ref,wg_ref,wl_ref)=refs[:21]
    bias_ref,gain_ref=vec_ref.at[2:3,0:512],vec_ref.at[3:4,0:VH]
    parts=refs[21:23]
    gt_ref,small_ref=refs[23:25]
    outs=refs[25:31]
    dstate,rcar,esc,dcs,dall,at_ref,dz_ref,low_acc,high_acc,gb_ref,gg_ref,smb,both,drs=refs[31:45]
    rest=refs[45:]
    step=pl.program_id(0); nc=(pl.num_programs(0)-1)//2
    p=Place(n,reps)
    items=[]
    for which,at,width,source in plan:
        count=7 if source is None else 6
        mem,rest=rest[:count],rest[count:]
        cols=pl.ds(at,width)
        out=[(lambda c,which=which,cols=cols: outs[which].at[c,:,cols],pl.ds(0,width))]
        if source is None:
            items.append(Reduce(p,out,mem[:4],mem[4:],part=parts[which].at[:,:,:,cols]))
        else:
            cols=pl.ds(source,width)
            items.append(Reduce(p,out,mem[:3],mem[3:],mine=both.at[0,:,:,cols],give=both.at[1,:,:,cols]))
    mem=rest
    small=Small(p,smb,small_ref,mem[:4],mem[4:])
    ready=[it for it in items if it.part is not None]
    fresh=[it for it in items if it.part is None]

    plan_at={}
    def book(it,times):
        for stage,t in enumerate(times): plan_at.setdefault(t,[]).append((stage,it))
    for j,it in enumerate(ready): book(it,(j//2,2+j,4+j,6+j,7+j,8+j,9+j))
    for j,it in enumerate(fresh): book(it,[8+j+s for s in range(Reduce.STAGES)])
    last=max(plan_at)+1

    def slot(t):
        for stage,it in sorted(plan_at.get(t,[]),key=lambda pair: pair[0]): it.stage(stage)

    @pl.when(step==0)
    def _():
        greet(Reduce.peers(p))
        for it in ready: it.start()
        for ref in (dstate,rcar,gb_ref,gg_ref,low_acc,high_acc,smb): ref[...]=jnp.zeros_like(ref)

    @pl.when(step<nc)
    def _():
        i=nc-1-step
        rows=pl.ds(pl.multiple_of(i*C,C),C)
        bwd_chunk(i,q_ref,k_ref,v_ref,g_ref,r_ref,o_ref,st_ref,dy_ref,wh_ref,bias_ref,gain_ref,segr_ref,m_ref,
                  dall.at[rows,0:512],dall.at[rows,512:1024],dall.at[rows,1024:2048],dall.at[rows,2048:3072],dz_ref,gb_ref,gg_ref,dstate,rcar,esc,dcs)
        dz=dz_ref[...]; a=a_ref[...]
        dr=dot_nt(dz,wh_ref[...]).astype(BF)
        drs[rows,:]=dr
        high_acc[...]+=dot_tn(r_ref[...],dz)
        low_acc[...]+=dot_tn(dr,a)
        at_ref[:,rows]=jnp.transpose(a)

    @pl.when(step>nc)
    def _():
        rows=pl.ds(pl.multiple_of((step-nc-1)*C,C),C)
        da=dot_nt(dall[rows,0:512],wq_ref[...])+dot_nt(dall[rows,512:1024],wk_ref[...])
        da=da+dot_nt(dall[rows,1024:2048],wv_ref[...])+dot_nt(dall[rows,2048:3072],wg_ref[...])+dot(drs[rows,:],wl_ref[...])
        x=x_ref[...].astype(F32)
        n1=lax.rsqrt(jnp.mean(x*x,axis=-1,keepdims=True)+1e-5)
        xn=x*n1
        dm=da*vec_ref[0:1,:]
        gt_ref[...]=dx_ref[...]+n1*(dm-xn*jnp.mean(dm*xn,axis=-1,keepdims=True))

    for t in range(8):
        @pl.when(step==t)
        def _(): slot(t)

    rs=2*half

    @pl.when(step==nc)
    def _():
        def product(at,width):
            cols=slice(at,at+width)
            w=dot(at_ref[...],dall[:,cols]).astype(BF)
            for s in range(n):
                both[p.core,s,:,cols]=w[s*rs:s*rs+half]
                both[1-p.core,s,:,cols]=w[s*rs+half:(s+1)*rs]

        smb[:,16:32,:]=jnp.broadcast_to(high_acc[...][None],(n,16,512))
        smb[:,32:33,:]=jnp.broadcast_to(gb_ref[...][None],(n,1,512))
        smb[:,33:34,0:256]=jnp.broadcast_to(gg_ref[...][None],(n,1,256))
        for s in range(n):
            at=slice(s*rs,(s+1)*rs)
            smb[s,0:16,0:rs]=low_acc[:,at]
            smb[s,35:36,0:rs]=nmlp_ref[:,at]
        for j,at in enumerate((2048,2560,1024,1536,0,512)):
            product(at,512)
            fresh[j].start()
            if j==1: small.swap().start()
            if j%2==1: slot(8+j//2)
            if j==5: small.stage(0)

    for t in range(11,19):
        @pl.when(step==t-11+nc+1)
        def _():
            slot(t)
            if t in (13,16): small.stage((t-10)//3)

    @pl.when(step==2*nc)
    def _():
        for t in range(19,last): slot(t)
        for it in items: it.settle()
        small.settle()

def backward(n,reps,q,k,v,g,r,o,st,dy,first,tokens,dx2,wh,vecs,nmlp,segr,weights,partials):
    T=q.shape[0]; nc=T//C; z=reps//2
    assert nc==8
    M=jnp.asarray(level_sums(),BF); nr=M.shape[0]
    blk=lambda w: pl.BlockSpec((C,w),lambda i:(jnp.maximum(nc-1-i,0),0))
    late=lambda w: pl.BlockSpec((C,w),lambda i:(jnp.clip(i-nc-1,0,nc-1),0))
    full=lambda *sh: pl.BlockSpec(sh,lambda i:(0,)*len(sh),pipeline_mode=pl.Buffered(1))
    sd=jax.ShapeDtypeStruct
    anywhere=pl.BlockSpec(memory_space=pl.ANY)
    half=first.shape[1]//(2*n)
    pairs=[q.reshape(n,2,q.shape[0]//(2*n),q.shape[1]) for q in partials]
    plan,scratch=[],[]
    for which,(pair,cut) in enumerate(zip(pairs,(4,2))):
        tiles=pair.shape[3]//128
        edges=[128*(tiles*j//cut) for j in range(cut+1)]
        for at,end in zip(edges[:-1],edges[1:]):
            plan.append((which,at,end-at,None)); scratch+=Reduce.scratch(n,z,pair.shape[2],end-at,True)
    for which,at,width,source in ((5,0,512,2048),(5,512,512,2560),(4,0,512,1024),(4,512,512,1536),(2,0,512,0),(3,0,512,512)):
        plan.append((which,at,width,source)); scratch+=Reduce.scratch(n,z,half,width,False)
    scratch+=Small.scratch(n,z,40,512)
    out=lambda h,w: sd((2,h,w),BF)
    res=pl.pallas_call(functools.partial(backward_kernel,n,reps,tuple(plan),half),grid=(2*nc+1,),
        in_specs=[blk(512),blk(512),blk(1024),blk(1024),blk(16),blk(1024),pl.BlockSpec((1,HEADS,VH,KH),lambda i:(jnp.maximum(nc-1-i,0),0,0,0)),blk(1024),
                  blk(1024),late(1024),late(1024),
                  full(16,512),full(8,1024),full(1,1024),full(nc,1,C),full(nr,C),
                  full(1024,512),full(1024,512),full(1024,1024),full(1024,1024),full(16,1024)]+[anywhere]*2,
        out_specs=[late(1024),pl.BlockSpec((40,512),lambda i:(0,0))]+[anywhere]*6,
        out_shape=[sd((T,1024),F32),sd((40,512),F32)]+[out(q.shape[2],q.shape[3]) for q in pairs]+[out(half,512),out(half,512),out(half,1024),out(half,1024)],
        scratch_shapes=[pltpu.VMEM((HEADS,VH,KH),F32),pltpu.VMEM((1,512),F32),pltpu.VMEM((nr,512),F32),pltpu.VMEM((C,1024),BF),
                        pltpu.VMEM((T,3072),BF),pltpu.VMEM((1024,T),BF),pltpu.VMEM((C,512),BF),pltpu.VMEM((16,1024),F32),pltpu.VMEM((16,512),F32),
                        pltpu.VMEM((1,512),F32),pltpu.VMEM((1,256),F32),pltpu.VMEM((n,40,512),F32),
                        pltpu.VMEM((2,n,half,3072),BF),pltpu.VMEM((T,16),BF)]+scratch,
        compiler_params=pltpu.CompilerParams(collective_id=2,has_side_effects=True,vmem_limit_bytes=63<<20),
        name="gla_bwd_reduce")(q,k,v,g,r,o,st,dy,first,tokens,dx2,wh,vecs,nmlp,segr,M,*weights,*pairs)
    return res[0],res[1],[x.reshape(-1,x.shape[2]) for x in res[2:]]


def matmul(left, right):
    return jnp.dot(left, right, preferred_element_type=F32)


def local(
    shards,
    reps,
    tokens,
    segments,
    cotangent,
    norm_mix,
    w_query,
    w_key,
    w_value,
    w_outgate,
    w_low,
    w_high,
    decay_bias,
    head_gain,
    w_out,
    norm_mlp,
    w_gate,
    w_up,
    w_down,
):
    total = tokens.shape[0] * tokens.shape[1]
    width = tokens.shape[2]
    segr = seg_rows(segments)
    pads = [-v.shape[0] % 128 for v in (decay_bias, head_gain)]
    zeros = [jnp.zeros((pad,), BF) for pad in pads]
    vec = jnp.concatenate([norm_mix, norm_mlp, decay_bias, zeros[0], head_gain, zeros[1]]).astype(F32)[None]
    (
        (first, query, keys, values, outgate, lowrank, mixed, heads, states, resid, second, vecs, high_w, low_w),
        (query_w, key_w, value_w, outgate_w, out_w, down_w, gate_w, up_w),
    ) = forward(
        shards,
        reps,
        tokens.reshape(total, width),
        segr,
        vec,
        w_high,
        w_low.T,
        (w_query, w_key, w_value, w_outgate, w_out, w_down, w_gate, w_up),
    )
    grad_out = cotangent.reshape(total, width)
    result, grad_resid, branch, part_norm_mlp, part_down, sum_gate, sum_up = feed(
        shards, reps, second, grad_out, resid, vecs, down_w, (gate_w, up_w), (w_gate, w_up)
    )
    part_out = dot_tn(mixed, branch)
    grad_mixed = dot_nt(branch, out_w).astype(BF)
    grad_inputs, small_sums, sums = backward(
        shards,
        reps,
        query,
        keys,
        values,
        outgate,
        lowrank,
        heads,
        states,
        grad_mixed,
        first,
        tokens.reshape(total, width),
        grad_resid,
        high_w,
        vecs,
        part_norm_mlp,
        segr,
        (query_w, key_w, value_w, outgate_w, low_w),
        (part_down, part_out.astype(BF)),
    )
    sum_gate, sum_up = [s.reshape(-1, s.shape[2]).astype(F32) for s in (sum_gate, sum_up)]
    sum_down, sum_out, sum_query, sum_key, sum_value, sum_outgate = [s.astype(F32) for s in sums]
    me = lax.axis_index("shard")
    rs = w_low.shape[0]

    def across(block, width):
        return lax.dynamic_slice_in_dim(block, me * width, width, axis=1)

    grad_low_w = small_sums[:16, :rs].T
    mixer = (
        (w_query, sum_query),
        (w_key, sum_key),
        (w_value, sum_value),
        (w_outgate, sum_outgate),
        (w_low, grad_low_w),
    )
    own = (
        sum(jnp.sum(w.astype(F32) * g, axis=1) for w, g in mixer) / norm_mix.astype(F32),
        small_sums[35, :rs],
        across(small_sums[32:33], decay_bias.shape[0]).reshape(-1),
        across(small_sums[33:34, :VH], head_gain.shape[0]).reshape(-1),
        grad_low_w,
        across(small_sums[16:32], w_high.shape[1]),
    )
    return (
        result.reshape(tokens.shape),
        grad_inputs.reshape(tokens.shape),
        own[0],
        sum_query,
        sum_key,
        sum_value,
        sum_outgate,
        own[4],
        own[5],
        own[2],
        own[3],
        sum_out,
        own[1],
        sum_gate,
        sum_up,
        sum_down,
    )


def solution(mesh):
    in_specs = (
        P(("rep", "shard"), None, None),
        P(("rep", "shard"), None),
        P(("rep", "shard"), None, None),
        P("shard"),
        P("shard", None),
        P("shard", None),
        P("shard", None),
        P("shard", None),
        P("shard", None),
        P(None, "shard"),
        P("shard"),
        P("shard"),
        P("shard", None),
        P("shard"),
        P("shard", None),
        P("shard", None),
        P("shard", None),
    )
    out_specs = (
        P(("rep", "shard"), None, None),
        P(("rep", "shard"), None, None),
        P("shard"),
        P("shard", None),
        P("shard", None),
        P("shard", None),
        P("shard", None),
        P("shard", None),
        P(None, "shard"),
        P("shard"),
        P("shard"),
        P("shard", None),
        P("shard"),
        P("shard", None),
        P("shard", None),
        P("shard", None),
    )
    return jax.shard_map(
        functools.partial(local, mesh.shape["shard"], mesh.shape["rep"]), mesh=mesh, in_specs=in_specs, out_specs=out_specs, check_vma=False)
```

```python
import functools
import numpy as np
import jax, jax.numpy as jnp
from jax import lax
from jax.experimental import pallas as pl
from jax.experimental.pallas import tpu as pltpu
from jax.sharding import PartitionSpec as P
HEADS=4; KH=128; VH=256; C=128
SCALE=KH**-0.5
LEVELS=(64,32,16,8,4,2,1)
F32=jnp.float32; BF=jnp.bfloat16

def level_sums():
    t=np.arange(C)[:,None]; u=np.arange(C)[None,:]
    rows=[]
    for h in LEVELS:
        ref=(t//(2*h))*(2*h)+h-1
        second=t>ref
        rows.append(np.where(second,(u>ref)&(u<=t),(u>t)&(u<=ref)))
    rows.append(u<=t); rows.append(u>t)
    return np.concatenate(rows,0).astype(np.float32)

def dot(a,b): return lax.dot_general(a,b,(((1,),(0,)),((),())),preferred_element_type=F32)
def dot_nt(a,b): return lax.dot_general(a,b,(((1,),(1,)),((),())),preferred_element_type=F32)
def dot_tn(a,b): return lax.dot_general(a,b,(((0,),(0,)),((),())),preferred_element_type=F32)

def gate_in(r_ref,wh_ref,bias_ref):
    return dot(r_ref[...],wh_ref[...])+bias_ref[...]

def log_rate(zb):
    return (jnp.minimum(zb,0.0)-jnp.log1p(jnp.exp(-jnp.abs(zb))))*(1.0/16.0)

def level_map(i,segr_ref):
    t=lax.broadcasted_iota(jnp.int32,(C,C),0); s=lax.broadcasted_iota(jnp.int32,(C,C),1)
    segr=segr_ref[i].astype(F32)
    prev=jnp.where(i==0,-1.0,segr_ref[jnp.maximum(i-1,0)][:,C-1:C].astype(F32))
    segc=jnp.sum(jnp.where(t==s,segr,0.0),axis=1,keepdims=True)
    before=jnp.sum(jnp.where(t==s+1,segr,0.0),axis=1,keepdims=True)
    first=lax.broadcasted_iota(jnp.int32,(C,1),0)==0
    start=jnp.where(first,prev,before)!=segc
    last=segr[:,C-1:C]
    lv=jnp.where(segc==segr,t^s,-1)
    return lv,t,s,(segc==prev).astype(F32),(segc==last).astype(F32),(prev==last).astype(F32),start

def fwd_chunk(i,q_ref,k_ref,v_ref,g_ref,r_ref,wh_ref,bias_ref,gain_ref,segr_ref,m_ref,y_ref,o_ref,st_ref,state,esc):
    f=log_rate(gate_in(r_ref,wh_ref,bias_ref)).astype(BF)
    esc[...]=jnp.exp(dot(m_ref[...],f))
    lv,t,s,keep,tail,stay,start=level_map(i,segr_ref)
    lv=jnp.where(t>=s,lv,-1)
    row=lax.broadcasted_iota(jnp.int32,(C,KH),0)
    nl=len(LEVELS)
    for h in range(HEADS):
        ks=slice(h*KH,(h+1)*KH); vs=slice(h*VH,(h+1)*VH)
        q=q_ref[:,ks].astype(F32)*SCALE; k=k_ref[:,ks].astype(F32); v=v_ref[:,vs]
        a=jnp.where(lv==0,dot_nt(q.astype(BF),k_ref[:,ks]),0.0)
        for l,hs in enumerate(LEVELS):
            x=(jnp.where((row&hs)!=0,q,k)*esc[l*C:(l+1)*C,ks]).astype(BF)
            a=jnp.where((lv>=hs)&(lv<2*hs),dot_nt(x,x),a)
        ec=esc[nl*C:(nl+1)*C,ks]; es=esc[(nl+1)*C:(nl+2)*C,ks]
        st=state[h]
        stb=st.astype(BF)
        st_ref[0,h]=stb
        o=dot(a.astype(BF),v)+dot_nt((q*ec*keep).astype(BF),stb)
        state[h]=st*(ec[C-1:C,:]*stay)+dot_tn(v,(k*es*tail).astype(BF))
        o_ref[:,vs]=o.astype(BF)
        m=lax.rsqrt(jnp.mean(o*o,axis=-1,keepdims=True)+1.0)
        g=g_ref[:,vs].astype(F32)
        y_ref[:,vs]=(o*m*gain_ref[...]*(g*jax.nn.sigmoid(g))).astype(BF)

def bwd_chunk(i,q_ref,k_ref,v_ref,g_ref,r_ref,o_ref,st_ref,dy_ref,wh_ref,bias_ref,gain_ref,segr_ref,m_ref,
             dq_ref,dk_ref,dv_ref,dg_ref,dz_ref,gb_ref,gg_ref,dstate,rcar,esc,dcs):
    zb=gate_in(r_ref,wh_ref,bias_ref)
    f=log_rate(zb).astype(BF)
    esc[...]=jnp.exp(dot(m_ref[...],f))
    lv,t,s,keep,tail,stay,start=level_map(i,segr_ref)
    lvu=jnp.where(t<=s,lv,-1)
    lower=t>=s
    row=lax.broadcasted_iota(jnp.int32,(C,KH),0)
    nl=len(LEVELS)
    gain=gain_ref[...]
    ggacc=jnp.zeros((1,VH),F32)
    for h in range(HEADS):
        ks=slice(h*KH,(h+1)*KH); vs=slice(h*VH,(h+1)*VH)
        o=o_ref[:,vs].astype(F32); g=g_ref[:,vs].astype(F32); dy=dy_ref[:,vs].astype(F32)
        m=lax.rsqrt(jnp.mean(o*o,axis=-1,keepdims=True)+1.0)
        sg=jax.nn.sigmoid(g); om=o*m
        u=dy*(g*sg)
        dg_ref[:,vs]=(dy*om*gain*(sg*(1.0+g*(1.0-sg)))).astype(BF)
        ggacc=ggacc+jnp.sum(u*om,axis=0,keepdims=True)
        ug=u*gain
        do=(m*ug-om*(m*m)*jnp.mean(ug*o,axis=-1,keepdims=True)).astype(BF)
        q=q_ref[:,ks].astype(F32)*SCALE; k=k_ref[:,ks].astype(F32); v=v_ref[:,vs]
        qb=q.astype(BF); kb=k_ref[:,ks]
        das=jnp.where(lower,dot_nt(do,v),dot_nt(v,do))
        dd=jnp.sum(jnp.where(t==s,das,0.0),axis=1,keepdims=True)
        at=jnp.where(lvu==0,dot_nt(kb,qb),0.0)
        ec=esc[nl*C:(nl+1)*C,ks]; es=esc[(nl+1)*C:(nl+2)*C,ks]
        stb=st_ref[0,h]
        ds=dstate[h]; dsb=ds.astype(BF)
        qe=(q*ec*keep).astype(BF); ke=(k*es*tail).astype(BF)
        dq=dd*k+dot(do,stb)*(ec*keep)
        dk=dd*q+dot(v,dsb)*(es*tail)
        for l,hs in enumerate(LEVELS):
            e=esc[l*C:(l+1)*C,ks]
            sec=(row&hs)!=0
            x=(jnp.where(sec,q,k)*e).astype(BF)
            sx=dot_nt(x,x)
            at=jnp.where((lvu>=hs)&(lvu<2*hs),sx,at)
            gl=jnp.where((lv>=hs)&(lv<2*hs),das,0.0).astype(BF)
            tt=dot(gl,x)*e
            dq=dq+jnp.where(sec,tt,0.0)
            dk=dk+jnp.where(sec,0.0,tt)
        dv_ref[:,vs]=(dot(at.astype(BF),do)+dot_nt(ke,dsb)).astype(BF)
        dq_ref[:,ks]=(dq*SCALE).astype(BF)
        dk_ref[:,ks]=dk.astype(BF)
        dsn=ds*(ec[C-1:C,:]*stay)+dot_tn(do,qe)
        dstate[h]=dsn
        dc=q*dq-k*dk
        hi=dc.astype(BF)
        dcs[:,ks]=hi; dcs[:,HEADS*KH+h*KH:HEADS*KH+(h+1)*KH]=(dc-hi.astype(F32)).astype(BF)
        rold=rcar[:,ks]
        rcar[:,ks]=jnp.sum(stb.astype(F32)*dsn,axis=0,keepdims=True)
        dcs2=rold
        um=jnp.where((lv>=0)&(t<=s),1.0,0.0).astype(BF)
        df=dot(um,dcs[:,ks])+dot(um,dcs[:,HEADS*KH+h*KH:HEADS*KH+(h+1)*KH])+tail*dcs2
        dp=jnp.where(start,0.0,df)*(jax.nn.sigmoid(-zb[:,ks])*(1.0/16.0))
        dz_ref[:,ks]=dp.astype(BF)
        gb_ref[:,ks]+=jnp.sum(dp,axis=0,keepdims=True)
    gg_ref[...]+=ggacc

def seg_rows(segments):
    b,l=segments.shape
    seg=segments if b==1 else segments+8*lax.broadcasted_iota(jnp.int32,(b,l),0)
    return seg.reshape(-1,1,C)


MESH = pl.DeviceIdType.MESH
TILE = 256
LEADS = (6, 3, 2)
EARLY = 3


class Place:
    def __init__(self, n, reps):
        self.n, self.z = n, reps // 2
        self.rep = lax.axis_index("rep")
        self.me = lax.axis_index("shard")
        self.core = lax.rem(self.rep, 2)
        self.chip = self.rep // 2
        self.sib = (self.rep + 1 - 2 * self.core, self.me)

    def peer(self, step):
        return lax.rem(self.me + step, self.n)

    def flip(self, bit):
        if bit == 1:
            return self.me + 1 - 2 * lax.rem(self.me, 2)
        return lax.rem(self.me + 2, 4)

    def first(self):
        return jnp.where(self.core == 0, self.flip(1), self.flip(2))

    def second(self):
        return jnp.where(self.core == 0, self.flip(2), self.flip(1))


def greet(ids):
    barrier = pltpu.get_barrier_semaphore()
    for d in ids:
        pl.semaphore_signal(barrier, inc=1, device_id=d, device_id_type=MESH)
    pl.semaphore_wait(barrier, len(ids))


def remote(src, dst, ssem, rsem, device):
    return pltpu.make_async_remote_copy(
        src_ref=src, dst_ref=dst, send_sem=ssem, recv_sem=rsem, device_id=device, device_id_type=MESH
    )


def gather_sems(n, count):
    kinds = 2 * (n - 1) + 1
    return [pltpu.SemaphoreType.DMA((count, kinds)), pltpu.SemaphoreType.DMA((count, kinds))]


class Gather:
    def __init__(self, place, owns, fulls, sems):
        self.p, self.owns, self.fulls = place, owns, fulls
        self.ssem, self.rsem = sems

    def peers(self):
        p = self.p
        return [(p.rep, p.peer(j)) for j in range(1, p.n)] + [p.sib]

    def same(self, i):
        kind = 2 * (self.p.n - 1)
        return remote(
            self.owns[i], self.fulls[i].at[self.p.me], self.ssem[i].at[kind], self.rsem[i].at[kind], self.p.sib
        )

    def direct(self, i, kind, target):
        p = self.p
        return remote(
            self.owns[i].at[p.core],
            self.fulls[i].at[p.me, p.core],
            self.ssem[i].at[kind],
            self.rsem[i].at[kind],
            (p.rep, target),
        )

    def onward(self, i, kind, block, device):
        p = self.p
        view = self.fulls[i].at[block, p.core]
        return remote(view, view, self.ssem[i].at[kind], self.rsem[i].at[kind], device)

    def start(self, i):
        p = self.p
        if p.n == 4:
            self.direct(i, 0, p.first()).start()
            self.direct(i, 1, p.second()).start()
        else:
            for j in range(1, p.n):
                self.direct(i, j - 1, p.peer(j)).start()
        self.same(i).start()

    def blocks(self):
        p = self.p
        if p.n == 4:
            return [p.first(), p.second(), 3 - p.me]
        return [p.peer(p.n - j) for j in range(1, p.n)]

    def relay(self, i):
        p, blocks, last = self.p, self.blocks(), self.p.n - 1
        if p.n == 4:
            self.direct(i, 1, blocks[1]).wait_recv()
            self.onward(i, 2, blocks[1], (p.rep, blocks[0])).start()
            self.onward(i, last + 1, blocks[1], p.sib).start()
            self.direct(i, 0, blocks[0]).wait_recv()
            self.onward(i, last, blocks[0], p.sib).start()
        else:
            for j in range(last):
                self.direct(i, j, p.me).wait_recv()
                self.onward(i, last + j, blocks[j], p.sib).start()

    def pass_on(self, i):
        p, blocks, last = self.p, self.blocks(), self.p.n - 1
        if p.n == 4:
            self.onward(i, 2, blocks[2], (p.rep, blocks[0])).wait_recv()
            self.onward(i, last + 2, blocks[2], p.sib).start()

    def done(self, i):
        p, blocks, last = self.p, self.blocks(), self.p.n - 1
        self.same(i).wait()
        for j in range(last):
            self.direct(i, j, p.me).wait_send()
            arrival = self.onward(i, last + j, blocks[j], p.sib)
            arrival.wait_send()
            arrival.wait_recv()


def halves(w):
    return w.reshape(2, w.shape[0] // 2, w.shape[1])


def add_rows(dst, a, b):
    rows = dst.shape[0]
    slab = 32 if rows % 32 == 0 else 16

    def step(j, _):
        at = pl.ds(pl.multiple_of(j * slab, slab), slab)
        dst[at, :] = a[at, :] + b[at, :]
        return 0

    lax.fori_loop(0, rows // slab, step, 0)


class Reduce:
    STAGES = 7

    def __init__(self, place, out, bufs, sems, mine=None, give=None, part=None):
        self.p, self.out = place, out
        self.part = part
        self.square = place.n == 4
        self.line = place.z == 4
        bufs = list(bufs)
        if part is not None:
            mine, give = bufs.pop(0), part.at[:, 1 - place.core]
        self.mine, self.give = mine, give
        self.other, self.group, self.ring = bufs
        self.own = mine.at[place.me]
        self.rest = mine.at[place.second()] if self.square else None
        self.ssem, self.rsem, self.lsem = sems
        self.zbase = place.n
        self.end = self.zbase + (3 if self.line else place.z - 1)
        self.total = self.ring.at[2] if self.line else self.group.at[0]

    def copy(self, kind, src, dst, device):
        return remote(src, dst, self.ssem.at[kind], self.rsem.at[kind], device)

    def load(self):
        return pltpu.make_async_copy(self.part.at[:, self.p.core], self.mine, self.lsem.at[0])

    def swap(self):
        return self.copy(0, self.give, self.other, self.p.sib)

    def start(self):
        self.swap().start()
        if self.part is not None:
            self.load().start()

    def group_sends(self):
        p = self.p
        if self.square:
            to = (p.rep, p.first())
            return [
                self.copy(1, self.mine.at[p.first()], self.group.at[0], to),
                self.copy(2, self.mine.at[3 - p.me], self.group.at[1], to),
            ]
        return [
            self.copy(j, self.mine.at[p.peer(j)], self.group.at[j - 1], (p.rep, p.peer(j))) for j in range(1, p.n)
        ]

    def second_send(self):
        p = self.p
        return self.copy(3, self.rest, self.group.at[2], (p.rep, p.second()))

    def line_send(self, step):
        p = self.p
        if step == 0:
            to = jnp.where(p.chip == 0, p.rep + 2, p.rep - 2)
            return self.copy(self.zbase, self.own, self.ring.at[0], (to, p.me))
        if step == 1:
            to = jnp.where(p.chip == 1, p.rep + 2, p.rep - 2)
            return self.copy(self.zbase + 1, self.own, self.ring.at[1], (to, p.me))
        to = jnp.where(p.chip == 1, p.rep - 2, p.rep + 2)
        return self.copy(self.zbase + 2, self.total, self.total, (to, p.me))

    def ring_sends(self):
        p = self.p
        return [
            self.copy(self.zbase + j - 1, self.own, self.ring.at[p.chip], (lax.rem(p.rep + 2 * j, 2 * p.z), p.me))
            for j in range(1, p.z)
        ]

    def last_swaps(self):
        return [
            self.copy(self.end + j, self.total.at[:, lanes], half(self.p.core), self.p.sib)
            for j, (half, lanes) in enumerate(self.out)
        ]

    def stores(self):
        return [
            pltpu.make_async_copy(self.total.at[:, lanes], half(self.p.core), self.lsem.at[2 + j])
            for j, (half, lanes) in enumerate(self.out)
        ]

    def stage(self, k):
        p = self.p
        outer = (p.chip == 0) | (p.chip == 3)
        if k == 0:
            if self.part is not None:
                self.load().wait()
            self.swap().wait_recv()
            for b in range(p.n):
                add_rows(self.mine.at[b], self.mine.at[b], self.other.at[b])
            for c in self.group_sends():
                c.start()
        elif k == 1:
            for c in self.group_sends():
                c.wait_recv()
            add_rows(self.own, self.own, self.group.at[0])
            if self.square:
                add_rows(self.rest, self.rest, self.group.at[1])
                self.second_send().start()
            else:
                for j in range(1, p.n - 1):
                    add_rows(self.own, self.own, self.group.at[j])
        elif k == 2:
            if self.square:
                self.second_send().wait_recv()
                add_rows(self.own, self.own, self.group.at[2])
            if self.line:

                @pl.when(outer)
                def _():
                    self.line_send(0).start()

            else:
                for c in self.ring_sends():
                    c.start()
        elif k == 3:
            if self.line:

                @pl.when(jnp.logical_not(outer))
                def _():
                    self.line_send(0).wait_recv()
                    add_rows(self.own, self.own, self.ring.at[0])
                    self.line_send(1).start()

            else:
                for c in self.ring_sends():
                    c.wait_recv()
                self.ring[p.chip] = self.own[...]
                add_rows(self.total, self.ring.at[0], self.ring.at[1])
                for j in range(2, p.z):
                    add_rows(self.total, self.total, self.ring.at[j])
        elif k == 4:
            if self.line:

                @pl.when(jnp.logical_not(outer))
                def _():
                    self.line_send(1).wait_recv()
                    add_rows(self.total, self.own, self.ring.at[1])
                    self.line_send(2).start()

        elif k == 5:
            if self.line:

                @pl.when(outer)
                def _():
                    self.line_send(2).wait_recv()

            for c in self.last_swaps() + self.stores():
                c.start()
        else:
            for c in self.last_swaps():
                c.wait_recv()
            for c in self.stores():
                c.wait()

    def settle(self):
        p = self.p
        outer = (p.chip == 0) | (p.chip == 3)
        self.swap().wait_send()
        for c in self.group_sends():
            c.wait_send()
        if self.square:
            self.second_send().wait_send()
        if self.line:

            @pl.when(outer)
            def _():
                self.line_send(0).wait_send()

            @pl.when(jnp.logical_not(outer))
            def _():
                self.line_send(1).wait_send()
                self.line_send(2).wait_send()

        else:
            for c in self.ring_sends():
                c.wait_send()
        for c in self.last_swaps():
            c.wait_send()

    @staticmethod
    def peers(p):
        group = [(p.rep, p.peer(j)) for j in range(1, p.n)]
        along = [(lax.rem(p.rep + 2 * j, 2 * p.z), p.me) for j in range(1, p.z)]
        return group + along + [p.sib]

    @staticmethod
    def kinds(n, z):
        return n + (3 if z == 4 else z - 1) + 2

    @staticmethod
    def scratch(n, z, half, width, loaded, lead=()):
        lead = tuple(lead)
        kinds = Reduce.kinds(n, z)
        return ([pltpu.VMEM(lead + (n, half, width), BF)] if loaded else []) + [
            pltpu.VMEM(lead + (n, half, width), BF),
            pltpu.VMEM(lead + (n - 1, half, width), BF),
            pltpu.VMEM(lead + (3 if z == 4 else z, half, width), BF),
            pltpu.SemaphoreType.DMA(lead + (kinds,)),
            pltpu.SemaphoreType.DMA(lead + (kinds,)),
            pltpu.SemaphoreType.DMA(lead + (4,)),
        ]


class Small:
    def __init__(self, place, part, out, bufs, sems):
        self.p, self.part, self.out = place, part, out
        self.pair, self.other, self.group, self.ring = bufs
        self.ssem, self.rsem = sems

    def copy(self, kind, src, dst, device):
        return remote(src, dst, self.ssem.at[kind], self.rsem.at[kind], device)

    def swap(self):
        return self.copy(0, self.part, self.other, self.p.sib)

    def sends(self):
        p = self.p
        return [
            self.copy(j, self.pair.at[p.peer(j)], self.group.at[j - 1], (p.rep, p.peer(j))) for j in range(1, p.n)
        ]

    def along(self):
        p = self.p
        return [
            self.copy(p.n + j - 1, self.pair.at[p.me], self.ring.at[p.chip], (lax.rem(p.rep + 2 * j, 2 * p.z), p.me))
            for j in range(1, p.z)
        ]

    def stage(self, k):
        p = self.p
        if k == 0:
            self.swap().wait_recv()
            self.pair[...] = self.part[...] + self.other[...]
            for c in self.sends():
                c.start()
        elif k == 1:
            for c in self.sends():
                c.wait_recv()
            own = self.pair[p.me]
            for j in range(p.n - 1):
                own = own + self.group[j]
            self.pair[p.me] = own
            self.ring[p.chip] = own
            for c in self.along():
                c.start()
        else:
            for c in self.along():
                c.wait_recv()
            own = self.ring[0]
            for j in range(1, p.z):
                own = own + self.ring[j]
            self.out[...] = own

    def settle(self):
        self.swap().wait_send()
        for c in self.sends() + self.along():
            c.wait_send()

    @staticmethod
    def scratch(n, z, rows, width):
        return [
            pltpu.VMEM((n, rows, width), F32),
            pltpu.VMEM((n, rows, width), F32),
            pltpu.VMEM((n - 1, rows, width), F32),
            pltpu.VMEM((z, rows, width), F32),
            pltpu.SemaphoreType.DMA((n + z - 1,)),
            pltpu.SemaphoreType.DMA((n + z - 1,)),
        ]


def feed_kernel(n, reps, half, tile, *refs):
    b_ref, e_ref, x_ref, gain_ref, wd_ref = refs[:5]
    first, owns = refs[5:7], refs[7:9]
    res_out, dx_out, dm_out, norm_ref, down_out, gate_out, up_out, *late = refs[9:18]
    bt, acc, hid, dgate, dup, both, other, group, ring, ssem, rsem, lsem = refs[18:30]
    xs, res_ref, dx_ref, dm_ref, down_ref, moved, gsend, grecv, wbuf, wsem = refs[30:]
    step, tiles = pl.program_id(0), pl.num_programs(0) - 1
    p = Place(n, reps)
    total = b_ref.shape[0]
    tiles_count = down_out.shape[0] // tile
    rs = 2 * half
    rows_at = lambda j, size: pl.ds(pl.multiple_of(j * size, size), size)

    def fetch():
        return pltpu.make_async_copy(x_ref, xs, moved.at[0])

    def write(k, ref, out, rows):
        return pltpu.make_async_copy(ref.at[rows], out.at[rows], moved.at[k])

    def tile_gather(j):
        at = pl.ds(pl.multiple_of(j * tile, tile), tile)
        to = pl.ds(pl.multiple_of((j - EARLY) * tile, tile), tile)
        return Gather(
            p,
            [own.at[:, :, at] for own in owns],
            [full.at[:, :, :, to] for full in late],
            [[sem.at[j - EARLY, i] for i in range(2)] for sem in (gsend, grecv)],
        )

    def weights(j, begin):
        buf = lax.rem(j, 2)

        def one(source, at):
            for i in range(2):
                c = pltpu.make_async_copy(
                    source[i].at[:, :, :, pl.ds(pl.multiple_of(at * tile, tile), tile)], wbuf.at[buf, i], wsem.at[buf, i]
                )
                c.start() if begin else c.wait()

        @pl.when(j < EARLY)
        def _():
            one(first, j)

        @pl.when(j >= EARLY)
        def _():
            one(late, j - EARLY)

    def ahead(lead, run):
        if lead > EARLY:

            @pl.when(step == 0)
            def _():
                for j in range(EARLY, min(lead, tiles_count)):
                    for i in range(2):
                        run(tile_gather(j), i)

        @pl.when((step + lead >= EARLY) & (step + lead < tiles))
        def _():
            for i in range(2):
                run(tile_gather(step + lead), i)

    def item(j):
        cols = pl.ds(pl.multiple_of(j * tile, tile), tile)
        out = [
            (lambda c: gate_out.at[c, :, cols], pl.ds(0, tile)),
            (lambda c: up_out.at[c, :, cols], pl.ds(tile, tile)),
        ]
        return Reduce(
            p,
            out,
            [other.at[j], group.at[j], ring.at[j]],
            [ssem.at[j], rsem.at[j], lsem.at[j]],
            mine=both.at[j, 0],
            give=both.at[j, 1],
        )

    def slot(t):
        for k in range(Reduce.STAGES):

            lag = k + (k > 0)

            @pl.when((t >= lag) & (t - lag < tiles))
            def _():
                item(t - lag).stage(k)

    @pl.when(step == 0)
    def _():
        greet(Reduce.peers(p))
        fetch().start()
        weights(0, True)
        acc[...] = jnp.zeros_like(acc)
        dx_ref[...] = jnp.zeros_like(dx_ref)

        def turn(j, _):
            rows = rows_at(j, 128)
            bt[:, rows] = jnp.transpose(b_ref[rows, :])
            return 0

        lax.fori_loop(0, total // 128, turn, 0)

    @pl.when(step < tiles)
    def _():
        ahead(LEADS[0], lambda g, i: g.start(i))
        weights(step, False)
        wg = wbuf[lax.rem(step, 2), 0].reshape(-1, tile)
        wu = wbuf[lax.rem(step, 2), 1].reshape(-1, tile)

        def rows_step(j, _):
            rows = rows_at(j, 512)
            b, e = b_ref[rows, :], e_ref[rows, :]
            gate = dot(b, wg)
            up = dot(b, wu)
            dh = dot_nt(e, wd_ref[...])
            sig = jax.nn.sigmoid(gate)
            swish = gate * sig
            h = (swish * up).astype(BF)
            dg = (dh * up * (sig * (1.0 + gate * (1.0 - sig)))).astype(BF)
            du = (dh * swish).astype(BF)
            down_ref[rows_at(step, tile), rows] = jnp.transpose(h)
            hid[rows, :] = h
            dgate[rows, :] = dg
            dup[rows, :] = du
            return 0

        def sums_step(j, _):
            rows = rows_at(j, 512)
            acc[rows, :] += dot(hid[rows, :], wd_ref[...])
            dx_ref[rows, :] += dot_nt(dgate[rows, :], wg) + dot_nt(dup[rows, :], wu)
            return 0

        lax.fori_loop(0, total // 512, rows_step, 0, unroll=True)

        ahead(LEADS[1], lambda g, i: g.relay(i))
        ahead(LEADS[2], lambda g, i: g.pass_on(i))
        ahead(1, lambda g, i: g.done(i))

        @pl.when(step + 1 < tiles)
        def _():
            weights(step + 1, True)

        @pl.when(step > 0)
        def _():
            slot(step - 1)

        for at, d in ((0, dgate), (tile, dup)):
            w = dot(bt[...], d[...]).astype(BF)
            for s in range(n):
                both[step, p.core, s, :, at : at + tile] = w[s * rs : s * rs + half]
                both[step, 1 - p.core, s, :, at : at + tile] = w[s * rs + half : (s + 1) * rs]
        item(step).start()
        lax.fori_loop(0, total // 512, sums_step, 0, unroll=True)

    @pl.when(step == tiles)
    def _():
        norm_ref[...] = jnp.zeros_like(norm_ref)

        def finish(j, _):
            rows = rows_at(j, 128)
            x = xs[rows, :]
            res_ref[rows, :] = (x + acc[rows, :]).astype(BF)
            inv = lax.rsqrt(jnp.mean(x * x, axis=-1, keepdims=True) + 1e-5)
            xn = x * inv
            db = dx_ref[rows, :]
            norm_ref[...] += jnp.sum(db * xn, axis=0, keepdims=True)
            dbg = db * gain_ref[1:2, :]
            dx = e_ref[rows, :].astype(F32) + inv * (dbg - xn * jnp.mean(dbg * xn, axis=-1, keepdims=True))
            dx_ref[rows, :] = dx
            dm_ref[rows, :] = dx.astype(BF)
            return 0

        fetch().wait()

        def turn_down(j, _):
            slot(tiles - 1 + j)
            rows = rows_at(j, down_ref.shape[0] // 4)
            down_ref[rows, :] = dot(down_ref[rows, :], e_ref[...]).astype(BF)
            write(1 + j, down_ref, down_out, rows).start()
            return 0

        lax.fori_loop(0, 4, turn_down, 0)
        slot(tiles + 3)
        lax.fori_loop(0, total // 128, finish, 0)
        every = pl.ds(0, total)
        results = [
            write(5, res_ref, res_out, every),
            write(6, dx_ref, dx_out, every),
            write(7, dm_ref, dm_out, every),
        ]
        for c in results:
            c.start()

        def tail(t, _):
            slot(t)
            return 0

        lax.fori_loop(tiles + 4, tiles + Reduce.STAGES, tail, 0)

        def settle(j, _):
            item(j).settle()
            return 0

        lax.fori_loop(0, tiles, settle, 0)
        for j in range(4):
            write(1 + j, down_ref, down_out, rows_at(j, down_ref.shape[0] // 4)).wait()
        for c in results:
            c.wait()


def feed(n, reps, b, e, x2, gain, wd, first, owns):
    total, width = b.shape
    owns = [halves(w) for w in owns]
    ff = wd.shape[0]
    tile, z = TILE, reps // 2
    tiles, half = ff // tile, width // (2 * n)
    once = lambda *sh: pl.BlockSpec(sh, lambda j: (0,) * len(sh), pipeline_mode=pl.Buffered(1))
    row = lambda: pl.BlockSpec((tile, width), lambda j: (jnp.minimum(j, tiles - 1), 0))
    anywhere = pl.BlockSpec(memory_space=pl.ANY)
    sd = jax.ShapeDtypeStruct
    return pl.pallas_call(
        functools.partial(feed_kernel, n, reps, half, tile),
        grid=(tiles + 1,),
        in_specs=[once(total, width)] * 2 + [anywhere, once(8, width), row()] + [anywhere] * 4,
        out_specs=[anywhere] * 3 + [once(1, width)] + [anywhere] * 5,
        out_shape=[
            sd((total, width), BF),
            sd((total, width), F32),
            sd((total, width), BF),
            sd((1, width), F32),
            sd((ff, total), BF),
            sd((2, half, ff), BF),
            sd((2, half, ff), BF),
            sd((n, 2, half, ff - EARLY * tile), BF),
            sd((n, 2, half, ff - EARLY * tile), BF),
        ],
        scratch_shapes=[
            pltpu.VMEM((width, total), BF),
            pltpu.VMEM((total, width), F32),
            pltpu.VMEM((total, tile), BF),
            pltpu.VMEM((total, tile), BF),
            pltpu.VMEM((total, tile), BF),
            pltpu.VMEM((tiles, 2, n, half, 2 * tile), BF),
        ]
        + Reduce.scratch(n, z, half, 2 * tile, False, (tiles,))
        + [
            pltpu.VMEM((total, width), F32),
            pltpu.VMEM((total, width), BF),
            pltpu.VMEM((total, width), F32),
            pltpu.VMEM((total, width), BF),
            pltpu.VMEM((ff, total), BF),
            pltpu.SemaphoreType.DMA((8,)),
            pltpu.SemaphoreType.DMA((tiles - EARLY, 2, 2 * (n - 1) + 1)),
            pltpu.SemaphoreType.DMA((tiles - EARLY, 2, 2 * (n - 1) + 1)),
            pltpu.VMEM((2, 2, n, 2, half, tile), BF),
            pltpu.SemaphoreType.DMA((2, 2)),
        ],
        compiler_params=pltpu.CompilerParams(collective_id=1, has_side_effects=True, vmem_limit_bytes=63 << 20),
        name="feed_forward",
    )(b, e, x2, gain, wd, *first, *owns)[:7]


def forward_kernel(n, reps, width, *refs):
    x_ref, segr_ref, m_ref, vec_ref, high_ref, low_ref = refs[:6]
    owns = refs[6:14]
    a_ref, q_ref, k_ref, v_ref, g_ref, r_ref, y_ref, o_ref, st_ref = refs[14:23]
    x2_ref, b_ref, vec_out, high_out, low_out = refs[23:28]
    outs = refs[28:36]
    state, esc, xs, ys, vecs, highs, lows = refs[36:43]
    kept = refs[43:48]
    small_send, small_recv, ssem, rsem, lsem = refs[48:]
    step, nc = pl.program_id(0), pl.num_programs(0) - 1
    p = Place(n, reps)
    early = outs[6].shape[3]
    owns = list(owns[:6]) + [own.at[:, :, 0:early] for own in owns[6:]]
    gather = Gather(
        p, owns, list(kept) + list(outs[5:]), [[sem.at[i] for i in range(8)] for sem in (ssem, rsem)]
    )
    smalls = [(vec_ref, vecs), (high_ref, highs), (low_ref, lows)]

    def small(k, j):
        src, dst = smalls[k]
        return remote(src, dst.at[p.me], small_send.at[k, j - 1], small_recv.at[k, j - 1], (p.rep, p.peer(j)))

    def keep(i):
        return pltpu.make_async_copy(kept[i], outs[i], lsem.at[i])

    def whole(i):
        w = kept[i][...]
        return w.reshape(-1, w.shape[-1])

    @pl.when(step == 0)
    def _():
        greet(gather.peers())
        for i in range(4):
            gather.start(i)
        for k in range(3):
            for j in range(1, n):
                small(k, j).start()
            src, dst = smalls[k]
            dst[p.me] = src[...]
        for i in range(4):
            gather.relay(i)
        for i in range(4, 8):
            gather.start(i)
        for k in range(3):
            for j in range(1, n):
                small(k, j).wait()
        rs = low_ref.shape[1]
        for s in range(n):
            at = slice(s * rs, (s + 1) * rs)
            vec_out[0:1, at] = vecs[s, :, 0:rs]
            vec_out[1:2, at] = vecs[s, :, rs : 2 * rs]
            low_out[:, at] = lows[s]

        def spread(part, out_width):
            own = part(0).shape[1]
            total = None
            for s in range(n):
                col = lax.broadcasted_iota(jnp.int32, (own, out_width), 1)
                row = lax.broadcasted_iota(jnp.int32, (own, out_width), 0)
                piece = dot(part(s), (col == row + s * own).astype(F32).astype(BF))
                total = piece if total is None else total + piece
            return total

        nb, ng = 512 // n, VH // n
        vec_out[2:3, 0:512] = spread(lambda s: vecs[s, :, 2 * rs : 2 * rs + nb].astype(BF), 512)
        vec_out[3:4, 0:VH] = spread(lambda s: vecs[s, :, -128:][:, 0:ng].astype(BF), VH)
        high_out[...] = spread(lambda s: highs[s], 512).astype(BF)
        for i in range(4):
            gather.pass_on(i)
        for i in range(4):
            gather.done(i)
            keep(i).start()
        state[...] = jnp.zeros_like(state)

    @pl.when(step < nc)
    def _():
        rows = pl.ds(pl.multiple_of(step * C, C), C)
        xb = x_ref[...]
        xs[rows, :] = xb
        x = xb.astype(F32)
        inv = lax.rsqrt(jnp.mean(x * x, axis=-1, keepdims=True) + 1e-5)
        a = (x * inv * vec_out[0:1, :]).astype(BF)
        a_ref[...] = a
        q_ref[...] = dot(a, whole(0)).astype(BF)
        k_ref[...] = dot(a, whole(1)).astype(BF)
        v_ref[...] = dot(a, whole(2)).astype(BF)
        g_ref[...] = dot(a, whole(3)).astype(BF)
        r_ref[...] = dot_nt(a, low_out[...]).astype(BF)
        fwd_chunk(
            step, q_ref, k_ref, v_ref, g_ref, r_ref, high_out, vec_out.at[2:3, 0:512], vec_out.at[3:4, 0:VH],
            segr_ref, m_ref, y_ref, o_ref, st_ref, state, esc,
        )
        ys[rows, :] = y_ref[...]

    for at, run in (
        (1, lambda: gather.relay(4)),
        (3, lambda: gather.pass_on(4)),
        (4, lambda: gather.relay(5)),
        (5, lambda: gather.relay(6)),
        (6, lambda: gather.relay(7)),
        (7, lambda: gather.pass_on(5)),
    ):
        pl.when(step == at)(run)

    @pl.when(step == nc)
    def _():
        gather.done(4)
        keep(4).start()

        def join(j, _):
            rows = pl.ds(pl.multiple_of(j * 256, 256), 256)
            x2 = xs[rows, :].astype(F32) + dot(ys[rows, :], whole(4))
            x2_ref[rows, :] = x2
            inv = lax.rsqrt(jnp.mean(x2 * x2, axis=-1, keepdims=True) + 1e-5)
            b_ref[rows, :] = (x2 * inv * vec_out[1:2, :]).astype(BF)
            return 0

        lax.fori_loop(0, xs.shape[0] // 256, join, 0)
        gather.pass_on(6)
        gather.pass_on(7)
        for i in range(5, 8):
            gather.done(i)
        for i in range(5):
            keep(i).wait()


def forward(n, reps, x, segr, vec, high, low, weights):
    T, width = x.shape
    nc = T // C
    M = jnp.asarray(level_sums(), BF)
    nr = M.shape[0]
    owns = [halves(w) for w in weights]
    last = lambda i: jnp.minimum(i, nc - 1)
    blk = lambda w: pl.BlockSpec((C, w), lambda i: (last(i), 0))
    full = lambda *sh: pl.BlockSpec(sh, lambda i: (0,) * len(sh), pipeline_mode=pl.Buffered(1))
    anywhere = pl.BlockSpec(memory_space=pl.ANY)
    sd = jax.ShapeDtypeStruct
    shapes = [(n,) + o.shape for o in owns[:6]] + [(n,) + o.shape[:2] + (EARLY * TILE,) for o in owns[6:]]
    kinds = 2 * (n - 1) + 1
    res = pl.pallas_call(
        functools.partial(forward_kernel, n, reps, width),
        grid=(nc + 1,),
        in_specs=[blk(width), full(nc, 1, C), full(nr, C), full(*vec.shape), full(*high.shape), full(*low.shape)]
        + [anywhere] * 8,
        out_specs=[blk(w) for w in (width, 512, 512, 1024, 1024, 16, 1024, 1024)]
        + [pl.BlockSpec((1, HEADS, VH, KH), lambda i: (last(i), 0, 0, 0))]
        + [full(T, width), full(T, width), full(8, width), full(16, 512), full(16, width)]
        + [anywhere] * 8,
        out_shape=[sd((T, w), BF) for w in (width, 512, 512, 1024, 1024, 16, 1024, 1024)]
        + [
            sd((nc, HEADS, VH, KH), BF),
            sd((T, width), F32),
            sd((T, width), BF),
            sd((8, width), F32),
            sd((16, 512), BF),
            sd((16, width), BF),
        ]
        + [sd(shape, BF) for shape in shapes],
        scratch_shapes=[
            pltpu.VMEM((HEADS, VH, KH), F32),
            pltpu.VMEM((nr, 512), F32),
            pltpu.VMEM((T, width), BF),
            pltpu.VMEM((T, 1024), BF),
            pltpu.VMEM((n,) + vec.shape, F32),
            pltpu.VMEM((n,) + high.shape, BF),
            pltpu.VMEM((n,) + low.shape, BF),
        ]
        + [pltpu.VMEM(shape, BF) for shape in shapes[:5]]
        + [
            pltpu.SemaphoreType.DMA((3, n - 1)),
            pltpu.SemaphoreType.DMA((3, n - 1)),
            pltpu.SemaphoreType.DMA((8, kinds)),
            pltpu.SemaphoreType.DMA((8, kinds)),
            pltpu.SemaphoreType.DMA((5,)),
        ],
        compiler_params=pltpu.CompilerParams(collective_id=0, has_side_effects=True, vmem_limit_bytes=60 << 20),
        name="gla_fwd_gather",
    )(x, segr, M, vec, high, low, *owns)
    return res[:14], [o.reshape(-1, o.shape[-1]) for o in res[14:20]] + list(res[20:])


def backward_kernel(n,reps,plan,half,*refs):
    (q_ref,k_ref,v_ref,g_ref,r_ref,o_ref,st_ref,dy_ref,a_ref,x_ref,dx_ref,
     wh_ref,vec_ref,nmlp_ref,segr_ref,m_ref,*w_any,wl_ref)=refs[:21]
    bias_ref,gain_ref=vec_ref.at[2:3,0:512],vec_ref.at[3:4,0:VH]
    parts=refs[21:23]
    gt_ref,small_ref=refs[23:25]
    outs=refs[25:31]
    dstate,rcar,esc,dcs,dall,at_ref,dz_ref,low_acc,high_acc,gb_ref,gg_ref,smb,both,drs,*w_kept,w_sem=refs[31:50]
    rest=refs[50:]
    step=pl.program_id(0); nc=(pl.num_programs(0)-1)//2
    p=Place(n,reps)
    items=[]
    for which,at,width,source in plan:
        count=7 if source is None else 6
        mem,rest=rest[:count],rest[count:]
        cols=pl.ds(at,width)
        out=[(lambda c,which=which,cols=cols: outs[which].at[c,:,cols],pl.ds(0,width))]
        if source is None:
            items.append(Reduce(p,out,mem[:4],mem[4:],part=parts[which].at[:,:,:,cols]))
        else:
            cols=pl.ds(source,width)
            items.append(Reduce(p,out,mem[:3],mem[3:],mine=both.at[0,:,:,cols],give=both.at[1,:,:,cols]))
    mem=rest
    small=Small(p,smb,small_ref,mem[:4],mem[4:])
    ready=[it for it in items if it.part is not None]
    fresh=[it for it in items if it.part is None]

    plan_at={}
    def book(it,times):
        for stage,t in enumerate(times): plan_at.setdefault(t,[]).append((stage,it))
    for j,it in enumerate(ready): book(it,(j//2,2+j,4+j,6+j,7+j,8+j,9+j))
    for j,it in enumerate(fresh): book(it,[8+j+s for s in range(Reduce.STAGES)])
    last=max(plan_at)+1

    def slot(t):
        for stage,it in sorted(plan_at.get(t,[]),key=lambda pair: pair[0]): it.stage(stage)

    def weight(j):
        return pltpu.make_async_copy(w_any[j],w_kept[j],w_sem.at[j])

    @pl.when(step==0)
    def _():
        greet(Reduce.peers(p))
        for j in range(4): weight(j).start()
        for it in ready: it.start()
        for ref in (dstate,rcar,gb_ref,gg_ref,low_acc,high_acc,smb): ref[...]=jnp.zeros_like(ref)

    @pl.when(step<nc)
    def _():
        i=nc-1-step
        rows=pl.ds(pl.multiple_of(i*C,C),C)
        bwd_chunk(i,q_ref,k_ref,v_ref,g_ref,r_ref,o_ref,st_ref,dy_ref,wh_ref,bias_ref,gain_ref,segr_ref,m_ref,
                  dall.at[rows,0:512],dall.at[rows,512:1024],dall.at[rows,1024:2048],dall.at[rows,2048:3072],dz_ref,gb_ref,gg_ref,dstate,rcar,esc,dcs)
        dz=dz_ref[...]; a=a_ref[...]
        dr=dot_nt(dz,wh_ref[...]).astype(BF)
        drs[rows,:]=dr
        high_acc[...]+=dot_tn(r_ref[...],dz)
        low_acc[...]+=dot_tn(dr,a)
        at_ref[:,rows]=jnp.transpose(a)

    @pl.when(step>nc)
    def _():
        rows=pl.ds(pl.multiple_of((step-nc-1)*C,C),C)
        da=dot_nt(dall[rows,0:512],w_kept[0][...])+dot_nt(dall[rows,512:1024],w_kept[1][...])
        da=da+dot_nt(dall[rows,1024:2048],w_kept[2][...])+dot_nt(dall[rows,2048:3072],w_kept[3][...])+dot(drs[rows,:],wl_ref[...])
        x=x_ref[...].astype(F32)
        n1=lax.rsqrt(jnp.mean(x*x,axis=-1,keepdims=True)+1e-5)
        xn=x*n1
        dm=da*vec_ref[0:1,:]
        gt_ref[...]=dx_ref[...]+n1*(dm-xn*jnp.mean(dm*xn,axis=-1,keepdims=True))

    for t in range(8):
        @pl.when(step==t)
        def _(): slot(t)

    rs=2*half

    @pl.when(step==nc)
    def _():
        def product(at,width):
            cols=slice(at,at+width)
            w=dot(at_ref[...],dall[:,cols]).astype(BF)
            for s in range(n):
                both[p.core,s,:,cols]=w[s*rs:s*rs+half]
                both[1-p.core,s,:,cols]=w[s*rs+half:(s+1)*rs]

        smb[:,16:32,:]=jnp.broadcast_to(high_acc[...][None],(n,16,512))
        smb[:,32:33,:]=jnp.broadcast_to(gb_ref[...][None],(n,1,512))
        smb[:,33:34,0:256]=jnp.broadcast_to(gg_ref[...][None],(n,1,256))
        for s in range(n):
            at=slice(s*rs,(s+1)*rs)
            smb[s,0:16,0:rs]=low_acc[:,at]
            smb[s,35:36,0:rs]=nmlp_ref[:,at]
        for j,at in enumerate((2048,2560,1024,1536,0,512)):
            product(at,512)
            fresh[j].start()
            if j==1: small.swap().start()
            if j%2==1: slot(8+j//2)
            if j==5: small.stage(0)
        for j in range(4): weight(j).wait()

    for t in range(11,19):
        @pl.when(step==t-11+nc+1)
        def _():
            slot(t)
            if t in (13,16): small.stage((t-10)//3)

    @pl.when(step==2*nc)
    def _():
        for t in range(19,last): slot(t)
        for it in items: it.settle()
        small.settle()

def backward(n,reps,q,k,v,g,r,o,st,dy,first,tokens,dx2,wh,vecs,nmlp,segr,weights,partials):
    T=q.shape[0]; nc=T//C; z=reps//2
    assert nc==8
    M=jnp.asarray(level_sums(),BF); nr=M.shape[0]
    blk=lambda w: pl.BlockSpec((C,w),lambda i:(jnp.maximum(nc-1-i,0),0))
    late=lambda w: pl.BlockSpec((C,w),lambda i:(jnp.clip(i-nc-1,0,nc-1),0))
    full=lambda *sh: pl.BlockSpec(sh,lambda i:(0,)*len(sh),pipeline_mode=pl.Buffered(1))
    sd=jax.ShapeDtypeStruct
    anywhere=pl.BlockSpec(memory_space=pl.ANY)
    half=first.shape[1]//(2*n)
    pairs=[q.reshape(n,2,q.shape[0]//(2*n),q.shape[1]) for q in partials]
    plan,scratch=[],[]
    for which,(pair,cut) in enumerate(zip(pairs,(4,2))):
        tiles=pair.shape[3]//128
        edges=[128*(tiles*j//cut) for j in range(cut+1)]
        for at,end in zip(edges[:-1],edges[1:]):
            plan.append((which,at,end-at,None)); scratch+=Reduce.scratch(n,z,pair.shape[2],end-at,True)
    for which,at,width,source in ((5,0,512,2048),(5,512,512,2560),(4,0,512,1024),(4,512,512,1536),(2,0,512,0),(3,0,512,512)):
        plan.append((which,at,width,source)); scratch+=Reduce.scratch(n,z,half,width,False)
    scratch+=Small.scratch(n,z,40,512)
    out=lambda h,w: sd((2,h,w),BF)
    res=pl.pallas_call(functools.partial(backward_kernel,n,reps,tuple(plan),half),grid=(2*nc+1,),
        in_specs=[blk(512),blk(512),blk(1024),blk(1024),blk(16),blk(1024),pl.BlockSpec((1,HEADS,VH,KH),lambda i:(jnp.maximum(nc-1-i,0),0,0,0)),blk(1024),
                  blk(1024),late(1024),late(1024),
                  full(16,512),full(8,1024),full(1,1024),full(nc,1,C),full(nr,C),
                  anywhere,anywhere,anywhere,anywhere,full(16,1024)]+[anywhere]*2,
        out_specs=[late(1024),pl.BlockSpec((40,512),lambda i:(0,0))]+[anywhere]*6,
        out_shape=[sd((T,1024),F32),sd((40,512),F32)]+[out(q.shape[2],q.shape[3]) for q in pairs]+[out(half,512),out(half,512),out(half,1024),out(half,1024)],
        scratch_shapes=[pltpu.VMEM((HEADS,VH,KH),F32),pltpu.VMEM((1,512),F32),pltpu.VMEM((nr,512),F32),pltpu.VMEM((C,1024),BF),
                        pltpu.VMEM((T,3072),BF),pltpu.VMEM((1024,T),BF),pltpu.VMEM((C,512),BF),pltpu.VMEM((16,1024),F32),pltpu.VMEM((16,512),F32),
                        pltpu.VMEM((1,512),F32),pltpu.VMEM((1,256),F32),pltpu.VMEM((n,40,512),F32),
                        pltpu.VMEM((2,n,half,3072),BF),pltpu.VMEM((T,16),BF)]
                       +[pltpu.VMEM((1024,w),BF) for w in (512,512,1024,1024)]+[pltpu.SemaphoreType.DMA((4,))]+scratch,
        compiler_params=pltpu.CompilerParams(collective_id=2,has_side_effects=True,vmem_limit_bytes=63<<20),
        name="gla_bwd_reduce")(q,k,v,g,r,o,st,dy,first,tokens,dx2,wh,vecs,nmlp,segr,M,*weights,*pairs)
    return res[0],res[1],[x.reshape(-1,x.shape[2]) for x in res[2:]]


def matmul(left, right):
    return jnp.dot(left, right, preferred_element_type=F32)


def local(
    shards,
    reps,
    tokens,
    segments,
    cotangent,
    norm_mix,
    w_query,
    w_key,
    w_value,
    w_outgate,
    w_low,
    w_high,
    decay_bias,
    head_gain,
    w_out,
    norm_mlp,
    w_gate,
    w_up,
    w_down,
):
    total = tokens.shape[0] * tokens.shape[1]
    width = tokens.shape[2]
    segr = seg_rows(segments)
    pads = [-v.shape[0] % 128 for v in (decay_bias, head_gain)]
    zeros = [jnp.zeros((pad,), BF) for pad in pads]
    vec = jnp.concatenate([norm_mix, norm_mlp, decay_bias, zeros[0], head_gain, zeros[1]]).astype(F32)[None]
    (
        (first, query, keys, values, outgate, lowrank, mixed, heads, states, resid, second, vecs, high_w, low_w),
        (query_w, key_w, value_w, outgate_w, out_w, down_w, gate_w, up_w),
    ) = forward(
        shards,
        reps,
        tokens.reshape(total, width),
        segr,
        vec,
        w_high,
        w_low.T,
        (w_query, w_key, w_value, w_outgate, w_out, w_down, w_gate, w_up),
    )
    grad_out = cotangent.reshape(total, width)
    result, grad_resid, branch, part_norm_mlp, part_down, sum_gate, sum_up = feed(
        shards, reps, second, grad_out, resid, vecs, down_w, (gate_w, up_w), (w_gate, w_up)
    )
    part_out = dot_tn(mixed, branch)
    grad_mixed = dot_nt(branch, out_w).astype(BF)
    grad_inputs, small_sums, sums = backward(
        shards,
        reps,
        query,
        keys,
        values,
        outgate,
        lowrank,
        heads,
        states,
        grad_mixed,
        first,
        tokens.reshape(total, width),
        grad_resid,
        high_w,
        vecs,
        part_norm_mlp,
        segr,
        (query_w, key_w, value_w, outgate_w, low_w),
        (part_down, part_out.astype(BF)),
    )
    sum_gate, sum_up = [s.reshape(-1, s.shape[2]).astype(F32) for s in (sum_gate, sum_up)]
    sum_down, sum_out, sum_query, sum_key, sum_value, sum_outgate = [s.astype(F32) for s in sums]
    me = lax.axis_index("shard")
    rs = w_low.shape[0]

    def across(block, width):
        return lax.dynamic_slice_in_dim(block, me * width, width, axis=1)

    grad_low_w = small_sums[:16, :rs].T
    mixer = (
        (w_query, sum_query),
        (w_key, sum_key),
        (w_value, sum_value),
        (w_outgate, sum_outgate),
        (w_low, grad_low_w),
    )
    own = (
        sum(jnp.sum(w.astype(F32) * g, axis=1) for w, g in mixer) / norm_mix.astype(F32),
        small_sums[35, :rs],
        across(small_sums[32:33], decay_bias.shape[0]).reshape(-1),
        across(small_sums[33:34, :VH], head_gain.shape[0]).reshape(-1),
        grad_low_w,
        across(small_sums[16:32], w_high.shape[1]),
    )
    return (
        result.reshape(tokens.shape),
        grad_inputs.reshape(tokens.shape),
        own[0],
        sum_query,
        sum_key,
        sum_value,
        sum_outgate,
        own[4],
        own[5],
        own[2],
        own[3],
        sum_out,
        own[1],
        sum_gate,
        sum_up,
        sum_down,
    )


def solution(mesh):
    in_specs = (
        P(("rep", "shard"), None, None),
        P(("rep", "shard"), None),
        P(("rep", "shard"), None, None),
        P("shard"),
        P("shard", None),
        P("shard", None),
        P("shard", None),
        P("shard", None),
        P("shard", None),
        P(None, "shard"),
        P("shard"),
        P("shard"),
        P("shard", None),
        P("shard"),
        P("shard", None),
        P("shard", None),
        P("shard", None),
    )
    out_specs = (
        P(("rep", "shard"), None, None),
        P(("rep", "shard"), None, None),
        P("shard"),
        P("shard", None),
        P("shard", None),
        P("shard", None),
        P("shard", None),
        P("shard", None),
        P(None, "shard"),
        P("shard"),
        P("shard"),
        P("shard", None),
        P("shard"),
        P("shard", None),
        P("shard", None),
        P("shard", None),
    )
    return jax.shard_map(
        functools.partial(local, mesh.shape["shard"], mesh.shape["rep"]), mesh=mesh, in_specs=in_specs, out_specs=out_specs, check_vma=False)
```

```python
import functools
import numpy as np
import jax, jax.numpy as jnp
from jax import lax
from jax.experimental import pallas as pl
from jax.experimental.pallas import tpu as pltpu
from jax.sharding import PartitionSpec as P
HEADS=4; KH=128; VH=256; C=128
SCALE=KH**-0.5
LEVELS=(64,32,16,8,4,2,1)
F32=jnp.float32; BF=jnp.bfloat16

def level_sums():
    t=np.arange(C)[:,None]; u=np.arange(C)[None,:]
    rows=[]
    for h in LEVELS:
        ref=(t//(2*h))*(2*h)+h-1
        second=t>ref
        rows.append(np.where(second,(u>ref)&(u<=t),(u>t)&(u<=ref)))
    rows.append(u<=t); rows.append(u>t)
    return np.concatenate(rows,0).astype(np.float32)

def dot(a,b): return lax.dot_general(a,b,(((1,),(0,)),((),())),preferred_element_type=F32)
def dot_nt(a,b): return lax.dot_general(a,b,(((1,),(1,)),((),())),preferred_element_type=F32)
def dot_tn(a,b): return lax.dot_general(a,b,(((0,),(0,)),((),())),preferred_element_type=F32)

def gate_in(r_ref,wh_ref,bias_ref):
    return dot(r_ref[...],wh_ref[...])+bias_ref[...]

def log_rate(zb):
    return (jnp.minimum(zb,0.0)-jnp.log1p(jnp.exp(-jnp.abs(zb))))*(1.0/16.0)

def level_map(i,segr_ref):
    t=lax.broadcasted_iota(jnp.int32,(C,C),0); s=lax.broadcasted_iota(jnp.int32,(C,C),1)
    segr=segr_ref[i].astype(F32)
    prev=jnp.where(i==0,-1.0,segr_ref[jnp.maximum(i-1,0)][:,C-1:C].astype(F32))
    segc=jnp.sum(jnp.where(t==s,segr,0.0),axis=1,keepdims=True)
    before=jnp.sum(jnp.where(t==s+1,segr,0.0),axis=1,keepdims=True)
    first=lax.broadcasted_iota(jnp.int32,(C,1),0)==0
    start=jnp.where(first,prev,before)!=segc
    last=segr[:,C-1:C]
    lv=jnp.where(segc==segr,t^s,-1)
    return lv,t,s,(segc==prev).astype(F32),(segc==last).astype(F32),(prev==last).astype(F32),start

def fwd_chunk(i,q_ref,k_ref,v_ref,g_ref,r_ref,wh_ref,bias_ref,gain_ref,segr_ref,m_ref,y_ref,o_ref,st_ref,state,esc):
    f=log_rate(gate_in(r_ref,wh_ref,bias_ref)).astype(BF)
    esc[...]=jnp.exp(dot(m_ref[...],f))
    lv,t,s,keep,tail,stay,start=level_map(i,segr_ref)
    lv=jnp.where(t>=s,lv,-1)
    row=lax.broadcasted_iota(jnp.int32,(C,KH),0)
    nl=len(LEVELS)
    for h in range(HEADS):
        ks=slice(h*KH,(h+1)*KH); vs=slice(h*VH,(h+1)*VH)
        q=q_ref[:,ks].astype(F32)*SCALE; k=k_ref[:,ks].astype(F32); v=v_ref[:,vs]
        a=jnp.where(lv==0,dot_nt(q.astype(BF),k_ref[:,ks]),0.0)
        for l,hs in enumerate(LEVELS):
            x=(jnp.where((row&hs)!=0,q,k)*esc[l*C:(l+1)*C,ks]).astype(BF)
            a=jnp.where((lv>=hs)&(lv<2*hs),dot_nt(x,x),a)
        ec=esc[nl*C:(nl+1)*C,ks]; es=esc[(nl+1)*C:(nl+2)*C,ks]
        st=state[h]
        stb=st.astype(BF)
        st_ref[0,h]=stb
        o=dot(a.astype(BF),v)+dot_nt((q*ec*keep).astype(BF),stb)
        state[h]=st*(ec[C-1:C,:]*stay)+dot_tn(v,(k*es*tail).astype(BF))
        o_ref[:,vs]=o.astype(BF)
        m=lax.rsqrt(jnp.mean(o*o,axis=-1,keepdims=True)+1.0)
        g=g_ref[:,vs].astype(F32)
        y_ref[:,vs]=(o*m*gain_ref[...]*(g*jax.nn.sigmoid(g))).astype(BF)

def bwd_chunk(i,q_ref,k_ref,v_ref,g_ref,r_ref,o_ref,st_ref,dy_ref,wh_ref,bias_ref,gain_ref,segr_ref,m_ref,
             dq_ref,dk_ref,dv_ref,dg_ref,dz_ref,gb_ref,gg_ref,dstate,rcar,esc,dcs):
    zb=gate_in(r_ref,wh_ref,bias_ref)
    f=log_rate(zb).astype(BF)
    esc[...]=jnp.exp(dot(m_ref[...],f))
    lv,t,s,keep,tail,stay,start=level_map(i,segr_ref)
    lvu=jnp.where(t<=s,lv,-1)
    lower=t>=s
    row=lax.broadcasted_iota(jnp.int32,(C,KH),0)
    nl=len(LEVELS)
    gain=gain_ref[...]
    ggacc=jnp.zeros((1,VH),F32)
    for h in range(HEADS):
        ks=slice(h*KH,(h+1)*KH); vs=slice(h*VH,(h+1)*VH)
        o=o_ref[:,vs].astype(F32); g=g_ref[:,vs].astype(F32); dy=dy_ref[:,vs].astype(F32)
        m=lax.rsqrt(jnp.mean(o*o,axis=-1,keepdims=True)+1.0)
        sg=jax.nn.sigmoid(g); om=o*m
        u=dy*(g*sg)
        dg_ref[:,vs]=(dy*om*gain*(sg*(1.0+g*(1.0-sg)))).astype(BF)
        ggacc=ggacc+jnp.sum(u*om,axis=0,keepdims=True)
        ug=u*gain
        do=(m*ug-om*(m*m)*jnp.mean(ug*o,axis=-1,keepdims=True)).astype(BF)
        q=q_ref[:,ks].astype(F32)*SCALE; k=k_ref[:,ks].astype(F32); v=v_ref[:,vs]
        qb=q.astype(BF); kb=k_ref[:,ks]
        das=jnp.where(lower,dot_nt(do,v),dot_nt(v,do))
        dd=jnp.sum(jnp.where(t==s,das,0.0),axis=1,keepdims=True)
        at=jnp.where(lvu==0,dot_nt(kb,qb),0.0)
        ec=esc[nl*C:(nl+1)*C,ks]; es=esc[(nl+1)*C:(nl+2)*C,ks]
        stb=st_ref[0,h]
        ds=dstate[h]; dsb=ds.astype(BF)
        qe=(q*ec*keep).astype(BF); ke=(k*es*tail).astype(BF)
        dq=dd*k+dot(do,stb)*(ec*keep)
        dk=dd*q+dot(v,dsb)*(es*tail)
        for l,hs in enumerate(LEVELS):
            e=esc[l*C:(l+1)*C,ks]
            sec=(row&hs)!=0
            x=(jnp.where(sec,q,k)*e).astype(BF)
            sx=dot_nt(x,x)
            at=jnp.where((lvu>=hs)&(lvu<2*hs),sx,at)
            gl=jnp.where((lv>=hs)&(lv<2*hs),das,0.0).astype(BF)
            tt=dot(gl,x)*e
            dq=dq+jnp.where(sec,tt,0.0)
            dk=dk+jnp.where(sec,0.0,tt)
        dv_ref[:,vs]=(dot(at.astype(BF),do)+dot_nt(ke,dsb)).astype(BF)
        dq_ref[:,ks]=(dq*SCALE).astype(BF)
        dk_ref[:,ks]=dk.astype(BF)
        dsn=ds*(ec[C-1:C,:]*stay)+dot_tn(do,qe)
        dstate[h]=dsn
        dc=q*dq-k*dk
        hi=dc.astype(BF)
        dcs[:,ks]=hi; dcs[:,HEADS*KH+h*KH:HEADS*KH+(h+1)*KH]=(dc-hi.astype(F32)).astype(BF)
        rold=rcar[:,ks]
        rcar[:,ks]=jnp.sum(stb.astype(F32)*dsn,axis=0,keepdims=True)
        dcs2=rold
        um=jnp.where((lv>=0)&(t<=s),1.0,0.0).astype(BF)
        df=dot(um,dcs[:,ks])+dot(um,dcs[:,HEADS*KH+h*KH:HEADS*KH+(h+1)*KH])+tail*dcs2
        dp=jnp.where(start,0.0,df)*(jax.nn.sigmoid(-zb[:,ks])*(1.0/16.0))
        dz_ref[:,ks]=dp.astype(BF)
        gb_ref[:,ks]+=jnp.sum(dp,axis=0,keepdims=True)
    gg_ref[...]+=ggacc

def seg_rows(segments):
    b,l=segments.shape
    seg=segments if b==1 else segments+8*lax.broadcasted_iota(jnp.int32,(b,l),0)
    return seg.reshape(-1,1,C)


MESH = pl.DeviceIdType.MESH
TILE = 256
LEADS = (7, 3, 2)
EARLY = 4


class Place:
    def __init__(self, n, reps):
        self.n, self.z = n, reps // 2
        self.rep = lax.axis_index("rep")
        self.me = lax.axis_index("shard")
        self.core = lax.rem(self.rep, 2)
        self.chip = self.rep // 2
        self.sib = (self.rep + 1 - 2 * self.core, self.me)

    def peer(self, step):
        return lax.rem(self.me + step, self.n)

    def flip(self, bit):
        if bit == 1:
            return self.me + 1 - 2 * lax.rem(self.me, 2)
        return lax.rem(self.me + 2, 4)

    def first(self):
        return jnp.where(self.core == 0, self.flip(1), self.flip(2))

    def second(self):
        return jnp.where(self.core == 0, self.flip(2), self.flip(1))


def greet(ids):
    barrier = pltpu.get_barrier_semaphore()
    for d in ids:
        pl.semaphore_signal(barrier, inc=1, device_id=d, device_id_type=MESH)
    pl.semaphore_wait(barrier, len(ids))


def remote(src, dst, ssem, rsem, device):
    return pltpu.make_async_remote_copy(
        src_ref=src, dst_ref=dst, send_sem=ssem, recv_sem=rsem, device_id=device, device_id_type=MESH
    )


def gather_sems(n, count):
    kinds = 2 * (n - 1) + 1
    return [pltpu.SemaphoreType.DMA((count, kinds)), pltpu.SemaphoreType.DMA((count, kinds))]


class Gather:
    def __init__(self, place, owns, fulls, sems):
        self.p, self.owns, self.fulls = place, owns, fulls
        self.ssem, self.rsem = sems

    def peers(self):
        p = self.p
        return [(p.rep, p.peer(j)) for j in range(1, p.n)] + [p.sib]

    def same(self, i):
        kind = 2 * (self.p.n - 1)
        return remote(
            self.owns[i], self.fulls[i].at[self.p.me], self.ssem[i].at[kind], self.rsem[i].at[kind], self.p.sib
        )

    def direct(self, i, kind, target):
        p = self.p
        return remote(
            self.owns[i].at[p.core],
            self.fulls[i].at[p.me, p.core],
            self.ssem[i].at[kind],
            self.rsem[i].at[kind],
            (p.rep, target),
        )

    def onward(self, i, kind, block, device):
        p = self.p
        view = self.fulls[i].at[block, p.core]
        return remote(view, view, self.ssem[i].at[kind], self.rsem[i].at[kind], device)

    def start(self, i):
        p = self.p
        if p.n == 4:
            self.direct(i, 0, p.first()).start()
            self.direct(i, 1, p.second()).start()
        else:
            for j in range(1, p.n):
                self.direct(i, j - 1, p.peer(j)).start()
        self.same(i).start()

    def blocks(self):
        p = self.p
        if p.n == 4:
            return [p.first(), p.second(), 3 - p.me]
        return [p.peer(p.n - j) for j in range(1, p.n)]

    def relay(self, i):
        p, blocks, last = self.p, self.blocks(), self.p.n - 1
        if p.n == 4:
            self.direct(i, 1, blocks[1]).wait_recv()
            self.onward(i, 2, blocks[1], (p.rep, blocks[0])).start()
            self.onward(i, last + 1, blocks[1], p.sib).start()
            self.direct(i, 0, blocks[0]).wait_recv()
            self.onward(i, last, blocks[0], p.sib).start()
        else:
            for j in range(last):
                self.direct(i, j, p.me).wait_recv()
                self.onward(i, last + j, blocks[j], p.sib).start()

    def pass_on(self, i):
        p, blocks, last = self.p, self.blocks(), self.p.n - 1
        if p.n == 4:
            self.onward(i, 2, blocks[2], (p.rep, blocks[0])).wait_recv()
            self.onward(i, last + 2, blocks[2], p.sib).start()

    def done(self, i):
        p, blocks, last = self.p, self.blocks(), self.p.n - 1
        self.same(i).wait()
        for j in range(last):
            self.direct(i, j, p.me).wait_send()
            arrival = self.onward(i, last + j, blocks[j], p.sib)
            arrival.wait_send()
            arrival.wait_recv()


def halves(w):
    return w.reshape(2, w.shape[0] // 2, w.shape[1])


def add_rows(dst, a, b):
    rows = dst.shape[0]
    slab = 32 if rows % 32 == 0 else 16

    def step(j, _):
        at = pl.ds(pl.multiple_of(j * slab, slab), slab)
        dst[at, :] = a[at, :] + b[at, :]
        return 0

    lax.fori_loop(0, rows // slab, step, 0)


class Reduce:
    STAGES = 7

    def __init__(self, place, out, bufs, sems, mine=None, give=None, part=None):
        self.p, self.out = place, out
        self.part = part
        self.square = place.n == 4
        self.line = place.z == 4
        bufs = list(bufs)
        if part is not None:
            mine, give = bufs.pop(0), part.at[:, 1 - place.core]
        self.mine, self.give = mine, give
        self.other, self.group, self.ring = bufs
        self.own = mine.at[place.me]
        self.rest = mine.at[place.second()] if self.square else None
        self.ssem, self.rsem, self.lsem = sems
        self.zbase = place.n
        self.end = self.zbase + (3 if self.line else place.z - 1)
        self.total = self.ring.at[2] if self.line else self.group.at[0]

    def copy(self, kind, src, dst, device):
        return remote(src, dst, self.ssem.at[kind], self.rsem.at[kind], device)

    def load(self):
        return pltpu.make_async_copy(self.part.at[:, self.p.core], self.mine, self.lsem.at[0])

    def swap(self):
        return self.copy(0, self.give, self.other, self.p.sib)

    def start(self):
        self.swap().start()
        if self.part is not None:
            self.load().start()

    def group_sends(self):
        p = self.p
        if self.square:
            to = (p.rep, p.first())
            return [
                self.copy(1, self.mine.at[p.first()], self.group.at[0], to),
                self.copy(2, self.mine.at[3 - p.me], self.group.at[1], to),
            ]
        return [
            self.copy(j, self.mine.at[p.peer(j)], self.group.at[j - 1], (p.rep, p.peer(j))) for j in range(1, p.n)
        ]

    def second_send(self):
        p = self.p
        return self.copy(3, self.rest, self.group.at[2], (p.rep, p.second()))

    def line_send(self, step):
        p = self.p
        if step == 0:
            to = jnp.where(p.chip == 0, p.rep + 2, p.rep - 2)
            return self.copy(self.zbase, self.own, self.ring.at[0], (to, p.me))
        if step == 1:
            to = jnp.where(p.chip == 1, p.rep + 2, p.rep - 2)
            return self.copy(self.zbase + 1, self.own, self.ring.at[1], (to, p.me))
        to = jnp.where(p.chip == 1, p.rep - 2, p.rep + 2)
        return self.copy(self.zbase + 2, self.total, self.total, (to, p.me))

    def ring_sends(self):
        p = self.p
        return [
            self.copy(self.zbase + j - 1, self.own, self.ring.at[p.chip], (lax.rem(p.rep + 2 * j, 2 * p.z), p.me))
            for j in range(1, p.z)
        ]

    def last_swaps(self):
        return [
            self.copy(self.end + j, self.total.at[:, lanes], half(self.p.core), self.p.sib)
            for j, (half, lanes) in enumerate(self.out)
        ]

    def stores(self):
        return [
            pltpu.make_async_copy(self.total.at[:, lanes], half(self.p.core), self.lsem.at[2 + j])
            for j, (half, lanes) in enumerate(self.out)
        ]

    def stage(self, k):
        p = self.p
        outer = (p.chip == 0) | (p.chip == 3)
        if k == 0:
            if self.part is not None:
                self.load().wait()
            self.swap().wait_recv()
            for b in range(p.n):
                add_rows(self.mine.at[b], self.mine.at[b], self.other.at[b])
            for c in self.group_sends():
                c.start()
        elif k == 1:
            for c in self.group_sends():
                c.wait_recv()
            add_rows(self.own, self.own, self.group.at[0])
            if self.square:
                add_rows(self.rest, self.rest, self.group.at[1])
                self.second_send().start()
            else:
                for j in range(1, p.n - 1):
                    add_rows(self.own, self.own, self.group.at[j])
        elif k == 2:
            if self.square:
                self.second_send().wait_recv()
                add_rows(self.own, self.own, self.group.at[2])
            if self.line:

                @pl.when(outer)
                def _():
                    self.line_send(0).start()

            else:
                for c in self.ring_sends():
                    c.start()
        elif k == 3:
            if self.line:

                @pl.when(jnp.logical_not(outer))
                def _():
                    self.line_send(0).wait_recv()
                    add_rows(self.own, self.own, self.ring.at[0])
                    self.line_send(1).start()

            else:
                for c in self.ring_sends():
                    c.wait_recv()
                self.ring[p.chip] = self.own[...]
                add_rows(self.total, self.ring.at[0], self.ring.at[1])
                for j in range(2, p.z):
                    add_rows(self.total, self.total, self.ring.at[j])
        elif k == 4:
            if self.line:

                @pl.when(jnp.logical_not(outer))
                def _():
                    self.line_send(1).wait_recv()
                    add_rows(self.total, self.own, self.ring.at[1])
                    self.line_send(2).start()

        elif k == 5:
            if self.line:

                @pl.when(outer)
                def _():
                    self.line_send(2).wait_recv()

            for c in self.last_swaps() + self.stores():
                c.start()
        else:
            for c in self.last_swaps():
                c.wait_recv()
            for c in self.stores():
                c.wait()

    def settle(self):
        p = self.p
        outer = (p.chip == 0) | (p.chip == 3)
        self.swap().wait_send()
        for c in self.group_sends():
            c.wait_send()
        if self.square:
            self.second_send().wait_send()
        if self.line:

            @pl.when(outer)
            def _():
                self.line_send(0).wait_send()

            @pl.when(jnp.logical_not(outer))
            def _():
                self.line_send(1).wait_send()
                self.line_send(2).wait_send()

        else:
            for c in self.ring_sends():
                c.wait_send()
        for c in self.last_swaps():
            c.wait_send()

    @staticmethod
    def peers(p):
        group = [(p.rep, p.peer(j)) for j in range(1, p.n)]
        along = [(lax.rem(p.rep + 2 * j, 2 * p.z), p.me) for j in range(1, p.z)]
        return group + along + [p.sib]

    @staticmethod
    def kinds(n, z):
        return n + (3 if z == 4 else z - 1) + 2

    @staticmethod
    def scratch(n, z, half, width, loaded, lead=()):
        lead = tuple(lead)
        kinds = Reduce.kinds(n, z)
        return ([pltpu.VMEM(lead + (n, half, width), BF)] if loaded else []) + [
            pltpu.VMEM(lead + (n, half, width), BF),
            pltpu.VMEM(lead + (n - 1, half, width), BF),
            pltpu.VMEM(lead + (3 if z == 4 else z, half, width), BF),
            pltpu.SemaphoreType.DMA(lead + (kinds,)),
            pltpu.SemaphoreType.DMA(lead + (kinds,)),
            pltpu.SemaphoreType.DMA(lead + (4,)),
        ]


class Small:
    def __init__(self, place, part, out, bufs, sems):
        self.p, self.part, self.out = place, part, out
        self.pair, self.other, self.group, self.ring = bufs
        self.ssem, self.rsem = sems

    def copy(self, kind, src, dst, device):
        return remote(src, dst, self.ssem.at[kind], self.rsem.at[kind], device)

    def swap(self):
        return self.copy(0, self.part, self.other, self.p.sib)

    def sends(self):
        p = self.p
        return [
            self.copy(j, self.pair.at[p.peer(j)], self.group.at[j - 1], (p.rep, p.peer(j))) for j in range(1, p.n)
        ]

    def along(self):
        p = self.p
        return [
            self.copy(p.n + j - 1, self.pair.at[p.me], self.ring.at[p.chip], (lax.rem(p.rep + 2 * j, 2 * p.z), p.me))
            for j in range(1, p.z)
        ]

    def stage(self, k):
        p = self.p
        if k == 0:
            self.swap().wait_recv()
            self.pair[...] = self.part[...] + self.other[...]
            for c in self.sends():
                c.start()
        elif k == 1:
            for c in self.sends():
                c.wait_recv()
            own = self.pair[p.me]
            for j in range(p.n - 1):
                own = own + self.group[j]
            self.pair[p.me] = own
            self.ring[p.chip] = own
            for c in self.along():
                c.start()
        else:
            for c in self.along():
                c.wait_recv()
            own = self.ring[0]
            for j in range(1, p.z):
                own = own + self.ring[j]
            self.out[...] = own

    def settle(self):
        self.swap().wait_send()
        for c in self.sends() + self.along():
            c.wait_send()

    @staticmethod
    def scratch(n, z, rows, width):
        return [
            pltpu.VMEM((n, rows, width), F32),
            pltpu.VMEM((n, rows, width), F32),
            pltpu.VMEM((n - 1, rows, width), F32),
            pltpu.VMEM((z, rows, width), F32),
            pltpu.SemaphoreType.DMA((n + z - 1,)),
            pltpu.SemaphoreType.DMA((n + z - 1,)),
        ]


def feed_kernel(n, reps, half, tile, *refs):
    b_ref, e_ref, x_ref, gain_ref, wd_ref = refs[:5]
    first, owns = refs[5:7], refs[7:9]
    res_out, dx_out, dm_out, norm_ref, down_out, gate_out, up_out, *late = refs[9:18]
    bt, acc, hid, dgate, dup, both, other, group, ring, ssem, rsem, lsem = refs[18:30]
    xs, res_ref, dx_ref, dm_ref, down_ref, moved, gsend, grecv, wbuf, wsem = refs[30:]
    step, tiles = pl.program_id(0), pl.num_programs(0) - 1
    p = Place(n, reps)
    total = b_ref.shape[0]
    tiles_count = down_out.shape[0] // tile
    rs = 2 * half
    rows_at = lambda j, size: pl.ds(pl.multiple_of(j * size, size), size)

    def fetch():
        return pltpu.make_async_copy(x_ref, xs, moved.at[0])

    def write(k, ref, out, rows):
        return pltpu.make_async_copy(ref.at[rows], out.at[rows], moved.at[k])

    def tile_gather(j):
        at = pl.ds(pl.multiple_of(j * tile, tile), tile)
        to = pl.ds(pl.multiple_of((j - EARLY) * tile, tile), tile)
        return Gather(
            p,
            [own.at[:, :, at] for own in owns],
            [full.at[:, :, :, to] for full in late],
            [[sem.at[j - EARLY, i] for i in range(2)] for sem in (gsend, grecv)],
        )

    def weights(j, begin):
        buf = lax.rem(j, 2)

        def one(source, at):
            for i in range(2):
                c = pltpu.make_async_copy(
                    source[i].at[:, :, :, pl.ds(pl.multiple_of(at * tile, tile), tile)], wbuf.at[buf, i], wsem.at[buf, i]
                )
                c.start() if begin else c.wait()

        @pl.when(j < EARLY)
        def _():
            one(first, j)

        @pl.when(j >= EARLY)
        def _():
            one(late, j - EARLY)

    def ahead(lead, run):
        if lead > EARLY:

            @pl.when(step == 0)
            def _():
                for j in range(EARLY, min(lead, tiles_count)):
                    for i in range(2):
                        run(tile_gather(j), i)

        @pl.when((step + lead >= EARLY) & (step + lead < tiles))
        def _():
            for i in range(2):
                run(tile_gather(step + lead), i)

    def item(j):
        cols = pl.ds(pl.multiple_of(j * tile, tile), tile)
        out = [
            (lambda c: gate_out.at[c, :, cols], pl.ds(0, tile)),
            (lambda c: up_out.at[c, :, cols], pl.ds(tile, tile)),
        ]
        return Reduce(
            p,
            out,
            [other.at[j], group.at[j], ring.at[j]],
            [ssem.at[j], rsem.at[j], lsem.at[j]],
            mine=both.at[j, 0],
            give=both.at[j, 1],
        )

    def slot(t):
        for k in range(Reduce.STAGES):

            lag = k + (k > 0)

            @pl.when((t >= lag) & (t - lag < tiles))
            def _():
                item(t - lag).stage(k)

    @pl.when(step == 0)
    def _():
        greet(Reduce.peers(p))
        fetch().start()
        weights(0, True)
        acc[...] = jnp.zeros_like(acc)
        dx_ref[...] = jnp.zeros_like(dx_ref)

        def turn(j, _):
            rows = rows_at(j, 128)
            bt[:, rows] = jnp.transpose(b_ref[rows, :])
            return 0

        lax.fori_loop(0, total // 128, turn, 0)

    @pl.when(step < tiles)
    def _():
        ahead(LEADS[0], lambda g, i: g.start(i))
        weights(step, False)
        wg = wbuf[lax.rem(step, 2), 0].reshape(-1, tile)
        wu = wbuf[lax.rem(step, 2), 1].reshape(-1, tile)

        def rows_step(j, _):
            rows = rows_at(j, 512)
            b, e = b_ref[rows, :], e_ref[rows, :]
            gate = dot(b, wg)
            up = dot(b, wu)
            dh = dot_nt(e, wd_ref[...])
            sig = jax.nn.sigmoid(gate)
            swish = gate * sig
            h = (swish * up).astype(BF)
            dg = (dh * up * (sig * (1.0 + gate * (1.0 - sig)))).astype(BF)
            du = (dh * swish).astype(BF)
            down_ref[rows_at(step, tile), rows] = jnp.transpose(h)
            hid[rows, :] = h
            dgate[rows, :] = dg
            dup[rows, :] = du
            return 0

        def sums_step(j, _):
            rows = rows_at(j, 512)
            acc[rows, :] += dot(hid[rows, :], wd_ref[...])
            dx_ref[rows, :] += dot_nt(dgate[rows, :], wg) + dot_nt(dup[rows, :], wu)
            return 0

        lax.fori_loop(0, total // 512, rows_step, 0, unroll=True)

        ahead(LEADS[1], lambda g, i: g.relay(i))
        ahead(LEADS[2], lambda g, i: g.pass_on(i))
        ahead(1, lambda g, i: g.done(i))

        @pl.when(step + 1 < tiles)
        def _():
            weights(step + 1, True)

        @pl.when(step > 0)
        def _():
            slot(step - 1)

        for at, d in ((0, dgate), (tile, dup)):
            w = dot(bt[...], d[...]).astype(BF)
            for s in range(n):
                both[step, p.core, s, :, at : at + tile] = w[s * rs : s * rs + half]
                both[step, 1 - p.core, s, :, at : at + tile] = w[s * rs + half : (s + 1) * rs]
        item(step).start()
        lax.fori_loop(0, total // 512, sums_step, 0, unroll=True)

    @pl.when(step == tiles)
    def _():
        norm_ref[...] = jnp.zeros_like(norm_ref)

        def finish(j, _):
            rows = rows_at(j, 128)
            x = xs[rows, :]
            res_ref[rows, :] = (x + acc[rows, :]).astype(BF)
            inv = lax.rsqrt(jnp.mean(x * x, axis=-1, keepdims=True) + 1e-5)
            xn = x * inv
            db = dx_ref[rows, :]
            norm_ref[...] += jnp.sum(db * xn, axis=0, keepdims=True)
            dbg = db * gain_ref[1:2, :]
            dx = e_ref[rows, :].astype(F32) + inv * (dbg - xn * jnp.mean(dbg * xn, axis=-1, keepdims=True))
            dx_ref[rows, :] = dx
            dm_ref[rows, :] = dx.astype(BF)
            return 0

        fetch().wait()

        def turn_down(j, _):
            slot(tiles - 1 + j)
            rows = rows_at(j, down_ref.shape[0] // 4)
            down_ref[rows, :] = dot(down_ref[rows, :], e_ref[...]).astype(BF)
            write(1 + j, down_ref, down_out, rows).start()
            return 0

        lax.fori_loop(0, 4, turn_down, 0)
        slot(tiles + 3)
        lax.fori_loop(0, total // 128, finish, 0)
        every = pl.ds(0, total)
        results = [
            write(5, res_ref, res_out, every),
            write(6, dx_ref, dx_out, every),
            write(7, dm_ref, dm_out, every),
        ]
        for c in results:
            c.start()

        def tail(t, _):
            slot(t)
            return 0

        lax.fori_loop(tiles + 4, tiles + Reduce.STAGES, tail, 0)

        def settle(j, _):
            item(j).settle()
            return 0

        lax.fori_loop(0, tiles, settle, 0)
        for j in range(4):
            write(1 + j, down_ref, down_out, rows_at(j, down_ref.shape[0] // 4)).wait()
        for c in results:
            c.wait()


def feed(n, reps, b, e, x2, gain, wd, first, owns):
    total, width = b.shape
    owns = [halves(w) for w in owns]
    ff = wd.shape[0]
    tile, z = TILE, reps // 2
    tiles, half = ff // tile, width // (2 * n)
    once = lambda *sh: pl.BlockSpec(sh, lambda j: (0,) * len(sh), pipeline_mode=pl.Buffered(1))
    row = lambda: pl.BlockSpec((tile, width), lambda j: (jnp.minimum(j, tiles - 1), 0))
    anywhere = pl.BlockSpec(memory_space=pl.ANY)
    sd = jax.ShapeDtypeStruct
    return pl.pallas_call(
        functools.partial(feed_kernel, n, reps, half, tile),
        grid=(tiles + 1,),
        in_specs=[once(total, width)] * 2 + [anywhere, once(8, width), row()] + [anywhere] * 4,
        out_specs=[anywhere] * 3 + [once(1, width)] + [anywhere] * 5,
        out_shape=[
            sd((total, width), BF),
            sd((total, width), F32),
            sd((total, width), BF),
            sd((1, width), F32),
            sd((ff, total), BF),
            sd((2, half, ff), BF),
            sd((2, half, ff), BF),
            sd((n, 2, half, ff - EARLY * tile), BF),
            sd((n, 2, half, ff - EARLY * tile), BF),
        ],
        scratch_shapes=[
            pltpu.VMEM((width, total), BF),
            pltpu.VMEM((total, width), F32),
            pltpu.VMEM((total, tile), BF),
            pltpu.VMEM((total, tile), BF),
            pltpu.VMEM((total, tile), BF),
            pltpu.VMEM((tiles, 2, n, half, 2 * tile), BF),
        ]
        + Reduce.scratch(n, z, half, 2 * tile, False, (tiles,))
        + [
            pltpu.VMEM((total, width), F32),
            pltpu.VMEM((total, width), BF),
            pltpu.VMEM((total, width), F32),
            pltpu.VMEM((total, width), BF),
            pltpu.VMEM((ff, total), BF),
            pltpu.SemaphoreType.DMA((8,)),
            pltpu.SemaphoreType.DMA((tiles - EARLY, 2, 2 * (n - 1) + 1)),
            pltpu.SemaphoreType.DMA((tiles - EARLY, 2, 2 * (n - 1) + 1)),
            pltpu.VMEM((2, 2, n, 2, half, tile), BF),
            pltpu.SemaphoreType.DMA((2, 2)),
        ],
        compiler_params=pltpu.CompilerParams(collective_id=1, has_side_effects=True, vmem_limit_bytes=63 << 20),
        name="feed_forward",
    )(b, e, x2, gain, wd, *first, *owns)[:7]


def forward_kernel(n, reps, width, *refs):
    x_ref, segr_ref, m_ref, vec_ref, high_ref, low_ref = refs[:6]
    owns = refs[6:14]
    a_ref, q_ref, k_ref, v_ref, g_ref, r_ref, y_ref, o_ref, st_ref = refs[14:23]
    x2_ref, b_ref, vec_out, high_out, low_out = refs[23:28]
    outs = refs[28:36]
    state, esc, xs, ys, vecs, highs, lows = refs[36:43]
    kept = refs[43:48]
    small_send, small_recv, ssem, rsem, lsem = refs[48:]
    step, nc = pl.program_id(0), pl.num_programs(0) - 1
    p = Place(n, reps)
    early = outs[6].shape[3]
    owns = list(owns[:6]) + [own.at[:, :, 0:early] for own in owns[6:]]
    gather = Gather(
        p, owns, list(kept) + list(outs[5:]), [[sem.at[i] for i in range(8)] for sem in (ssem, rsem)]
    )
    smalls = [(vec_ref, vecs), (high_ref, highs), (low_ref, lows)]

    def small(k, j):
        src, dst = smalls[k]
        return remote(src, dst.at[p.me], small_send.at[k, j - 1], small_recv.at[k, j - 1], (p.rep, p.peer(j)))

    def keep(i):
        return pltpu.make_async_copy(kept[i], outs[i], lsem.at[i])

    def whole(i):
        w = kept[i][...]
        return w.reshape(-1, w.shape[-1])

    @pl.when(step == 0)
    def _():
        greet(gather.peers())
        for i in range(4):
            gather.start(i)
        for k in range(3):
            for j in range(1, n):
                small(k, j).start()
            src, dst = smalls[k]
            dst[p.me] = src[...]
        for i in range(4):
            gather.relay(i)
        for i in range(4, 8):
            gather.start(i)
        for k in range(3):
            for j in range(1, n):
                small(k, j).wait()
        rs = low_ref.shape[1]
        for s in range(n):
            at = slice(s * rs, (s + 1) * rs)
            vec_out[0:1, at] = vecs[s, :, 0:rs]
            vec_out[1:2, at] = vecs[s, :, rs : 2 * rs]
            low_out[:, at] = lows[s]

        def spread(part, out_width):
            own = part(0).shape[1]
            total = None
            for s in range(n):
                col = lax.broadcasted_iota(jnp.int32, (own, out_width), 1)
                row = lax.broadcasted_iota(jnp.int32, (own, out_width), 0)
                piece = dot(part(s), (col == row + s * own).astype(F32).astype(BF))
                total = piece if total is None else total + piece
            return total

        nb, ng = 512 // n, VH // n
        vec_out[2:3, 0:512] = spread(lambda s: vecs[s, :, 2 * rs : 2 * rs + nb].astype(BF), 512)
        vec_out[3:4, 0:VH] = spread(lambda s: vecs[s, :, -128:][:, 0:ng].astype(BF), VH)
        high_out[...] = spread(lambda s: highs[s], 512).astype(BF)
        for i in range(4):
            gather.pass_on(i)
        for i in range(4):
            gather.done(i)
            keep(i).start()
        state[...] = jnp.zeros_like(state)

    @pl.when(step < nc)
    def _():
        rows = pl.ds(pl.multiple_of(step * C, C), C)
        xb = x_ref[...]
        xs[rows, :] = xb
        x = xb.astype(F32)
        inv = lax.rsqrt(jnp.mean(x * x, axis=-1, keepdims=True) + 1e-5)
        a = (x * inv * vec_out[0:1, :]).astype(BF)
        a_ref[...] = a
        q_ref[...] = dot(a, whole(0)).astype(BF)
        k_ref[...] = dot(a, whole(1)).astype(BF)
        v_ref[...] = dot(a, whole(2)).astype(BF)
        g_ref[...] = dot(a, whole(3)).astype(BF)
        r_ref[...] = dot_nt(a, low_out[...]).astype(BF)
        fwd_chunk(
            step, q_ref, k_ref, v_ref, g_ref, r_ref, high_out, vec_out.at[2:3, 0:512], vec_out.at[3:4, 0:VH],
            segr_ref, m_ref, y_ref, o_ref, st_ref, state, esc,
        )
        ys[rows, :] = y_ref[...]

    for at, run in (
        (1, lambda: gather.relay(4)),
        (3, lambda: gather.pass_on(4)),
        (4, lambda: gather.relay(5)),
        (5, lambda: gather.relay(6)),
        (6, lambda: gather.relay(7)),
        (7, lambda: gather.pass_on(5)),
    ):
        pl.when(step == at)(run)

    @pl.when(step == nc)
    def _():
        gather.done(4)
        keep(4).start()

        def join(j, _):
            rows = pl.ds(pl.multiple_of(j * 256, 256), 256)
            x2 = xs[rows, :].astype(F32) + dot(ys[rows, :], whole(4))
            x2_ref[rows, :] = x2
            inv = lax.rsqrt(jnp.mean(x2 * x2, axis=-1, keepdims=True) + 1e-5)
            b_ref[rows, :] = (x2 * inv * vec_out[1:2, :]).astype(BF)
            return 0

        lax.fori_loop(0, xs.shape[0] // 256, join, 0)
        gather.pass_on(6)
        gather.pass_on(7)
        for i in range(5, 8):
            gather.done(i)
        for i in range(5):
            keep(i).wait()


def forward(n, reps, x, segr, vec, high, low, weights):
    T, width = x.shape
    nc = T // C
    M = jnp.asarray(level_sums(), BF)
    nr = M.shape[0]
    owns = [halves(w) for w in weights]
    last = lambda i: jnp.minimum(i, nc - 1)
    blk = lambda w: pl.BlockSpec((C, w), lambda i: (last(i), 0))
    full = lambda *sh: pl.BlockSpec(sh, lambda i: (0,) * len(sh), pipeline_mode=pl.Buffered(1))
    anywhere = pl.BlockSpec(memory_space=pl.ANY)
    sd = jax.ShapeDtypeStruct
    shapes = [(n,) + o.shape for o in owns[:6]] + [(n,) + o.shape[:2] + (EARLY * TILE,) for o in owns[6:]]
    kinds = 2 * (n - 1) + 1
    res = pl.pallas_call(
        functools.partial(forward_kernel, n, reps, width),
        grid=(nc + 1,),
        in_specs=[blk(width), full(nc, 1, C), full(nr, C), full(*vec.shape), full(*high.shape), full(*low.shape)]
        + [anywhere] * 8,
        out_specs=[blk(w) for w in (width, 512, 512, 1024, 1024, 16, 1024, 1024)]
        + [pl.BlockSpec((1, HEADS, VH, KH), lambda i: (last(i), 0, 0, 0))]
        + [full(T, width), full(T, width), full(8, width), full(16, 512), full(16, width)]
        + [anywhere] * 8,
        out_shape=[sd((T, w), BF) for w in (width, 512, 512, 1024, 1024, 16, 1024, 1024)]
        + [
            sd((nc, HEADS, VH, KH), BF),
            sd((T, width), F32),
            sd((T, width), BF),
            sd((8, width), F32),
            sd((16, 512), BF),
            sd((16, width), BF),
        ]
        + [sd(shape, BF) for shape in shapes],
        scratch_shapes=[
            pltpu.VMEM((HEADS, VH, KH), F32),
            pltpu.VMEM((nr, 512), F32),
            pltpu.VMEM((T, width), BF),
            pltpu.VMEM((T, 1024), BF),
            pltpu.VMEM((n,) + vec.shape, F32),
            pltpu.VMEM((n,) + high.shape, BF),
            pltpu.VMEM((n,) + low.shape, BF),
        ]
        + [pltpu.VMEM(shape, BF) for shape in shapes[:5]]
        + [
            pltpu.SemaphoreType.DMA((3, n - 1)),
            pltpu.SemaphoreType.DMA((3, n - 1)),
            pltpu.SemaphoreType.DMA((8, kinds)),
            pltpu.SemaphoreType.DMA((8, kinds)),
            pltpu.SemaphoreType.DMA((5,)),
        ],
        compiler_params=pltpu.CompilerParams(collective_id=0, has_side_effects=True, vmem_limit_bytes=60 << 20),
        name="gla_fwd_gather",
    )(x, segr, M, vec, high, low, *owns)
    return res[:14], [o.reshape(-1, o.shape[-1]) for o in res[14:20]] + list(res[20:])


def backward_kernel(n,reps,plan,half,*refs):
    (q_ref,k_ref,v_ref,g_ref,r_ref,o_ref,st_ref,dy_ref,a_ref,x_ref,dx_ref,
     wh_ref,vec_ref,nmlp_ref,segr_ref,m_ref,*w_any,wl_ref)=refs[:21]
    bias_ref,gain_ref=vec_ref.at[2:3,0:512],vec_ref.at[3:4,0:VH]
    parts=refs[21:23]
    gt_ref,small_ref=refs[23:25]
    outs=refs[25:31]
    dstate,rcar,esc,dcs,dall,at_ref,dz_ref,low_acc,high_acc,gb_ref,gg_ref,smb,both,drs,*w_kept,w_sem=refs[31:50]
    rest=refs[50:]
    step=pl.program_id(0); nc=(pl.num_programs(0)-1)//2
    p=Place(n,reps)
    items=[]
    for which,at,width,source in plan:
        count=7 if source is None else 6
        mem,rest=rest[:count],rest[count:]
        cols=pl.ds(at,width)
        out=[(lambda c,which=which,cols=cols: outs[which].at[c,:,cols],pl.ds(0,width))]
        if source is None:
            items.append(Reduce(p,out,mem[:4],mem[4:],part=parts[which].at[:,:,:,cols]))
        else:
            cols=pl.ds(source,width)
            items.append(Reduce(p,out,mem[:3],mem[3:],mine=both.at[0,:,:,cols],give=both.at[1,:,:,cols]))
    mem=rest
    small=Small(p,smb,small_ref,mem[:4],mem[4:])
    ready=[it for it in items if it.part is not None]
    fresh=[it for it in items if it.part is None]

    plan_at={}
    def book(it,times):
        for stage,t in enumerate(times): plan_at.setdefault(t,[]).append((stage,it))
    for j,it in enumerate(ready): book(it,(j//2,2+j,4+j,6+j,7+j,8+j,9+j))
    for j,it in enumerate(fresh): book(it,[8+j+s for s in range(Reduce.STAGES)])
    last=max(plan_at)+1

    def slot(t):
        for stage,it in sorted(plan_at.get(t,[]),key=lambda pair: pair[0]): it.stage(stage)

    def weight(j):
        return pltpu.make_async_copy(w_any[j],w_kept[j],w_sem.at[j])

    @pl.when(step==0)
    def _():
        greet(Reduce.peers(p))
        for j in range(4): weight(j).start()
        for it in ready: it.start()
        for ref in (dstate,rcar,gb_ref,gg_ref,low_acc,high_acc,smb): ref[...]=jnp.zeros_like(ref)

    @pl.when(step<nc)
    def _():
        i=nc-1-step
        rows=pl.ds(pl.multiple_of(i*C,C),C)
        bwd_chunk(i,q_ref,k_ref,v_ref,g_ref,r_ref,o_ref,st_ref,dy_ref,wh_ref,bias_ref,gain_ref,segr_ref,m_ref,
                  dall.at[rows,0:512],dall.at[rows,512:1024],dall.at[rows,1024:2048],dall.at[rows,2048:3072],dz_ref,gb_ref,gg_ref,dstate,rcar,esc,dcs)
        dz=dz_ref[...]; a=a_ref[...]
        dr=dot_nt(dz,wh_ref[...]).astype(BF)
        drs[rows,:]=dr
        high_acc[...]+=dot_tn(r_ref[...],dz)
        low_acc[...]+=dot_tn(dr,a)
        at_ref[:,rows]=jnp.transpose(a)

    @pl.when(step>nc)
    def _():
        rows=pl.ds(pl.multiple_of((step-nc-1)*C,C),C)
        da=dot_nt(dall[rows,0:512],w_kept[0][...])+dot_nt(dall[rows,512:1024],w_kept[1][...])
        da=da+dot_nt(dall[rows,1024:2048],w_kept[2][...])+dot_nt(dall[rows,2048:3072],w_kept[3][...])+dot(drs[rows,:],wl_ref[...])
        x=x_ref[...].astype(F32)
        n1=lax.rsqrt(jnp.mean(x*x,axis=-1,keepdims=True)+1e-5)
        xn=x*n1
        dm=da*vec_ref[0:1,:]
        gt_ref[...]=dx_ref[...]+n1*(dm-xn*jnp.mean(dm*xn,axis=-1,keepdims=True))

    for t in range(8):
        @pl.when(step==t)
        def _(): slot(t)

    rs=2*half

    @pl.when(step==nc)
    def _():
        def product(at,width):
            cols=slice(at,at+width)
            w=dot(at_ref[...],dall[:,cols]).astype(BF)
            for s in range(n):
                both[p.core,s,:,cols]=w[s*rs:s*rs+half]
                both[1-p.core,s,:,cols]=w[s*rs+half:(s+1)*rs]

        smb[:,16:32,:]=jnp.broadcast_to(high_acc[...][None],(n,16,512))
        smb[:,32:33,:]=jnp.broadcast_to(gb_ref[...][None],(n,1,512))
        smb[:,33:34,0:256]=jnp.broadcast_to(gg_ref[...][None],(n,1,256))
        for s in range(n):
            at=slice(s*rs,(s+1)*rs)
            smb[s,0:16,0:rs]=low_acc[:,at]
            smb[s,35:36,0:rs]=nmlp_ref[:,at]
        for j,at in enumerate((2048,2560,1024,1536,0,512)):
            product(at,512)
            fresh[j].start()
            if j==1: small.swap().start()
            if j%2==1: slot(8+j//2)
            if j==5: small.stage(0)
        for j in range(4): weight(j).wait()

    for t in range(11,19):
        @pl.when(step==t-11+nc+1)
        def _():
            slot(t)
            if t in (13,16): small.stage((t-10)//3)

    @pl.when(step==2*nc)
    def _():
        for t in range(19,last): slot(t)
        for it in items: it.settle()
        small.settle()

def backward(n,reps,q,k,v,g,r,o,st,dy,first,tokens,dx2,wh,vecs,nmlp,segr,weights,partials):
    T=q.shape[0]; nc=T//C; z=reps//2
    assert nc==8
    M=jnp.asarray(level_sums(),BF); nr=M.shape[0]
    blk=lambda w: pl.BlockSpec((C,w),lambda i:(jnp.maximum(nc-1-i,0),0))
    late=lambda w: pl.BlockSpec((C,w),lambda i:(jnp.clip(i-nc-1,0,nc-1),0))
    full=lambda *sh: pl.BlockSpec(sh,lambda i:(0,)*len(sh),pipeline_mode=pl.Buffered(1))
    sd=jax.ShapeDtypeStruct
    anywhere=pl.BlockSpec(memory_space=pl.ANY)
    half=first.shape[1]//(2*n)
    pairs=[q.reshape(n,2,q.shape[0]//(2*n),q.shape[1]) for q in partials]
    plan,scratch=[],[]
    for which,(pair,cut) in enumerate(zip(pairs,(4,2))):
        tiles=pair.shape[3]//128
        edges=[128*(tiles*j//cut) for j in range(cut+1)]
        for at,end in zip(edges[:-1],edges[1:]):
            plan.append((which,at,end-at,None)); scratch+=Reduce.scratch(n,z,pair.shape[2],end-at,True)
    for which,at,width,source in ((5,0,512,2048),(5,512,512,2560),(4,0,512,1024),(4,512,512,1536),(2,0,512,0),(3,0,512,512)):
        plan.append((which,at,width,source)); scratch+=Reduce.scratch(n,z,half,width,False)
    scratch+=Small.scratch(n,z,40,512)
    out=lambda h,w: sd((2,h,w),BF)
    res=pl.pallas_call(functools.partial(backward_kernel,n,reps,tuple(plan),half),grid=(2*nc+1,),
        in_specs=[blk(512),blk(512),blk(1024),blk(1024),blk(16),blk(1024),pl.BlockSpec((1,HEADS,VH,KH),lambda i:(jnp.maximum(nc-1-i,0),0,0,0)),blk(1024),
                  blk(1024),late(1024),late(1024),
                  full(16,512),full(8,1024),full(1,1024),full(nc,1,C),full(nr,C),
                  anywhere,anywhere,anywhere,anywhere,full(16,1024)]+[anywhere]*2,
        out_specs=[late(1024),pl.BlockSpec((40,512),lambda i:(0,0))]+[anywhere]*6,
        out_shape=[sd((T,1024),F32),sd((40,512),F32)]+[out(q.shape[2],q.shape[3]) for q in pairs]+[out(half,512),out(half,512),out(half,1024),out(half,1024)],
        scratch_shapes=[pltpu.VMEM((HEADS,VH,KH),F32),pltpu.VMEM((1,512),F32),pltpu.VMEM((nr,512),F32),pltpu.VMEM((C,1024),BF),
                        pltpu.VMEM((T,3072),BF),pltpu.VMEM((1024,T),BF),pltpu.VMEM((C,512),BF),pltpu.VMEM((16,1024),F32),pltpu.VMEM((16,512),F32),
                        pltpu.VMEM((1,512),F32),pltpu.VMEM((1,256),F32),pltpu.VMEM((n,40,512),F32),
                        pltpu.VMEM((2,n,half,3072),BF),pltpu.VMEM((T,16),BF)]
                       +[pltpu.VMEM((1024,w),BF) for w in (512,512,1024,1024)]+[pltpu.SemaphoreType.DMA((4,))]+scratch,
        compiler_params=pltpu.CompilerParams(collective_id=2,has_side_effects=True,vmem_limit_bytes=63<<20),
        name="gla_bwd_reduce")(q,k,v,g,r,o,st,dy,first,tokens,dx2,wh,vecs,nmlp,segr,M,*weights,*pairs)
    return res[0],res[1],[x.reshape(-1,x.shape[2]) for x in res[2:]]


def matmul(left, right):
    return jnp.dot(left, right, preferred_element_type=F32)


def local(
    shards,
    reps,
    tokens,
    segments,
    cotangent,
    norm_mix,
    w_query,
    w_key,
    w_value,
    w_outgate,
    w_low,
    w_high,
    decay_bias,
    head_gain,
    w_out,
    norm_mlp,
    w_gate,
    w_up,
    w_down,
):
    total = tokens.shape[0] * tokens.shape[1]
    width = tokens.shape[2]
    segr = seg_rows(segments)
    pads = [-v.shape[0] % 128 for v in (decay_bias, head_gain)]
    zeros = [jnp.zeros((pad,), BF) for pad in pads]
    vec = jnp.concatenate([norm_mix, norm_mlp, decay_bias, zeros[0], head_gain, zeros[1]]).astype(F32)[None]
    (
        (first, query, keys, values, outgate, lowrank, mixed, heads, states, resid, second, vecs, high_w, low_w),
        (query_w, key_w, value_w, outgate_w, out_w, down_w, gate_w, up_w),
    ) = forward(
        shards,
        reps,
        tokens.reshape(total, width),
        segr,
        vec,
        w_high,
        w_low.T,
        (w_query, w_key, w_value, w_outgate, w_out, w_down, w_gate, w_up),
    )
    grad_out = cotangent.reshape(total, width)
    result, grad_resid, branch, part_norm_mlp, part_down, sum_gate, sum_up = feed(
        shards, reps, second, grad_out, resid, vecs, down_w, (gate_w, up_w), (w_gate, w_up)
    )
    part_out = dot_tn(mixed, branch)
    grad_mixed = dot_nt(branch, out_w).astype(BF)
    grad_inputs, small_sums, sums = backward(
        shards,
        reps,
        query,
        keys,
        values,
        outgate,
        lowrank,
        heads,
        states,
        grad_mixed,
        first,
        tokens.reshape(total, width),
        grad_resid,
        high_w,
        vecs,
        part_norm_mlp,
        segr,
        (query_w, key_w, value_w, outgate_w, low_w),
        (part_down, part_out.astype(BF)),
    )
    sum_gate, sum_up = [s.reshape(-1, s.shape[2]).astype(F32) for s in (sum_gate, sum_up)]
    sum_down, sum_out, sum_query, sum_key, sum_value, sum_outgate = [s.astype(F32) for s in sums]
    me = lax.axis_index("shard")
    rs = w_low.shape[0]

    def across(block, width):
        return lax.dynamic_slice_in_dim(block, me * width, width, axis=1)

    grad_low_w = small_sums[:16, :rs].T
    mixer = (
        (w_query, sum_query),
        (w_key, sum_key),
        (w_value, sum_value),
        (w_outgate, sum_outgate),
        (w_low, grad_low_w),
    )
    own = (
        sum(jnp.sum(w.astype(F32) * g, axis=1) for w, g in mixer) / norm_mix.astype(F32),
        small_sums[35, :rs],
        across(small_sums[32:33], decay_bias.shape[0]).reshape(-1),
        across(small_sums[33:34, :VH], head_gain.shape[0]).reshape(-1),
        grad_low_w,
        across(small_sums[16:32], w_high.shape[1]),
    )
    return (
        result.reshape(tokens.shape),
        grad_inputs.reshape(tokens.shape),
        own[0],
        sum_query,
        sum_key,
        sum_value,
        sum_outgate,
        own[4],
        own[5],
        own[2],
        own[3],
        sum_out,
        own[1],
        sum_gate,
        sum_up,
        sum_down,
    )


def solution(mesh):
    in_specs = (
        P(("rep", "shard"), None, None),
        P(("rep", "shard"), None),
        P(("rep", "shard"), None, None),
        P("shard"),
        P("shard", None),
        P("shard", None),
        P("shard", None),
        P("shard", None),
        P("shard", None),
        P(None, "shard"),
        P("shard"),
        P("shard"),
        P("shard", None),
        P("shard"),
        P("shard", None),
        P("shard", None),
        P("shard", None),
    )
    out_specs = (
        P(("rep", "shard"), None, None),
        P(("rep", "shard"), None, None),
        P("shard"),
        P("shard", None),
        P("shard", None),
        P("shard", None),
        P("shard", None),
        P("shard", None),
        P(None, "shard"),
        P("shard"),
        P("shard"),
        P("shard", None),
        P("shard"),
        P("shard", None),
        P("shard", None),
        P("shard", None),
    )
    return jax.shard_map(
        functools.partial(local, mesh.shape["shard"], mesh.shape["rep"]), mesh=mesh, in_specs=in_specs, out_specs=out_specs, check_vma=False)
```
